128 devices in a mesh: member: 8 (over y, core), tile: 16 (over z, x).
Axes of the slice: x: 4, y: 4, z: 4, core: 2. Of those that a mesh axis runs over, the one named last changes fastest.
Arguments:
- perturb: bfloat16 [128, 256, 2560], P('member', 'tile'), may hold values from -0.5 to 0.5
- weights: float32 [128, 64, 1280], P('member', 'tile'), may hold values from -1.2 to 1.2
- column_map: bfloat16 [1280, 2560], replicated, may hold values from -0.15625 to 0.15625
- background: float32 [256, 2560], P('tile', 'member'), may hold values from -6 to 6
- stencil_index: int32 [16, 128, 8, 8], P('tile'), may hold values from 0 to 4798, as said below
- row_fraction: float32 [16, 128, 8, 8], P('tile'), may hold values from 0 to 1
- column_fraction: float32 [16, 128, 8, 8], P('tile'), may hold values from 0 to 1
- block_lengths: int32 [16, 128, 8], P('tile'), may hold values from 0 to 8, as said below
- obs_value: float32 [128, 128, 8], P(('member', 'tile')), may hold values from -6 to 6
- obs_error: float32 [128, 128, 8], P(('member', 'tile')), may hold values from 0.3 to 1
- instrument_gain: float32 [128], P(('member', 'tile')), may hold values from 0.2 to 0.8
Outputs:
- analysis_weights: float32 [128, 64, 1280], P('member', 'tile')
- analysis_increment: float32 [256, 2560], P('tile', 'member')
The draws below stay inside these ranges and needn't reach their ends.
Inputs may be any that keep to these rules, and one draw needn't show every extreme that they name: stencil_index = r * 320 + c with 0 <= r < 15 and 0 <= c < 319. `block_lengths`: in every draw some owner (one tile and one member index) has all its blocks full.
All inputs are finite; a program needn't handle non-finite values.
Results may differ from the reference program's by a relative error of at most 0.0022.
Values may be sent and summed in bfloat16 or wider, within the bound.
No kernel may reach another device: no remote copies, remote signals or barrier semaphores. Data moves between devices by JAX's collectives and lax.ppermute only.
A program may use at most 64 MiB of HBM per device.

```python
import math
import jax
import jax.numpy as jnp
from jax import lax

RATIO = 4
KSM = 3
ITERS = 1
CC = 1280
FC = 2560
MEM_DEV = 16
CAP = 8
MEMBERS = 128
TILES = 16
GROUPS = 8
NCR = 64
FR = 16
NFR = 256
CW = 320
N_MEMBER = 8
N_TILE = 16
DEVICES = 128


def draw_stencil_index(key, part):
    array_shape = (TILES, DEVICES, GROUPS, CAP)
    first_key, second_key = jax.random.split(key)
    row_pick = jax.random.randint(first_key, array_shape, 0, FR - 1)
    column_pick = jax.random.randint(second_key, array_shape, 0, CW - 1)
    return (row_pick * CW + column_pick).astype(jnp.int32)


def draw_block_lengths(key, part):
    first_key, second_key, third_key, fourth_key = jax.random.split(key, 4)
    base_counts = jax.random.randint(first_key, (TILES, DEVICES, GROUPS), 0, CAP // 2 + 1)
    busy_owner = jax.random.randint(second_key, (TILES, 1, GROUPS), 0, 8) == 0
    chosen_tile = jax.random.randint(third_key, (), 0, TILES)
    chosen_group = jax.random.randint(fourth_key, (), 0, GROUPS)
    tile_ids = lax.broadcasted_iota(jnp.int32, (TILES, 1, GROUPS), 0)
    group_ids = lax.broadcasted_iota(jnp.int32, (TILES, 1, GROUPS), 2)
    forced = (tile_ids == chosen_tile) & (group_ids == chosen_group)
    return jnp.where(busy_owner | forced, CAP, base_counts).astype(jnp.int32)


def shard_levels(stream_key, shape, cuts, least, high):
    loudness, own = 1.0, jax.random.fold_in(stream_key, 6)
    for axis_at, parts in cuts:
        heights = jnp.exp(jax.random.uniform(jax.random.fold_in(own, axis_at), (parts,), jnp.float32, least / len(cuts), high / len(cuts)))
        loudness = loudness * jnp.repeat(heights, shape[axis_at] // parts).reshape([-1 if axis == axis_at else 1 for axis in range(len(shape))])
    return loudness


def scatter_about(key, extent, scale, limit, cuts=(), kind=jnp.bfloat16):
    factor_of = shard_levels(key, extent, cuts, -0.22, 0.18) if cuts else 1.0
    array = jax.random.normal(key, extent, jnp.float32) * scale * factor_of
    return jnp.minimum(jnp.maximum(array, -limit), limit).astype(kind)


def setup_inputs(seed: int = 0) -> dict:
    arg_keys = jax.random.split(jax.random.key(seed), 12)
    perturb = scatter_about(arg_keys[0], (MEMBERS, NFR, FC), MEMBERS ** -0.5, 0.5, ((0, 8), (1, 16)))
    weights = scatter_about(arg_keys[1], (MEMBERS, NCR, CC), 0.2, 1.2, ((0, 8), (1, 16)), jnp.float32)
    column_map = scatter_about(arg_keys[2], (CC, FC), CC ** -0.5, 0.15625)
    background = scatter_about(arg_keys[3], (NFR, FC), 1.0, 6.0, ((0, 16), (1, 8)), jnp.float32)
    stencil_index = draw_stencil_index(jax.random.fold_in(arg_keys[11], 71), 0)
    row_fraction = jnp.clip(1.0 * jax.random.uniform(arg_keys[5], (TILES, DEVICES, GROUPS, CAP), jnp.float32) ** shard_levels(arg_keys[5], (TILES, DEVICES, GROUPS, CAP), ((0, 16),), -0.2, 0.2), 0.0, 1.0)
    column_fraction = jnp.clip(1.0 * jax.random.uniform(arg_keys[6], (TILES, DEVICES, GROUPS, CAP), jnp.float32) ** shard_levels(arg_keys[6], (TILES, DEVICES, GROUPS, CAP), ((0, 16),), -0.2, 0.2), 0.0, 1.0)
    block_lengths = draw_block_lengths(jax.random.fold_in(arg_keys[11], 71), 0)
    obs_value = scatter_about(arg_keys[8], (DEVICES, DEVICES, CAP), 1.0, 6.0, ((0, 128),), jnp.float32)
    obs_error = jnp.clip(jnp.exp(math.log(1.0) - 1.2039728 * jax.random.uniform(arg_keys[9], (DEVICES, DEVICES, CAP), jnp.float32) ** shard_levels(arg_keys[9], (DEVICES, DEVICES, CAP), ((0, 128),), -0.2, 0.2)), 0.3, 1.0)
    instrument_gain = jnp.clip(0.2 + 0.6 * jax.random.uniform(arg_keys[10], (DEVICES,), jnp.float32) ** shard_levels(arg_keys[10], (DEVICES,), ((0, 128),), -0.2, 0.2), 0.2, 0.8)
    return dict(perturb=perturb, weights=weights, column_map=column_map, background=background, stencil_index=stencil_index, row_fraction=row_fraction, column_fraction=column_fraction, block_lengths=block_lengths, obs_value=obs_value, obs_error=obs_error, instrument_gain=instrument_gain)


DIFFUSION = 0.45


def smooth(grid_values):
    for pass_index in range(KSM):
        padded = jnp.pad(grid_values, ((0, 0), (1, 1), (0, 0)))
        grid_values = grid_values + DIFFUSION * (padded[:, :-2] + padded[:, 2:] - 2.0 * grid_values)
    return grid_values


def refine(extended):
    members_here, row_count, col_count = extended.shape
    lower_rows = extended[:, :-2]
    middle = extended[:, 1:-1]
    upper_rows = extended[:, 2:]
    pieces = []
    for offset in range(RATIO):
        shift_value = (offset + 0.5) / RATIO - 0.5
        if shift_value < 0:
            pieces.append((1.0 + shift_value) * middle - shift_value * lower_rows)
        else:
            pieces.append((1.0 - shift_value) * middle + shift_value * upper_rows)
    return jnp.stack(pieces, axis=2).reshape(members_here, (row_count - 2) * RATIO, col_count)


def refine_adjoint(fine_field):
    members_here, fine_count, col_count = fine_field.shape
    row_count = fine_count // RATIO
    blocks = fine_field.reshape(members_here, row_count, RATIO, col_count)
    middle = jnp.zeros_like(blocks[:, :, 0])
    lower_rows = jnp.zeros_like(middle)
    upper_rows = jnp.zeros_like(middle)
    for offset in range(RATIO):
        shift_value = (offset + 0.5) / RATIO - 0.5
        fine_layer = blocks[:, :, offset]
        if shift_value < 0:
            middle = middle + (1.0 + shift_value) * fine_layer
            lower_rows = lower_rows - shift_value * fine_layer
        else:
            middle = middle + (1.0 - shift_value) * fine_layer
            upper_rows = upper_rows + shift_value * fine_layer
    return (jnp.pad(middle, ((0, 0), (1, 1), (0, 0))) + jnp.pad(lower_rows, ((0, 0), (0, 2), (0, 0)))
            + jnp.pad(upper_rows, ((0, 0), (2, 0), (0, 0))))


def forward(coarse, perturb, column_map):
    smoothed_all = smooth(coarse).reshape(N_MEMBER, MEM_DEV, NCR, CC)
    members_grouped = perturb.reshape(N_MEMBER, MEM_DEV, NFR, FC)

    def add_group(accumulated, group_items):
        smoothed_part, perturb_part = group_items
        mapped = jnp.dot(smoothed_part.astype(jnp.bfloat16).reshape(-1, CC), column_map,
                         preferred_element_type=jnp.float32).reshape(MEM_DEV, NCR, FC)
        fine_field = refine(jnp.pad(mapped, ((0, 0), (1, 1), (0, 0))))
        return accumulated + jnp.sum(fine_field * perturb_part.astype(jnp.float32), axis=0), None

    accumulated, unused = lax.scan(add_group, jnp.zeros((NFR, FC), jnp.float32), (smoothed_all, members_grouped))
    return accumulated


def adjoint_map(spread_field, perturb, column_map):
    members_grouped = perturb.reshape(N_MEMBER, MEM_DEV, NFR, FC)

    def one_group(perturb_part):
        edge_terms = refine_adjoint(perturb_part.astype(jnp.float32) * spread_field)
        inner_rows = edge_terms[:, 1:-1].astype(jnp.bfloat16)
        pulled = lax.dot_general(inner_rows.reshape(-1, FC), column_map, (((1,), (1,)), ((), ())),
                                 preferred_element_type=jnp.float32)
        return pulled.reshape(MEM_DEV, NCR, CC)

    pulled_all = lax.map(one_group, members_grouped).reshape(MEMBERS, NCR, CC)
    return smooth(pulled_all)


def global_points(stencil_index):
    tile_ids = lax.broadcasted_iota(jnp.int32, stencil_index.shape, 0)
    group_ids = lax.broadcasted_iota(jnp.int32, stencil_index.shape, 2)
    row_ids = tile_ids * FR + stencil_index // CW
    col_ids = group_ids * CW + stencil_index % CW
    return (row_ids * FC + col_ids).astype(jnp.int32)


def interpolate(field_flat, corner, row_fraction, column_fraction, stride):
    return ((1.0 - row_fraction) * (1.0 - column_fraction) * field_flat[corner]
            + (1.0 - row_fraction) * column_fraction * field_flat[corner + 1]
            + row_fraction * (1.0 - column_fraction) * field_flat[corner + stride]
            + row_fraction * column_fraction * field_flat[corner + stride + 1])


def spread(residual, corner, row_fraction, column_fraction, stride, total_size):
    positions = jnp.concatenate([corner.reshape(-1), (corner + 1).reshape(-1),
                                 (corner + stride).reshape(-1), (corner + stride + 1).reshape(-1)])
    amounts = jnp.concatenate([
        ((1.0 - row_fraction) * (1.0 - column_fraction) * residual).reshape(-1),
        ((1.0 - row_fraction) * column_fraction * residual).reshape(-1),
        (row_fraction * (1.0 - column_fraction) * residual).reshape(-1),
        (row_fraction * column_fraction * residual).reshape(-1)])
    return jnp.zeros((total_size,), jnp.float32).at[positions].add(amounts)


def innovation(obs_state, obs_value, obs_error, instrument):
    bounded = jnp.tanh(obs_state)
    derivative = 1.0 + instrument * (1.0 - bounded * bounded)
    misfit = obs_state + instrument * bounded - obs_value
    precision_obs = 1.0 / (obs_error * obs_error)
    return derivative * misfit * precision_obs, derivative * derivative * precision_obs


def to_owner_layout(values):
    return jnp.transpose(values.reshape(DEVICES, N_MEMBER, N_TILE, CAP), (2, 0, 1, 3))


def reference(perturb, weights, column_map, background, stencil_index, row_fraction, column_fraction,
              block_lengths, obs_value, obs_error, instrument_gain):
    corner = global_points(stencil_index)
    slot_ids = lax.broadcasted_iota(jnp.int32, stencil_index.shape, 3)
    valid_slots = (slot_ids < block_lengths[:, :, :, None]).astype(jnp.float32)
    coarse = weights
    increment = forward(coarse, perturb, column_map)
    obs_state = interpolate((background + increment).reshape(-1), corner, row_fraction, column_fraction, FC)
    for iteration in range(ITERS):
        batch_state = jnp.transpose(obs_state, (1, 2, 0, 3)).reshape(DEVICES, DEVICES, CAP)
        residual, obs_weight = innovation(batch_state, obs_value, obs_error, instrument_gain[:, None, None])
        residual = to_owner_layout(residual) * valid_slots
        obs_weight = to_owner_layout(obs_weight)
        spread_field = spread(residual, corner, row_fraction, column_fraction, FC, NFR * FC).reshape(NFR, FC)
        gradient = coarse + adjoint_map(spread_field, perturb, column_map)
        grad_square = jnp.sum(gradient * gradient)
        grad_image = forward(gradient, perturb, column_map)
        grad_obs = interpolate(grad_image.reshape(-1), corner, row_fraction, column_fraction, FC)
        curvature = jnp.sum(valid_slots * obs_weight * grad_obs * grad_obs)
        step_size = grad_square / (grad_square + curvature)
        coarse = coarse - step_size * gradient
        increment = increment - step_size * grad_image
        obs_state = obs_state - step_size * grad_obs
    return coarse, increment
```

```python
import jax
import jax.numpy as jnp
import numpy as np
from jax import lax
from jax.sharding import PartitionSpec as P

RATIO = 4
KSM = 3
DIFFUSION = 0.45
NTILE = 16
NMEMBER = 8
NCORE = 2
NY = NMEMBER // NCORE
FLOAT, HALF = jnp.float32, jnp.bfloat16


def turn(values, step, axis):
    count = lax.axis_size(axis)
    return lax.ppermute(values, axis, [(i, (i + step) % count) for i in range(count)])


def swap_core(values):
    return lax.ppermute(values, "member", [(i, i ^ 1) for i in range(NMEMBER)])


def sum_y(values):
    return (
        values
        + turn(values, NCORE, "member")
        + turn(values, 2 * NCORE, "member")
        + turn(values, 3 * NCORE, "member")
    )


def row_mask(tile_pos, first, count):
    rows = tile_pos * 4 + first + jnp.arange(count)
    return ((rows >= 0) & (rows < 4 * NTILE)).astype(FLOAT)[None, :, None]


def sweeps(values, tile_pos, first):
    for _ in range(KSM):
        values = values * row_mask(tile_pos, first, values.shape[1])
        middle = values[:, 1:-1]
        values = middle + DIFFUSION * (values[:, :-2] + values[:, 2:] - 2.0 * middle)
        first += 1
    return values * row_mask(tile_pos, first, values.shape[1])


def refine(extended):
    members_here, row_count, col_count = extended.shape
    lower_rows = extended[:, :-2]
    middle = extended[:, 1:-1]
    upper_rows = extended[:, 2:]
    pieces = []
    for offset in range(RATIO):
        shift_value = (offset + 0.5) / RATIO - 0.5
        if shift_value < 0:
            pieces.append((1.0 + shift_value) * middle - shift_value * lower_rows)
        else:
            pieces.append((1.0 - shift_value) * middle + shift_value * upper_rows)
    return jnp.stack(pieces, axis=2).reshape(members_here, (row_count - 2) * RATIO, col_count)


def refine_adjoint(fine_field):
    members_here, fine_count, col_count = fine_field.shape
    row_count = fine_count // RATIO
    blocks = fine_field.reshape(members_here, row_count, RATIO, col_count)
    middle = jnp.zeros_like(blocks[:, :, 0])
    lower_rows = jnp.zeros_like(middle)
    upper_rows = jnp.zeros_like(middle)
    for offset in range(RATIO):
        shift_value = (offset + 0.5) / RATIO - 0.5
        fine_layer = blocks[:, :, offset]
        if shift_value < 0:
            middle = middle + (1.0 + shift_value) * fine_layer
            lower_rows = lower_rows - shift_value * fine_layer
        else:
            middle = middle + (1.0 - shift_value) * fine_layer
            upper_rows = upper_rows + shift_value * fine_layer
    return (
        jnp.pad(middle, ((0, 0), (1, 1), (0, 0)))
        + jnp.pad(lower_rows, ((0, 0), (0, 2), (0, 0)))
        + jnp.pad(upper_rows, ((0, 0), (2, 0), (0, 0)))
    )


def partial_forward(low, own, high, tile_pos, perturb, column_map):
    smooth = sweeps(jnp.concatenate([low.astype(FLOAT), own, high.astype(FLOAT)], axis=1), tile_pos, -4)
    members_here, row_count, coarse_cols = smooth.shape
    mapped = jnp.dot(
        smooth.astype(HALF).reshape(-1, coarse_cols), column_map, preferred_element_type=FLOAT
    )
    fine_field = refine(mapped.reshape(members_here, row_count, -1))
    return jnp.sum(fine_field * perturb, axis=0)


def by_parity(field):
    rows, cols = field.shape
    width = cols // NMEMBER
    return jnp.transpose(field.reshape(rows, NY, NCORE, width), (2, 1, 0, 3))


def owner_sum(field, core_pos):
    parts = by_parity(field)
    mine = lax.dynamic_index_in_dim(parts, core_pos, 0, False)
    other = lax.dynamic_index_in_dim(parts, 1 - core_pos, 0, False)
    return sum_y(mine + swap_core(other))


def column_pick(column, width):
    ids = lax.broadcasted_iota(jnp.int32, column.shape[:1] + (width,) + column.shape[1:], 1)
    return (ids == column[:, None]).astype(HALF)


def split_half(values):
    high = lax.reduce_precision(values, 8, 7)
    return high.astype(HALF), (values - high).astype(HALF)


def interpolate(fields, picks, row_factor, column_frac):
    nxt = jnp.concatenate([fields[:, :, 1:], fields[:, :, :1]], axis=2)
    both = jnp.concatenate([fields, nxt], axis=1)
    high, low = split_half(both)
    got = jnp.einsum(
        "yrc,ycn->yrn", jnp.concatenate([high, low], axis=1), picks, preferred_element_type=FLOAT
    )
    rows = fields.shape[1]
    left = got[:, :rows] + got[:, 2 * rows : 3 * rows]
    right = got[:, rows : 2 * rows] + got[:, 3 * rows :]
    mixed = left * (1.0 - column_frac[:, None]) + right * column_frac[:, None]
    return jnp.sum(mixed * row_factor, axis=1)


def spread_regions(residual, picks, row_factor, column_frac):
    weighted = row_factor * residual[:, None]
    both = jnp.concatenate(
        [weighted * (1.0 - column_frac[:, None]), weighted * column_frac[:, None]], axis=1
    )
    high, low = split_half(both)
    got = jnp.einsum(
        "yrn,ycn->yrc", jnp.concatenate([high, low], axis=1), picks, preferred_element_type=FLOAT
    )
    rows = row_factor.shape[1]
    left = got[:, :rows] + got[:, 2 * rows : 3 * rows]
    right = got[:, rows : 2 * rows] + got[:, 3 * rows :]
    return left + jnp.concatenate([right[:, :, -1:], right[:, :, :-1]], axis=2)


def innovation(obs_state, obs_value, obs_error, instrument):
    bounded = jnp.tanh(obs_state)
    derivative = 1.0 + instrument * (1.0 - bounded * bounded)
    misfit = obs_state + instrument * bounded - obs_value
    precision_obs = 1.0 / (obs_error * obs_error)
    return (derivative * misfit * precision_obs, derivative * derivative * precision_obs)


def shards(
    perturb,
    weights,
    column_map,
    background,
    stencil_index,
    row_fraction,
    column_fraction,
    block_lengths,
    obs_value,
    obs_error,
    instrument_gain,
):
    member_pos = lax.axis_index("member")
    core_pos = member_pos % NCORE
    y_pos = member_pos // NCORE
    tile_pos = lax.axis_index("tile")
    fine_rows, width = background.shape
    slots = obs_value.shape[2]
    devices = obs_value.shape[1]

    half_weights = weights.astype(HALF)
    low, high = turn(half_weights, 1, "tile"), turn(half_weights, -1, "tile")

    stacked = jnp.stack([obs_value[0], obs_error[0]])
    stacked = stacked.reshape(2, NY, NCORE, NTILE, slots)
    stacked = jnp.transpose(stacked, (2, 3, 0, 1, 4)).reshape(NCORE, NTILE, 2 * NY * slots)
    gains = jnp.broadcast_to(instrument_gain, (NCORE, NTILE, 2 * NY * slots))
    stacked = jnp.concatenate([stacked, gains], axis=-1)
    sent = jnp.broadcast_to(stacked[None], (NY,) + stacked.shape).reshape(devices, -1)
    got = lax.all_to_all(sent, ("member", "tile"), split_axis=0, concat_axis=0, tiled=True)
    got = got.T
    values = got[: NY * slots].reshape(NY, slots * devices)
    errors = got[NY * slots : 2 * NY * slots].reshape(NY, slots * devices)
    gains = got[2 * NY * slots : 3 * NY * slots].reshape(NY, slots * devices)

    def of_core(array):
        mine = lax.dynamic_index_in_dim(
            array.reshape(devices, NY, NCORE, slots), core_pos, 2, False
        )
        return jnp.transpose(mine, (1, 2, 0)).reshape(NY, slots * devices)

    index = of_core(stencil_index[0])
    row_frac = of_core(row_fraction[0])
    column_frac = of_core(column_fraction[0])
    slot_ids = lax.broadcasted_iota(jnp.int32, stencil_index.shape[1:], 2)
    live = of_core((slot_ids < block_lengths[0][:, :, None]).astype(FLOAT))
    row_pos = index // width
    picks = column_pick(index % width, width)
    row_ids = lax.broadcasted_iota(jnp.int32, (NY, fine_rows, slots * devices), 1)
    row_factor = jnp.where(row_ids == row_pos[:, None], 1.0 - row_frac[:, None], 0.0) + jnp.where(
        row_ids == row_pos[:, None] + 1, row_frac[:, None], 0.0
    )

    base = background

    increment = owner_sum(
        partial_forward(low, weights, high, tile_pos, perturb, column_map), core_pos
    )
    regions = jnp.stack([base, turn(base, NCORE, "member"), turn(base, 2 * NCORE, "member"),
                         turn(base, 3 * NCORE, "member")])
    order = (y_pos - jnp.arange(NY)) % NY
    regions = jnp.take(regions, order, axis=0)
    state = interpolate(regions + increment, picks, row_factor, column_frac)
    residual, obs_weight = innovation(state, values, errors, gains)
    mine = spread_regions(residual * live, picks, row_factor, column_frac)
    other = swap_core(mine)
    even = jnp.where(core_pos == 0, mine, other)
    odd = jnp.where(core_pos == 0, other, mine)
    spread = jnp.transpose(jnp.stack([even, odd], axis=1), (2, 0, 1, 3)).reshape(fine_rows, -1)

    pulled = refine_adjoint(perturb * spread).astype(HALF)
    members_here, row_count, fine_cols = pulled.shape
    part = lax.dot_general(
        pulled.reshape(-1, fine_cols),
        column_map,
        (((1,), (1,)), ((), ())),
        preferred_element_type=FLOAT,
    ).reshape(members_here, row_count, -1)
    from_low = turn(part[:, 2:].astype(HALF), 1, "tile").astype(FLOAT)
    from_high = turn(part[:, :4].astype(HALF), -1, "tile").astype(FLOAT)
    full = (
        jnp.pad(part, ((0, 0), (2, 2), (0, 0)))
        + jnp.pad(from_low * (tile_pos > 0), ((0, 0), (0, 6), (0, 0)))
        + jnp.pad(from_high * (tile_pos < NTILE - 1), ((0, 0), (6, 0), (0, 0)))
    )
    gradient = weights + sweeps(full, tile_pos, -3)
    half_gradient = gradient.astype(HALF)
    grad_low, grad_high = turn(half_gradient, 1, "tile"), turn(half_gradient, -1, "tile")
    grad_square = jnp.sum(gradient * gradient)
    grad_image = owner_sum(
        partial_forward(grad_low, gradient, grad_high, tile_pos, perturb, column_map), core_pos
    )

    def own(array):
        return lax.dynamic_slice_in_dim(array, y_pos, 1, 0)

    grad_own = own(grad_image)
    grad_obs = interpolate(grad_own, own(picks), own(row_factor), own(column_frac))
    curvature = jnp.sum(own(live) * own(obs_weight) * grad_obs * grad_obs)
    pair = jnp.where(jnp.arange(128) < 64, grad_square, curvature)
    shared = lax.all_to_all(
        jnp.broadcast_to(pair[None], (devices, 128)),
        ("member", "tile"),
        split_axis=0,
        concat_axis=0,
        tiled=True,
    )
    totals = jnp.sum(shared, axis=0)
    step_size = totals[0] / (totals[0] + totals[127])
    return (weights - step_size * gradient, own(increment)[0] - step_size * grad_own[0])


def solution(mesh):
    placed = (
        P("member", "tile", None),
        P("member", "tile", None),
        P(),
        P("tile", "member"),
        P("tile", None, None, None),
        P("tile", None, None, None),
        P("tile", None, None, None),
        P("tile", None, None),
        P(("member", "tile"), None, None),
        P(("member", "tile"), None, None),
        P(("member", "tile")),
    )
    return jax.shard_map(
        shards,
        mesh=mesh,
        in_specs=placed,
        out_specs=(P("member", "tile", None), P("tile", "member")),
        check_vma=False,
    )
```

```python
import jax
import jax.numpy as jnp
import numpy as np
from jax import lax
from jax.experimental import pallas as pl
from jax.experimental.pallas import tpu as pltpu
from jax.sharding import PartitionSpec as P

RATIO = 4
KSM = 3
DIFFUSION = 0.45
NTILE = 16
NMEMBER = 8
NCORE = 2
NY = NMEMBER // NCORE
MEMBERS_HERE = 16
ROWS = 4
FINE_ROWS = 16
COARSE_COLS = 1280
FINE_COLS = 2560
WIDTH = 320
CHUNK = NCORE * WIDTH
SLOTS = 8
BATCHES = 128
FLOAT, HALF = jnp.float32, jnp.bfloat16


def refine_matrix():
    table = np.zeros((FINE_ROWS, ROWS + 2))
    for row in range(ROWS):
        for offset in range(RATIO):
            shift = (offset + 0.5) / RATIO - 0.5
            fine = RATIO * row + offset
            if shift < 0:
                table[fine, row + 1] += 1.0 + shift
                table[fine, row] -= shift
            else:
                table[fine, row + 1] += 1.0 - shift
                table[fine, row + 2] += shift
    return table


def member_matrix():
    return np.einsum("fr,kl->kfrl", refine_matrix(), np.eye(MEMBERS_HERE)).reshape(
        MEMBERS_HERE * FINE_ROWS, (ROWS + 2) * MEMBERS_HERE
    )


def turn(values, step, axis):
    count = lax.axis_size(axis)
    return lax.ppermute(values, axis, [(i, (i + step) % count) for i in range(count)])


def swap_core(values):
    return lax.ppermute(values, "member", [(i, i ^ 1) for i in range(NMEMBER)])


VMEM = pl.BlockSpec(memory_space=pltpu.VMEM)
SMEM = pl.BlockSpec(memory_space=pltpu.SMEM)


def call(kernel, out_shapes, arguments, smem=0, scratch=()):
    specs = [SMEM] * smem + [VMEM] * (len(arguments) - smem)
    return pl.pallas_call(
        kernel,
        out_shape=out_shapes,
        in_specs=specs,
        out_specs=jax.tree.map(lambda _: VMEM, out_shapes),
        scratch_shapes=list(scratch),
    )(*arguments)


def swept(rows, masks):
    for _ in range(KSM):
        rows = [v if m is None else v * m for v, m in zip(rows, masks)]
        rows = [
            rows[i] + DIFFUSION * (rows[i - 1] + rows[i + 1] - 2.0 * rows[i])
            for i in range(1, len(rows) - 1)
        ]
        masks = masks[1:-1]
    return [v if m is None else v * m for v, m in zip(rows, masks)]


def row_slice(row):
    return pl.ds(row * MEMBERS_HERE, MEMBERS_HERE)


def forward_kernel(
    place_ref, low_ref, own_ref, high_ref, perturb_ref, map_ref, refine_ref, out_ref, smooth_ref
):
    tile_pos, core_pos = place_ref[0], place_ref[1]
    below = jnp.where(tile_pos > 0, 1.0, 0.0)
    above = jnp.where(tile_pos < NTILE - 1, 1.0, 0.0)
    masks = [below] * 4 + [None] * 4 + [above] * 4
    for start in range(0, COARSE_COLS, 128):
        cols = pl.ds(start, 128)
        rows = [low_ref[row_slice(r), cols].astype(FLOAT) for r in range(4)]
        rows += [own_ref[row_slice(r), cols] for r in range(4)]
        rows += [high_ref[row_slice(r), cols].astype(FLOAT) for r in range(4)]
        for r, value in enumerate(swept(rows, masks)[0:]):
            smooth_ref[row_slice(r), cols] = value.astype(HALF)
    smooth = smooth_ref[...]
    for y in range(NY):
        cols = pl.ds(y * CHUNK, CHUNK)
        mapped = jnp.dot(smooth, map_ref[:, cols], preferred_element_type=FLOAT)
        high = mapped.astype(HALF)
        low = (mapped - high.astype(FLOAT)).astype(HALF)
        fine = jnp.dot(
            refine_ref[...], jnp.concatenate([high, low], axis=0), preferred_element_type=FLOAT
        )
        total = None
        for k in range(MEMBERS_HERE):
            term = fine[k * FINE_ROWS : (k + 1) * FINE_ROWS] * perturb_ref[k, :, cols].astype(FLOAT)
            total = term if total is None else total + term
        out_ref[core_pos, y] = total[:, :WIDTH]
        out_ref[1 - core_pos, y] = total[:, WIDTH:]


def partial_forward(place, low, own, high, perturb, column_map):
    matrix = member_matrix()
    matrix = jnp.asarray(np.concatenate([matrix, matrix], axis=1), HALF)
    return call(
        forward_kernel,
        jax.ShapeDtypeStruct((NCORE, NY, FINE_ROWS, WIDTH), FLOAT),
        (place, low, own, high, perturb, column_map, matrix),
        smem=1,
        scratch=[pltpu.VMEM(((ROWS + 2) * MEMBERS_HERE, COARSE_COLS), HALF)],
    )


def adjoint_kernel(
    place_ref, mine_ref, other_ref, perturb_ref, map_ref, back_ref, part_ref, up_ref, down_ref
):
    core_pos = place_ref[1]
    total = None
    for y in range(NY):
        cols = pl.ds(y * CHUNK, CHUNK)
        mine, other = mine_ref[y], other_ref[y]
        first = jnp.where(core_pos == 0, mine, other)
        second = jnp.where(core_pos == 0, other, mine)
        spread = jnp.concatenate([first, second], axis=1)
        highs, lows = [], []
        for k in range(MEMBERS_HERE):
            term = perturb_ref[k, :, cols].astype(FLOAT) * spread
            high = term.astype(HALF)
            highs.append(high)
            lows.append((term - high.astype(FLOAT)).astype(HALF))
        pulled = jnp.dot(
            back_ref[...], jnp.concatenate(highs + lows, axis=0), preferred_element_type=FLOAT
        )
        part = lax.dot_general(
            pulled.astype(HALF),
            map_ref[:, cols],
            (((1,), (1,)), ((), ())),
            preferred_element_type=FLOAT,
        )
        total = part if total is None else total + part
    part_ref[...] = total
    up_ref[...] = total[2 * MEMBERS_HERE :].astype(HALF)
    down_ref[...] = total[: 4 * MEMBERS_HERE].astype(HALF)


def partial_adjoint(place, mine, other, perturb, column_map):
    matrix = member_matrix().T
    matrix = jnp.asarray(np.concatenate([matrix, matrix], axis=1), HALF)
    rim = jax.ShapeDtypeStruct((4 * MEMBERS_HERE, COARSE_COLS), HALF)
    return call(
        adjoint_kernel,
        (jax.ShapeDtypeStruct(((ROWS + 2) * MEMBERS_HERE, COARSE_COLS), FLOAT), rim, rim),
        (place, mine, other, perturb, column_map, matrix),
        smem=1,
    )


def gradient_kernel(place_ref, low_ref, part_ref, high_ref, own_ref, grad_ref, half_ref, square_ref):
    tile_pos = place_ref[0]
    below = jnp.where(tile_pos > 0, 1.0, 0.0)
    above = jnp.where(tile_pos < NTILE - 1, 1.0, 0.0)
    masks = [below] * 3 + [None] * 4 + [above] * 3
    square = None
    for start in range(0, COARSE_COLS, 128):
        cols = pl.ds(start, 128)
        low = [low_ref[row_slice(r), cols].astype(FLOAT) for r in range(4)]
        part = [part_ref[row_slice(r), cols] for r in range(6)]
        high = [high_ref[row_slice(r), cols].astype(FLOAT) for r in range(4)]
        rows = [low[0], low[1], low[2] + part[0], low[3] * below + part[1], part[2], part[3]]
        rows += [part[4] + high[0] * above, part[5] + high[1], high[2], high[3]]
        for r, value in enumerate(swept(rows, masks)):
            gradient = own_ref[row_slice(r), cols] + value
            grad_ref[row_slice(r), cols] = gradient
            half_ref[row_slice(r), cols] = gradient.astype(HALF)
            term = gradient * gradient
            square = term if square is None else square + term
    square_ref[...] = square[:8] + square[8:]


def gradient_of(place, low, part, high, own):
    shape = (ROWS * MEMBERS_HERE, COARSE_COLS)
    return call(
        gradient_kernel,
        (
            jax.ShapeDtypeStruct(shape, FLOAT),
            jax.ShapeDtypeStruct(shape, HALF),
            jax.ShapeDtypeStruct((8, 128), FLOAT),
        ),
        (place, low, part, high, own),
        smem=1,
    )


def column_picks(column):
    ids = lax.broadcasted_iota(jnp.int32, (WIDTH, BATCHES), 0)
    return jnp.concatenate(
        [(ids == column[s : s + 1]).astype(FLOAT).astype(HALF) for s in range(SLOTS)], axis=1
    )


def row_factors(row, fraction):
    ids = lax.broadcasted_iota(jnp.int32, (FINE_ROWS, BATCHES), 0)
    return jnp.concatenate(
        [
            jnp.where(ids == row[s : s + 1], 1.0 - fraction[s : s + 1], 0.0)
            + jnp.where(ids == row[s : s + 1] + 1, fraction[s : s + 1], 0.0)
            for s in range(SLOTS)
        ],
        axis=1,
    )


def on_lanes(values):
    return jnp.concatenate([values[s : s + 1] for s in range(SLOTS)], axis=1)


def on_slots(values):
    return jnp.concatenate(
        [values[:, s * BATCHES : (s + 1) * BATCHES] for s in range(SLOTS)], axis=0
    )


def halves(values):
    high = values.astype(HALF)
    return jnp.concatenate([high, (values - high.astype(FLOAT)).astype(HALF)], axis=0)


def interpolated(field, picks, factors, fraction):
    got = jnp.dot(halves(field), picks, preferred_element_type=FLOAT)
    left = got[:FINE_ROWS] + got[FINE_ROWS:]
    shifted = jnp.concatenate([field[:, 1:], field[:, :1]], axis=1)
    got = jnp.dot(halves(shifted), picks, preferred_element_type=FLOAT)
    right = got[:FINE_ROWS] + got[FINE_ROWS:]
    mixed = left * (1.0 - fraction) + right * fraction
    return on_slots(jnp.sum(mixed * factors, axis=0, keepdims=True))


def located(index):
    row = index // WIDTH
    return row, index - row * WIDTH


def obs_kernel(
    place_ref, a_ref, b_ref, c_ref, d_ref, index_ref, row_ref, column_ref, live_ref, data_ref,
    spread_ref, weight_ref, full_ref,
):
    own = place_ref[2]
    data = jnp.transpose(data_ref[...])
    for y in range(NY):
        field = a_ref[y] + b_ref[y] + c_ref[y] + d_ref[y]
        row, column = located(index_ref[y])
        picks = column_picks(column)
        factors = row_factors(row, row_ref[y])
        fraction = on_lanes(column_ref[y])
        state = interpolated(field, picks, factors, fraction)
        value = data[y * SLOTS : (y + 1) * SLOTS]
        error = data[(NY + y) * SLOTS : (NY + y + 1) * SLOTS]
        gain = data[2 * NY * SLOTS : 2 * NY * SLOTS + SLOTS]
        bounded = jnp.tanh(state)
        derivative = 1.0 + gain * (1.0 - bounded * bounded)
        misfit = state + gain * bounded - value
        precision = live_ref[y] / (error * error)
        residual = derivative * misfit * precision
        weight_ref[y] = derivative * derivative * precision
        full_ref[y] = field
        weighted = factors * on_lanes(residual)
        spread = []
        for part in (weighted * (1.0 - fraction), weighted * fraction):
            got = lax.dot_general(
                halves(part), picks, (((1,), (1,)), ((), ())), preferred_element_type=FLOAT
            )
            spread.append(got[:FINE_ROWS] + got[FINE_ROWS:])
        left, right = spread
        spread_ref[y] = left + jnp.concatenate([right[:, -1:], right[:, :-1]], axis=1)


def obs_spread(place, pieces, index, row_frac, column_frac, live, data):
    regions = jax.ShapeDtypeStruct((NY, FINE_ROWS, WIDTH), FLOAT)
    return call(
        obs_kernel,
        (regions, jax.ShapeDtypeStruct((NY, SLOTS, BATCHES), FLOAT), regions),
        (place, *pieces, index, row_frac, column_frac, live, data),
        smem=1,
    )


def curve_kernel(
    place_ref, a_ref, b_ref, c_ref, d_ref, index_ref, row_ref, column_ref, weight_ref, square_ref,
    field_ref, sent_ref,
):
    own = place_ref[2]
    field = a_ref[...] + b_ref[...] + c_ref[...] + d_ref[...]
    field_ref[...] = field
    row, column = located(index_ref[own])
    observed = interpolated(
        field, column_picks(column), row_factors(row, row_ref[own]), on_lanes(column_ref[own])
    )
    curvature = jnp.sum(weight_ref[own] * observed * observed, keepdims=True)
    square = jnp.sum(square_ref[...], keepdims=True)
    lanes = lax.broadcasted_iota(jnp.int32, (BATCHES, 128), 1)
    sent_ref[...] = jnp.where(lanes < 64, square, curvature)


def curve_of(place, pieces, index, row_frac, column_frac, weight, square):
    return call(
        curve_kernel,
        (
            jax.ShapeDtypeStruct((FINE_ROWS, WIDTH), FLOAT),
            jax.ShapeDtypeStruct((BATCHES, 128), FLOAT),
        ),
        (place, *pieces, index, row_frac, column_frac, weight, square),
        smem=1,
    )


def step_kernel(
    place_ref, shared_ref, own_ref, grad_ref, full_ref, base_ref, image_ref, coarse_ref, increment_ref
):
    totals = jnp.sum(shared_ref[...], axis=0, keepdims=True)
    lanes = lax.broadcasted_iota(jnp.int32, (1, 128), 1)
    square = jnp.sum(jnp.where(lanes == 0, totals, 0.0), keepdims=True)
    curvature = jnp.sum(jnp.where(lanes == 127, totals, 0.0), keepdims=True)
    step = square / (square + curvature)
    coarse_ref[...] = own_ref[...] - step * grad_ref[...]
    increment_ref[...] = full_ref[place_ref[2]] - base_ref[...] - step * image_ref[...]


def stepped(place, shared, own, gradient, full, base, image):
    return call(
        step_kernel,
        (
            jax.ShapeDtypeStruct(own.shape, FLOAT),
            jax.ShapeDtypeStruct((FINE_ROWS, WIDTH), FLOAT),
        ),
        (place, shared, own, gradient, full, base, image),
        smem=1,
    )


def shards(
    perturb,
    weights,
    column_map,
    background,
    stencil_index,
    row_fraction,
    column_fraction,
    block_lengths,
    obs_value,
    obs_error,
    instrument_gain,
):
    member_pos = lax.axis_index("member")
    core_pos = member_pos % NCORE
    y_pos = member_pos // NCORE
    tile_pos = lax.axis_index("tile")
    place = jnp.stack([tile_pos, core_pos, y_pos]).astype(jnp.int32)

    flat = (ROWS * MEMBERS_HERE, COARSE_COLS)
    own = jnp.transpose(weights, (1, 0, 2)).reshape(flat)
    half = own.astype(HALF)
    low, high = turn(half, 1, "tile"), turn(half, -1, "tile")

    stacked = jnp.stack([obs_value[0], obs_error[0]])
    stacked = stacked.reshape(2, NY, NCORE, NTILE, SLOTS)
    stacked = jnp.transpose(stacked, (2, 3, 0, 1, 4)).reshape(NCORE, NTILE, 2 * NY * SLOTS)
    gains = jnp.broadcast_to(instrument_gain, (NCORE, NTILE, 2 * NY * SLOTS))
    stacked = jnp.concatenate([stacked, gains], axis=-1)
    sent = jnp.broadcast_to(stacked[None], (NY,) + stacked.shape).reshape(BATCHES, -1)
    data = lax.all_to_all(sent, ("member", "tile"), split_axis=0, concat_axis=0, tiled=True)

    def of_core(array):
        mine = lax.dynamic_index_in_dim(
            array.reshape(BATCHES, NY, NCORE, SLOTS), core_pos, 2, False
        )
        return jnp.transpose(mine, (1, 2, 0))

    index = of_core(stencil_index[0])
    row_frac = of_core(row_fraction[0])
    column_frac = of_core(column_fraction[0])
    slot_ids = lax.broadcasted_iota(jnp.int32, stencil_index.shape[1:], 2)
    live = of_core((slot_ids < block_lengths[0][:, :, None]).astype(FLOAT))

    first = partial_forward(place, low, own, high, perturb, column_map)
    ours = (jnp.arange(NY) == y_pos).astype(FLOAT)[:, None, None]
    mine = first[0] + swap_core(first[1]) + ours * background
    pieces = [mine] + [turn(mine, NCORE * i, "member") for i in range(1, NY)]
    spread, weight, full = obs_spread(place, pieces, index, row_frac, column_frac, live, data)
    part, up, down = partial_adjoint(place, spread, swap_core(spread), perturb, column_map)
    gradient, half, square = gradient_of(
        place, turn(up, 1, "tile"), part, turn(down, -1, "tile"), own
    )
    second = partial_forward(
        place, turn(half, 1, "tile"), gradient, turn(half, -1, "tile"), perturb, column_map
    )
    mine = second[0] + swap_core(second[1])

    def region(step):
        return lax.dynamic_index_in_dim(mine, (y_pos + step) % NY, 0, False)

    pieces = [region(0)] + [turn(region(i), NCORE * i, "member") for i in range(1, NY)]
    image, sent = curve_of(place, pieces, index, row_frac, column_frac, weight, square)
    shared = lax.all_to_all(sent, ("member", "tile"), split_axis=0, concat_axis=0, tiled=True)
    coarse, increment = stepped(place, shared, own, gradient, full, background, image)
    coarse = jnp.transpose(coarse.reshape(ROWS, MEMBERS_HERE, COARSE_COLS), (1, 0, 2))
    return coarse, increment


def solution(mesh):
    placed = (
        P("member", "tile", None),
        P("member", "tile", None),
        P(),
        P("tile", "member"),
        P("tile", None, None, None),
        P("tile", None, None, None),
        P("tile", None, None, None),
        P("tile", None, None),
        P(("member", "tile"), None, None),
        P(("member", "tile"), None, None),
        P(("member", "tile")),
    )
    return jax.shard_map(
        shards,
        mesh=mesh,
        in_specs=placed,
        out_specs=(P("member", "tile", None), P("tile", "member")),
        check_vma=False,
    )
```

```python
import jax
import jax.numpy as jnp
import numpy as np
from jax import lax
from jax.experimental import pallas as pl
from jax.experimental.pallas import tpu as pltpu
from jax.sharding import PartitionSpec as P

RATIO = 4
KSM = 3
DIFFUSION = 0.45
NTILE = 16
NMEMBER = 8
NCORE = 2
NY = NMEMBER // NCORE
MEMBERS_HERE = 16
ROWS = 4
FINE_ROWS = 16
COARSE_COLS = 1280
WIDTH = 320
CHUNK = NCORE * WIDTH
SLOTS = 8
BATCHES = 128
ROOM = 24 << 20
FLOAT, HALF = jnp.float32, jnp.bfloat16


def refine_matrix():
    table = np.zeros((FINE_ROWS, ROWS + 2))
    for row in range(ROWS):
        for offset in range(RATIO):
            shift = (offset + 0.5) / RATIO - 0.5
            fine = RATIO * row + offset
            if shift < 0:
                table[fine, row + 1] += 1.0 + shift
                table[fine, row] -= shift
            else:
                table[fine, row + 1] += 1.0 - shift
                table[fine, row + 2] += shift
    return table


def member_matrix():
    return np.einsum("fr,kl->kfrl", refine_matrix(), np.eye(MEMBERS_HERE)).reshape(
        MEMBERS_HERE * FINE_ROWS, (ROWS + 2) * MEMBERS_HERE
    )


def turn(values, step, axis):
    count = lax.axis_size(axis)
    return lax.ppermute(values, axis, [(i, (i + step) % count) for i in range(count)])


def swap_core(values):
    return lax.ppermute(values, "member", [(i, i ^ 1) for i in range(NMEMBER)])


NEAR = pl.BlockSpec(memory_space=pltpu.VMEM)
FAR = pl.BlockSpec(memory_space=pltpu.HBM)
SCALAR = pl.BlockSpec(memory_space=pltpu.SMEM)


def near(values):
    return pltpu.with_memory_space_constraint(values, pltpu.VMEM)


def distant(values):
    return pltpu.with_memory_space_constraint(values, pltpu.HBM)


def call(kernel, out_shapes, arguments, far=(), scratch=(), far_out=(), scalar=()):
    specs = [
        SCALAR if i in scalar else FAR if i in far else NEAR for i in range(len(arguments))
    ]
    arguments = tuple(
        x if i in scalar else distant(x) if i in far else near(x)
        for i, x in enumerate(arguments)
    )
    return pl.pallas_call(
        kernel,
        out_shape=tuple(
            jax.ShapeDtypeStruct(shape, kind) if i in far_out else pltpu.VMEM(shape, kind)
            for i, (shape, kind) in enumerate(out_shapes)
        ),
        in_specs=specs,
        out_specs=tuple(NEAR for _ in out_shapes),
        scratch_shapes=list(scratch),
        compiler_params=pltpu.CompilerParams(vmem_limit_bytes=ROOM),
        cost_estimate=pl.CostEstimate(flops=10**9, transcendentals=0, bytes_accessed=8 << 20),
    )(*arguments)


def place():
    member_pos = lax.axis_index("member")
    return lax.axis_index("tile"), lax.rem(member_pos, NCORE), lax.div(member_pos, NCORE)


def edges():
    tile_pos = lax.axis_index("tile")
    return jnp.where(tile_pos > 0, 1.0, 0.0), jnp.where(tile_pos < NTILE - 1, 1.0, 0.0)


def streams(perturb_ref, map_ref, perturb_buf, map_buf, sem):
    copies = []
    for y in range(NY):
        cols = pl.ds(y * CHUNK, CHUNK)
        copies.append(
            (
                pltpu.make_async_copy(map_ref.at[:, cols], map_buf.at[y], sem.at[0, y]),
                pltpu.make_async_copy(
                    perturb_ref.at[:, :, cols], perturb_buf.at[y], sem.at[1, y]
                ),
            )
        )
    return copies


BUFFERS = [
    pltpu.VMEM((NY, MEMBERS_HERE, FINE_ROWS, CHUNK), HALF),
    pltpu.VMEM((NY, COARSE_COLS, CHUNK), HALF),
    pltpu.SemaphoreType.DMA((2, NY)),
]


def swept(rows, masks):
    for _ in range(KSM):
        rows = [v if m is None else v * m for v, m in zip(rows, masks)]
        rows = [
            rows[i] + DIFFUSION * (rows[i - 1] + rows[i + 1] - 2.0 * rows[i])
            for i in range(1, len(rows) - 1)
        ]
        masks = masks[1:-1]
    return [v if m is None else v * m for v, m in zip(rows, masks)]


def row_slice(row):
    return pl.ds(row * MEMBERS_HERE, MEMBERS_HERE)


def forward_kernel(
    low_ref, own_ref, high_ref, refine_ref, perturb_ref, map_ref,
    mine_ref, other_ref, smooth_ref, perturb_buf, map_buf, sem,
):
    copies = streams(perturb_ref, map_ref, perturb_buf, map_buf, sem)
    for pair in copies:
        for copy in pair:
            copy.start()
    _, core_pos, _ = place()
    below, above = edges()
    masks = [below] * 4 + [None] * 4 + [above] * 4
    for start in range(0, COARSE_COLS, 128):
        cols = pl.ds(start, 128)
        rows = [low_ref[row_slice(r), cols].astype(FLOAT) for r in range(4)]
        rows += [own_ref[row_slice(r), cols] for r in range(4)]
        rows += [high_ref[row_slice(r), cols].astype(FLOAT) for r in range(4)]
        for r, value in enumerate(swept(rows, masks)):
            smooth_ref[row_slice(r), cols] = value.astype(HALF)
    smooth = smooth_ref[...]
    for y, (map_copy, perturb_copy) in enumerate(copies):
        map_copy.wait()
        mapped = jnp.dot(smooth, map_buf[y], preferred_element_type=FLOAT)
        high = mapped.astype(HALF)
        low = (mapped - high.astype(FLOAT)).astype(HALF)
        fine = jnp.dot(
            refine_ref[...], jnp.concatenate([high, low], axis=0), preferred_element_type=FLOAT
        )
        perturb_copy.wait()
        total = None
        for k in range(MEMBERS_HERE):
            term = fine[k * FINE_ROWS : (k + 1) * FINE_ROWS] * perturb_buf[y, k].astype(FLOAT)
            total = term if total is None else total + term
        first, second = total[:, :WIDTH], total[:, WIDTH:]
        mine_ref[y] = jnp.where(core_pos == 0, first, second)
        other_ref[y] = jnp.where(core_pos == 0, second, first)


REGIONS = ((NY, FINE_ROWS, WIDTH), FLOAT)


def partial_forward(low, own, high, perturb, column_map):
    matrix = member_matrix()
    matrix = jnp.asarray(np.concatenate([matrix, matrix], axis=1), HALF)
    return call(
        forward_kernel,
        (REGIONS, REGIONS),
        (low, own, high, matrix, perturb, column_map),
        far=(4, 5),
        scratch=[pltpu.VMEM(((ROWS + 2) * MEMBERS_HERE, COARSE_COLS), HALF)] + BUFFERS,
    )


def adjoint_kernel(
    mine_ref, other_ref, back_ref, perturb_ref, map_ref,
    part_ref, up_ref, down_ref, perturb_buf, map_buf, sem,
):
    copies = streams(perturb_ref, map_ref, perturb_buf, map_buf, sem)
    for pair in copies:
        for copy in pair[::-1]:
            copy.start()
    _, core_pos, _ = place()
    total = None
    for y, (map_copy, perturb_copy) in enumerate(copies):
        mine, other = mine_ref[y], other_ref[y]
        first = jnp.where(core_pos == 0, mine, other)
        second = jnp.where(core_pos == 0, other, mine)
        spread = jnp.concatenate([first, second], axis=1)
        perturb_copy.wait()
        highs, lows = [], []
        for k in range(MEMBERS_HERE):
            term = perturb_buf[y, k].astype(FLOAT) * spread
            high = term.astype(HALF)
            highs.append(high)
            lows.append((term - high.astype(FLOAT)).astype(HALF))
        pulled = jnp.dot(
            back_ref[...], jnp.concatenate(highs + lows, axis=0), preferred_element_type=FLOAT
        )
        map_copy.wait()
        part = lax.dot_general(
            pulled.astype(HALF),
            map_buf[y],
            (((1,), (1,)), ((), ())),
            preferred_element_type=FLOAT,
        )
        total = part if total is None else total + part
    part_ref[...] = total
    up_ref[...] = total[2 * MEMBERS_HERE :].astype(HALF)
    down_ref[...] = total[: 4 * MEMBERS_HERE].astype(HALF)


def partial_adjoint(mine, other, perturb, column_map):
    matrix = member_matrix().T
    matrix = jnp.asarray(np.concatenate([matrix, matrix], axis=1), HALF)
    rim = ((4 * MEMBERS_HERE, COARSE_COLS), HALF)
    return call(
        adjoint_kernel,
        ((((ROWS + 2) * MEMBERS_HERE, COARSE_COLS), FLOAT), rim, rim),
        (mine, other, matrix, perturb, column_map),
        far=(3, 4),
        scratch=BUFFERS,
    )


def gradient_kernel(low_ref, part_ref, high_ref, own_ref, grad_ref, half_ref, square_ref):
    below, above = edges()
    masks = [below] * 3 + [None] * 4 + [above] * 3
    square = None
    for start in range(0, COARSE_COLS, 128):
        cols = pl.ds(start, 128)
        low = [low_ref[row_slice(r), cols].astype(FLOAT) for r in range(4)]
        part = [part_ref[row_slice(r), cols] for r in range(6)]
        high = [high_ref[row_slice(r), cols].astype(FLOAT) for r in range(4)]
        rows = [low[0], low[1], low[2] + part[0], low[3] * below + part[1], part[2], part[3]]
        rows += [part[4] + high[0] * above, part[5] + high[1], high[2], high[3]]
        for r, value in enumerate(swept(rows, masks)):
            gradient = own_ref[row_slice(r), cols] + value
            grad_ref[row_slice(r), cols] = gradient
            half_ref[row_slice(r), cols] = gradient.astype(HALF)
            term = gradient * gradient
            square = term if square is None else square + term
    square_ref[...] = square[:8] + square[8:]


def gradient_of(low, part, high, own):
    shape = (ROWS * MEMBERS_HERE, COARSE_COLS)
    return call(
        gradient_kernel,
        ((shape, FLOAT), (shape, HALF), ((8, 128), FLOAT)),
        (low, part, high, own),
    )


def send_kernel(value_ref, error_ref, gain_ref, sent_ref):
    lanes = lax.broadcasted_iota(jnp.int32, (SLOTS, BATCHES), 1)
    block = lanes // (NCORE * NTILE)
    rows = []
    for ref in (value_ref, error_ref):
        values = ref[...]
        turned = [values] + [
            pltpu.roll(values, NCORE * NTILE * i, 1) for i in range(1, NY)
        ]
        for y in range(NY):
            out = turned[0]
            for j in range(NY):
                out = jnp.where(block == j, turned[(j - y) % NY], out)
            rows.append(out)
    gain = jnp.full((2 * NY * SLOTS, BATCHES), gain_ref[0], FLOAT)
    sent_ref[...] = jnp.transpose(jnp.concatenate(rows + [gain], axis=0))


def add_kernel(a_ref, b_ref, base_ref, out_ref):
    _, _, y_pos = place()
    for y in range(NY):
        out_ref[y] = a_ref[y] + b_ref[y]
    out_ref[y_pos] += base_ref[...]


def pick_kernel(a_ref, b_ref, *out_refs):
    _, _, y_pos = place()
    for step, ref in enumerate(out_refs):
        y = lax.rem(y_pos + step, NY)
        ref[...] = a_ref[y] + b_ref[y]


def column_picks(column):
    ids = lax.broadcasted_iota(jnp.int32, (WIDTH, BATCHES), 0)
    return jnp.concatenate(
        [(ids == column[s : s + 1]).astype(FLOAT).astype(HALF) for s in range(SLOTS)], axis=1
    )


def row_factors(row, fraction):
    ids = lax.broadcasted_iota(jnp.int32, (FINE_ROWS, BATCHES), 0)
    return jnp.concatenate(
        [
            jnp.where(ids == row[s : s + 1], 1.0 - fraction[s : s + 1], 0.0)
            + jnp.where(ids == row[s : s + 1] + 1, fraction[s : s + 1], 0.0)
            for s in range(SLOTS)
        ],
        axis=1,
    )


def on_lanes(values):
    return jnp.concatenate([values[s : s + 1] for s in range(SLOTS)], axis=1)


def on_slots(values):
    return jnp.concatenate(
        [values[:, s * BATCHES : (s + 1) * BATCHES] for s in range(SLOTS)], axis=0
    )


def halves(values):
    high = values.astype(HALF)
    return jnp.concatenate([high, (values - high.astype(FLOAT)).astype(HALF)], axis=0)


def interpolated(field, picks, factors, fraction):
    shifted = jnp.concatenate([field[:, 1:], field[:, :1]], axis=1)
    got = jnp.dot(
        halves(jnp.concatenate([field, shifted], axis=0)), picks, preferred_element_type=FLOAT
    )
    got = got[: 2 * FINE_ROWS] + got[2 * FINE_ROWS :]
    left, right = got[:FINE_ROWS], got[FINE_ROWS:]
    mixed = left * (1.0 - fraction) + right * fraction
    return on_slots(jnp.sum(mixed * factors, axis=0, keepdims=True))


def located(index):
    row = index // WIDTH
    return row, index - row * WIDTH


def obs_kernel(
    a_ref, b_ref, c_ref, d_ref, index_ref, row_ref, column_ref, length_ref, data_ref,
    spread_ref, weight_ref, full_ref,
):
    _, core_pos, y_pos = place()
    data = jnp.transpose(data_ref[...])
    gain = data[2 * NY * SLOTS : 2 * NY * SLOTS + SLOTS]
    slots = lax.broadcasted_iota(jnp.int32, (SLOTS, BATCHES), 0)
    for y in range(NY):
        field = a_ref[y] + b_ref[y] + c_ref[y] + d_ref[y]
        group = NCORE * y + core_pos
        row, column = located(index_ref[group])
        picks = column_picks(column)
        factors = row_factors(row, row_ref[group])
        fraction = on_lanes(column_ref[group])
        live = jnp.where(slots < length_ref[pl.ds(group, 1)], 1.0, 0.0)
        state = interpolated(field, picks, factors, fraction)
        value = data[y * SLOTS : (y + 1) * SLOTS]
        error = data[(NY + y) * SLOTS : (NY + y + 1) * SLOTS]
        bounded = jnp.tanh(state)
        derivative = 1.0 + gain * (1.0 - bounded * bounded)
        misfit = state + gain * bounded - value
        precision = live / (error * error)
        residual = derivative * misfit * precision

        @pl.when(y == y_pos)
        def _():
            weight_ref[...] = derivative * derivative * precision
            full_ref[...] = field

        weighted = factors * on_lanes(residual)
        both = jnp.concatenate([weighted * (1.0 - fraction), weighted * fraction], axis=0)
        got = lax.dot_general(
            halves(both), picks, (((1,), (1,)), ((), ())), preferred_element_type=FLOAT
        )
        got = got[: 2 * FINE_ROWS] + got[2 * FINE_ROWS :]
        left, right = got[:FINE_ROWS], got[FINE_ROWS:]
        spread_ref[y] = left + jnp.concatenate([right[:, -1:], right[:, :-1]], axis=1)


def curve_kernel(
    a_ref, b_ref, c_ref, d_ref, index_ref, row_ref, column_ref, weight_ref, square_ref,
    field_ref, sent_ref,
):
    _, core_pos, y_pos = place()
    own = NCORE * y_pos + core_pos
    field = a_ref[...] + b_ref[...] + c_ref[...] + d_ref[...]
    field_ref[...] = field
    row, column = located(index_ref[own])
    observed = interpolated(
        field, column_picks(column), row_factors(row, row_ref[own]), on_lanes(column_ref[own])
    )
    curvature = jnp.sum(weight_ref[...] * observed * observed, keepdims=True)
    square = jnp.sum(square_ref[...], keepdims=True)
    lanes = lax.broadcasted_iota(jnp.int32, (BATCHES, 128), 1)
    sent_ref[...] = jnp.where(lanes < 64, square, curvature)


def step_kernel(
    shared_ref, own_ref, grad_ref, full_ref, base_ref, image_ref, coarse_ref, increment_ref
):
    totals = jnp.sum(shared_ref[...], axis=0, keepdims=True)
    lanes = lax.broadcasted_iota(jnp.int32, (1, 128), 1)
    square = jnp.sum(jnp.where(lanes == 0, totals, 0.0), keepdims=True)
    curvature = jnp.sum(jnp.where(lanes == 127, totals, 0.0), keepdims=True)
    step = square / (square + curvature)
    for r in range(ROWS):
        coarse_ref[:, r, :] = own_ref[row_slice(r)] - step * grad_ref[row_slice(r)]
    increment_ref[...] = full_ref[...] - base_ref[...] - step * image_ref[...]


def shards(
    perturb,
    weights,
    column_map,
    background,
    stencil_index,
    row_fraction,
    column_fraction,
    block_lengths,
    obs_value,
    obs_error,
    instrument_gain,
):
    flat = (ROWS * MEMBERS_HERE, COARSE_COLS)
    own = jnp.transpose(weights, (1, 0, 2)).reshape(flat)
    half = own.astype(HALF)
    low, high = turn(half, 1, "tile"), turn(half, -1, "tile")

    (sent,) = call(
        send_kernel,
        (((BATCHES, BATCHES), FLOAT),),
        (obs_value[0].T, obs_error[0].T, instrument_gain),
        scalar=(2,),
    )
    data = lax.all_to_all(sent, ("member", "tile"), split_axis=0, concat_axis=0, tiled=True)

    index = jnp.transpose(stencil_index[0], (1, 2, 0))
    row_frac = jnp.transpose(row_fraction[0], (1, 2, 0))
    column_frac = jnp.transpose(column_fraction[0], (1, 2, 0))
    lengths = block_lengths[0].T

    mine, other = partial_forward(low, own, high, perturb, column_map)
    (mine,) = call(add_kernel, (REGIONS,), (mine, swap_core(other), background))
    pieces = [mine] + [turn(mine, NCORE * i, "member") for i in range(1, NY)]
    region = ((FINE_ROWS, WIDTH), FLOAT)
    spread, weight, full = call(
        obs_kernel,
        (REGIONS, ((SLOTS, BATCHES), FLOAT), region),
        (*pieces, index, row_frac, column_frac, lengths, data),
    )
    part, up, down = partial_adjoint(spread, swap_core(spread), perturb, column_map)
    gradient, half, square = gradient_of(turn(up, 1, "tile"), part, turn(down, -1, "tile"), own)
    mine, other = partial_forward(
        turn(half, 1, "tile"), gradient, turn(half, -1, "tile"), perturb, column_map
    )
    pieces = call(pick_kernel, (region,) * NY, (mine, swap_core(other)))
    pieces = [pieces[0]] + [turn(pieces[i], NCORE * i, "member") for i in range(1, NY)]
    image, sent = call(
        curve_kernel,
        (region, ((BATCHES, 128), FLOAT)),
        (*pieces, index, row_frac, column_frac, weight, square),
    )
    shared = lax.all_to_all(sent, ("member", "tile"), split_axis=0, concat_axis=0, tiled=True)
    return call(
        step_kernel,
        (((MEMBERS_HERE, ROWS, COARSE_COLS), FLOAT), region),
        (shared, own, gradient, full, background, image),
        far_out=(0, 1),
    )


def solution(mesh):
    placed = (
        P("member", "tile", None),
        P("member", "tile", None),
        P(),
        P("tile", "member"),
        P("tile", None, None, None),
        P("tile", None, None, None),
        P("tile", None, None, None),
        P("tile", None, None),
        P(("member", "tile"), None, None),
        P(("member", "tile"), None, None),
        P(("member", "tile")),
    )
    return jax.shard_map(
        shards,
        mesh=mesh,
        in_specs=placed,
        out_specs=(P("member", "tile", None), P("tile", "member")),
        check_vma=False,
    )
```

```python
import jax
import jax.numpy as jnp
import numpy as np
from jax import lax
from jax.experimental import pallas as pl
from jax.experimental.pallas import tpu as pltpu
from jax.sharding import PartitionSpec as P

RATIO = 4
KSM = 3
DIFFUSION = 0.45
NTILE = 16
NMEMBER = 8
NCORE = 2
NY = NMEMBER // NCORE
MEMBERS_HERE = 16
ROWS = 4
FINE_ROWS = 16
COARSE_COLS = 1280
WIDTH = 320
CHUNK = NCORE * WIDTH
SLOTS = 8
BATCHES = 128
ROOM = 12 << 20
FLOAT, HALF = jnp.float32, jnp.bfloat16


def refine_matrix():
    table = np.zeros((FINE_ROWS, ROWS + 2))
    for row in range(ROWS):
        for offset in range(RATIO):
            shift = (offset + 0.5) / RATIO - 0.5
            fine = RATIO * row + offset
            if shift < 0:
                table[fine, row + 1] += 1.0 + shift
                table[fine, row] -= shift
            else:
                table[fine, row + 1] += 1.0 - shift
                table[fine, row + 2] += shift
    return table


def member_matrix():
    return np.einsum("fr,kl->kfrl", refine_matrix(), np.eye(MEMBERS_HERE)).reshape(
        MEMBERS_HERE * FINE_ROWS, (ROWS + 2) * MEMBERS_HERE
    )


def turn(values, step, axis):
    count = lax.axis_size(axis)
    return lax.ppermute(values, axis, [(i, (i + step) % count) for i in range(count)])


def swap_near(values):
    return lax.ppermute(values, "tile", [(i, i ^ 1) for i in range(NTILE)])


def swap_far(values):
    pairs = [(0, 0), (NTILE - 1, NTILE - 1)]
    for i in range(1, NTILE - 1, 2):
        pairs += [(i, i + 1), (i + 1, i)]
    return lax.ppermute(values, "tile", pairs)


def swap_core(values):
    return lax.ppermute(values, "member", [(i, i ^ 1) for i in range(NMEMBER)])


NEAR = pl.BlockSpec(memory_space=pltpu.VMEM)
FAR = pl.BlockSpec(memory_space=pltpu.HBM)
SCALAR = pl.BlockSpec(memory_space=pltpu.SMEM)


def near(values):
    return pltpu.with_memory_space_constraint(values, pltpu.VMEM)


def distant(values):
    return pltpu.with_memory_space_constraint(values, pltpu.HBM)


def call(kernel, out_shapes, arguments, far=(), scratch=(), far_out=(), scalar=()):
    specs = [
        SCALAR if i in scalar else FAR if i in far else NEAR for i in range(len(arguments))
    ]
    arguments = tuple(
        x if i in scalar else distant(x) if i in far else near(x)
        for i, x in enumerate(arguments)
    )
    return pl.pallas_call(
        kernel,
        out_shape=tuple(
            jax.ShapeDtypeStruct(shape, kind) if i in far_out else pltpu.VMEM(shape, kind)
            for i, (shape, kind) in enumerate(out_shapes)
        ),
        in_specs=specs,
        out_specs=tuple(NEAR for _ in out_shapes),
        scratch_shapes=list(scratch),
        compiler_params=pltpu.CompilerParams(vmem_limit_bytes=ROOM),
        cost_estimate=pl.CostEstimate(flops=10**9, transcendentals=0, bytes_accessed=8 << 20),
    )(*arguments)


def place():
    member_pos = lax.axis_index("member")
    return lax.axis_index("tile"), lax.rem(member_pos, NCORE), lax.div(member_pos, NCORE)


def edges():
    tile_pos = lax.axis_index("tile")
    return jnp.where(tile_pos > 0, 1.0, 0.0), jnp.where(tile_pos < NTILE - 1, 1.0, 0.0)


def swept(rows, masks):
    for _ in range(KSM):
        rows = [v if m is None else v * m for v, m in zip(rows, masks)]
        rows = [
            rows[i] + DIFFUSION * (rows[i - 1] + rows[i + 1] - 2.0 * rows[i])
            for i in range(1, len(rows) - 1)
        ]
        masks = masks[1:-1]
    return [v if m is None else v * m for v, m in zip(rows, masks)]


def row_slice(row):
    return pl.ds(row * MEMBERS_HERE, MEMBERS_HERE)


def is_even():
    return lax.rem(lax.axis_index("tile"), 2) == 0


def sides(a_ref, b_ref, cols, even):
    first = [a_ref[row_slice(r), cols].astype(FLOAT) for r in range(4)]
    second = [b_ref[row_slice(r), cols].astype(FLOAT) for r in range(4)]
    low = [jnp.where(even, v, u) for u, v in zip(first, second)]
    high = [jnp.where(even, u, v) for u, v in zip(first, second)]
    return low, high


def streamed_kernel(
    a_ref, own_ref, b_ref, refine_hbm, perturb_hbm, map_hbm, after_ref,
    mine_ref, other_ref, refine_ref, perturb_ref, map_ref, smooth_ref, sem,
):
    copies = [(pltpu.make_async_copy(refine_hbm, refine_ref, sem.at[0, NY]),)]
    for y in range(NY):
        cols = pl.ds(y * CHUNK, CHUNK)
        copies.append(
            (
                pltpu.make_async_copy(map_hbm.at[:, cols], map_ref.at[:, cols], sem.at[0, y]),
                pltpu.make_async_copy(
                    perturb_hbm.at[:, :, cols], perturb_ref.at[:, :, cols], sem.at[1, y]
                ),
            )
        )
    for group in copies[1:2] + copies[:1] + copies[2:]:
        for copy in group:
            copy.start()

    def arrived(y):
        for copy in copies[y + 1] + (copies[0] if y == 0 else ()):
            copy.wait()

    forward_kernel(
        a_ref, own_ref, b_ref, refine_ref, perturb_ref, map_ref, mine_ref, other_ref, smooth_ref,
        arrived=arrived,
    )


def forward_kernel(
    a_ref, own_ref, b_ref, refine_ref, perturb_ref, map_ref, mine_ref, other_ref, smooth_ref,
    arrived=None,
):
    _, core_pos, _ = place()
    even = is_even()
    below, above = edges()
    masks = [below] * 4 + [None] * 4 + [above] * 4
    for start in range(0, COARSE_COLS, 128):
        cols = pl.ds(start, 128)
        low, high = sides(a_ref, b_ref, cols, even)
        rows = low + [own_ref[row_slice(r), cols] for r in range(4)] + high
        for r, value in enumerate(swept(rows, masks)):
            smooth_ref[row_slice(r), cols] = value.astype(HALF)
    smooth = smooth_ref[...]
    for y in range(NY):
        cols = pl.ds(y * CHUNK, CHUNK)
        if arrived is not None:
            arrived(y)
        mapped = jnp.dot(smooth, map_ref[:, cols], preferred_element_type=FLOAT)
        high = mapped.astype(HALF)
        low = (mapped - high.astype(FLOAT)).astype(HALF)
        fine = jnp.dot(
            refine_ref[...], jnp.concatenate([high, low], axis=0), preferred_element_type=FLOAT
        )
        total = None
        for k in range(MEMBERS_HERE):
            term = fine[k * FINE_ROWS : (k + 1) * FINE_ROWS] * perturb_ref[k, :, cols].astype(FLOAT)
            total = term if total is None else total + term
        first, second = total[:, :WIDTH], total[:, WIDTH:]
        mine_ref[y] = jnp.where(core_pos == 0, first, second)
        other_ref[y] = jnp.where(core_pos == 0, second, first)


REGIONS = ((NY, FINE_ROWS, WIDTH), FLOAT)


SMOOTH = pltpu.VMEM(((ROWS + 2) * MEMBERS_HERE, COARSE_COLS), HALF)


def first_forward(first, own, second, perturb, column_map, after):
    matrix = member_matrix()
    matrix = jnp.asarray(np.concatenate([matrix, matrix], axis=1), HALF)
    operators = (matrix, perturb, column_map)
    return call(
        streamed_kernel,
        (REGIONS, REGIONS) + tuple((x.shape, x.dtype) for x in operators),
        (first, own, second) + operators + (after,),
        far=(3, 4, 5),
        scratch=[SMOOTH, pltpu.SemaphoreType.DMA((2, NY + 1))],
    )


def later_forward(first, own, second, *operators):
    return call(
        forward_kernel, (REGIONS, REGIONS), (first, own, second) + operators, scratch=[SMOOTH]
    )


def adjoint_kernel(
    mine_ref, other_ref, back_ref, perturb_ref, map_ref,
    part_ref, a_ref, b_ref,
):
    _, core_pos, _ = place()
    even = is_even()
    total = None
    for y in range(NY):
        cols = pl.ds(y * CHUNK, CHUNK)
        mine, other = mine_ref[y], other_ref[y]
        first = jnp.where(core_pos == 0, mine, other)
        second = jnp.where(core_pos == 0, other, mine)
        spread = jnp.concatenate([first, second], axis=1)
        highs, lows = [], []
        for k in range(MEMBERS_HERE):
            term = perturb_ref[k, :, cols].astype(FLOAT) * spread
            high = term.astype(HALF)
            highs.append(high)
            lows.append((term - high.astype(FLOAT)).astype(HALF))
        pulled = jnp.dot(
            back_ref[...], jnp.concatenate(highs + lows, axis=0), preferred_element_type=FLOAT
        )
        part = lax.dot_general(
            pulled.astype(HALF),
            map_ref[:, cols],
            (((1,), (1,)), ((), ())),
            preferred_element_type=FLOAT,
        )
        total = part if total is None else total + part
    part_ref[...] = total
    up = total[2 * MEMBERS_HERE :].astype(HALF)
    down = total[: 4 * MEMBERS_HERE].astype(HALF)
    a_ref[...] = jnp.where(even, up, down)
    b_ref[...] = jnp.where(even, down, up)


def partial_adjoint(mine, other, perturb, column_map):
    matrix = member_matrix().T
    matrix = jnp.asarray(np.concatenate([matrix, matrix], axis=1), HALF)
    rim = ((4 * MEMBERS_HERE, COARSE_COLS), HALF)
    return call(
        adjoint_kernel,
        ((((ROWS + 2) * MEMBERS_HERE, COARSE_COLS), FLOAT), rim, rim),
        (mine, other, matrix, perturb, column_map),
    )


def gradient_kernel(a_ref, part_ref, b_ref, own_ref, grad_ref, half_ref, square_ref):
    below, above = edges()
    masks = [below] * 3 + [None] * 4 + [above] * 3
    even = is_even()
    square = None
    for start in range(0, COARSE_COLS, 128):
        cols = pl.ds(start, 128)
        low, high = sides(a_ref, b_ref, cols, even)
        part = [part_ref[row_slice(r), cols] for r in range(6)]
        rows = [low[0], low[1], low[2] + part[0], low[3] * below + part[1], part[2], part[3]]
        rows += [part[4] + high[0] * above, part[5] + high[1], high[2], high[3]]
        for r, value in enumerate(swept(rows, masks)):
            gradient = own_ref[row_slice(r), cols] + value
            grad_ref[row_slice(r), cols] = gradient
            half_ref[row_slice(r), cols] = gradient.astype(HALF)
            term = gradient * gradient
            square = term if square is None else square + term
    square_ref[...] = square[:8] + square[8:]


def gradient_of(low, part, high, own):
    shape = (ROWS * MEMBERS_HERE, COARSE_COLS)
    return call(
        gradient_kernel,
        ((shape, FLOAT), (shape, HALF), ((8, 128), FLOAT)),
        (low, part, high, own),
    )


def send_kernel(value_hbm, error_hbm, gain_ref, sent_ref, value_ref, error_ref, sem):
    copies = [
        pltpu.make_async_copy(value_hbm, value_ref, sem.at[0]),
        pltpu.make_async_copy(error_hbm, error_ref, sem.at[1]),
    ]
    for copy in copies:
        copy.start()
    for copy in copies:
        copy.wait()
    lanes = lax.broadcasted_iota(jnp.int32, (SLOTS, BATCHES), 1)
    block = lanes // (NCORE * NTILE)
    rows = []
    for ref in (value_ref, error_ref):
        values = ref[...]
        turned = [values] + [
            pltpu.roll(values, NCORE * NTILE * i, 1) for i in range(1, NY)
        ]
        for y in range(NY):
            out = turned[0]
            for j in range(NY):
                out = jnp.where(block == j, turned[(j - y) % NY], out)
            rows.append(out)
    gain = jnp.full((2 * NY * SLOTS, BATCHES), gain_ref[0], FLOAT)
    sent_ref[...] = jnp.transpose(jnp.concatenate(rows + [gain], axis=0))


def add_kernel(a_ref, b_ref, base_ref, out_ref):
    _, _, y_pos = place()
    for y in range(NY):
        out_ref[y] = a_ref[y] + b_ref[y]
    out_ref[y_pos] += base_ref[...]


def pick_kernel(a_ref, b_ref, *out_refs):
    _, _, y_pos = place()
    for step, ref in enumerate(out_refs):
        y = lax.rem(y_pos + step, NY)
        ref[...] = a_ref[y] + b_ref[y]


def column_picks(column):
    ids = lax.broadcasted_iota(jnp.int32, (WIDTH, BATCHES), 0)
    return jnp.concatenate(
        [(ids == column[s : s + 1]).astype(FLOAT).astype(HALF) for s in range(SLOTS)], axis=1
    )


def row_factors(row, fraction):
    ids = lax.broadcasted_iota(jnp.int32, (FINE_ROWS, BATCHES), 0)
    return jnp.concatenate(
        [
            jnp.where(ids == row[s : s + 1], 1.0 - fraction[s : s + 1], 0.0)
            + jnp.where(ids == row[s : s + 1] + 1, fraction[s : s + 1], 0.0)
            for s in range(SLOTS)
        ],
        axis=1,
    )


def on_lanes(values):
    return jnp.concatenate([values[s : s + 1] for s in range(SLOTS)], axis=1)


def on_slots(values):
    return jnp.concatenate(
        [values[:, s * BATCHES : (s + 1) * BATCHES] for s in range(SLOTS)], axis=0
    )


def halves(values):
    high = values.astype(HALF)
    return jnp.concatenate([high, (values - high.astype(FLOAT)).astype(HALF)], axis=0)


def interpolated(field, picks, factors, fraction):
    shifted = jnp.concatenate([field[:, 1:], field[:, :1]], axis=1)
    got = jnp.dot(
        halves(jnp.concatenate([field, shifted], axis=0)), picks, preferred_element_type=FLOAT
    )
    got = got[: 2 * FINE_ROWS] + got[2 * FINE_ROWS :]
    left, right = got[:FINE_ROWS], got[FINE_ROWS:]
    mixed = left * (1.0 - fraction) + right * fraction
    return on_slots(jnp.sum(mixed * factors, axis=0, keepdims=True))


def located(index):
    row = index // WIDTH
    return row, index - row * WIDTH


def obs_kernel(
    a_ref, b_ref, c_ref, d_ref, index_ref, row_ref, column_ref, length_ref, data_ref,
    spread_ref, weight_ref, full_ref,
):
    _, core_pos, y_pos = place()
    data = jnp.transpose(data_ref[...])
    gain = data[2 * NY * SLOTS : 2 * NY * SLOTS + SLOTS]
    slots = lax.broadcasted_iota(jnp.int32, (SLOTS, BATCHES), 0)
    for y in range(NY):
        field = a_ref[y] + b_ref[y] + c_ref[y] + d_ref[y]
        group = NCORE * y + core_pos
        row, column = located(index_ref[group])
        picks = column_picks(column)
        factors = row_factors(row, row_ref[group])
        fraction = on_lanes(column_ref[group])
        live = jnp.where(slots < length_ref[pl.ds(group, 1)], 1.0, 0.0)
        state = interpolated(field, picks, factors, fraction)
        value = data[y * SLOTS : (y + 1) * SLOTS]
        error = data[(NY + y) * SLOTS : (NY + y + 1) * SLOTS]
        bounded = jnp.tanh(state)
        derivative = 1.0 + gain * (1.0 - bounded * bounded)
        misfit = state + gain * bounded - value
        precision = live / (error * error)
        residual = derivative * misfit * precision

        @pl.when(y == y_pos)
        def _():
            weight_ref[...] = derivative * derivative * precision
            full_ref[...] = field

        weighted = factors * on_lanes(residual)
        both = jnp.concatenate([weighted * (1.0 - fraction), weighted * fraction], axis=0)
        got = lax.dot_general(
            halves(both), picks, (((1,), (1,)), ((), ())), preferred_element_type=FLOAT
        )
        got = got[: 2 * FINE_ROWS] + got[2 * FINE_ROWS :]
        left, right = got[:FINE_ROWS], got[FINE_ROWS:]
        spread_ref[y] = left + jnp.concatenate([right[:, -1:], right[:, :-1]], axis=1)


def curve_kernel(
    a_ref, b_ref, c_ref, d_ref, index_ref, row_ref, column_ref, weight_ref, square_ref,
    field_ref, sent_ref,
):
    _, core_pos, y_pos = place()
    own = NCORE * y_pos + core_pos
    field = a_ref[...] + b_ref[...] + c_ref[...] + d_ref[...]
    field_ref[...] = field
    row, column = located(index_ref[own])
    observed = interpolated(
        field, column_picks(column), row_factors(row, row_ref[own]), on_lanes(column_ref[own])
    )
    curvature = jnp.sum(weight_ref[...] * observed * observed, keepdims=True)
    square = jnp.sum(square_ref[...], keepdims=True)
    lanes = lax.broadcasted_iota(jnp.int32, (BATCHES, 128), 1)
    sent_ref[...] = jnp.where(lanes < 64, square, curvature)


def step_kernel(
    shared_ref, own_ref, grad_ref, full_ref, base_ref, image_ref, coarse_ref, increment_ref
):
    totals = jnp.sum(shared_ref[...], axis=0, keepdims=True)
    lanes = lax.broadcasted_iota(jnp.int32, (1, 128), 1)
    square = jnp.sum(jnp.where(lanes == 0, totals, 0.0), keepdims=True)
    curvature = jnp.sum(jnp.where(lanes == 127, totals, 0.0), keepdims=True)
    step = square / (square + curvature)
    for r in range(ROWS):
        coarse_ref[:, r, :] = own_ref[row_slice(r)] - step * grad_ref[row_slice(r)]
    increment_ref[...] = full_ref[...] - base_ref[...] - step * image_ref[...]


def shards(
    perturb,
    weights,
    column_map,
    background,
    stencil_index,
    row_fraction,
    column_fraction,
    block_lengths,
    obs_value,
    obs_error,
    instrument_gain,
):
    flat = (ROWS * MEMBERS_HERE, COARSE_COLS)
    own = jnp.transpose(weights, (1, 0, 2)).reshape(flat)
    half = own.astype(HALF)
    near_rows, far_rows = swap_near(half), swap_far(half)

    (sent,) = call(
        send_kernel,
        (((BATCHES, BATCHES), FLOAT),),
        (obs_value[0].T, obs_error[0].T, instrument_gain),
        far=(0, 1),
        scalar=(2,),
        scratch=[pltpu.VMEM((SLOTS, BATCHES), FLOAT)] * 2 + [pltpu.SemaphoreType.DMA((2,))],
    )
    data = lax.all_to_all(sent, ("member", "tile"), split_axis=0, concat_axis=0, tiled=True)

    index = jnp.transpose(stencil_index[0], (1, 2, 0))
    row_frac = jnp.transpose(row_fraction[0], (1, 2, 0))
    column_frac = jnp.transpose(column_fraction[0], (1, 2, 0))
    lengths = block_lengths[0].T

    mine, other, matrix, perturb, column_map = first_forward(
        near_rows, own, far_rows, perturb, column_map, data
    )
    (mine,) = call(add_kernel, (REGIONS,), (mine, swap_core(other), background))
    pieces = [mine] + [turn(mine, NCORE * i, "member") for i in range(1, NY)]
    region = ((FINE_ROWS, WIDTH), FLOAT)
    spread, weight, full = call(
        obs_kernel,
        (REGIONS, ((SLOTS, BATCHES), FLOAT), region),
        (*pieces, index, row_frac, column_frac, lengths, data),
    )
    part, up, down = partial_adjoint(spread, swap_core(spread), perturb, column_map)
    gradient, half, square = gradient_of(swap_near(up), part, swap_far(down), own)
    mine, other = later_forward(
        swap_near(half), gradient, swap_far(half), matrix, perturb, column_map
    )
    pieces = call(pick_kernel, (region,) * NY, (mine, swap_core(other)))
    pieces = [pieces[0]] + [turn(pieces[i], NCORE * i, "member") for i in range(1, NY)]
    image, sent = call(
        curve_kernel,
        (region, ((BATCHES, 128), FLOAT)),
        (*pieces, index, row_frac, column_frac, weight, square),
    )
    shared = lax.all_to_all(sent, ("member", "tile"), split_axis=0, concat_axis=0, tiled=True)
    return call(
        step_kernel,
        (((MEMBERS_HERE, ROWS, COARSE_COLS), FLOAT), region),
        (shared, own, gradient, full, background, image),
        far_out=(0, 1),
    )


def solution(mesh):
    placed = (
        P("member", "tile", None),
        P("member", "tile", None),
        P(),
        P("tile", "member"),
        P("tile", None, None, None),
        P("tile", None, None, None),
        P("tile", None, None, None),
        P("tile", None, None),
        P(("member", "tile"), None, None),
        P(("member", "tile"), None, None),
        P(("member", "tile")),
    )
    return jax.shard_map(
        shards,
        mesh=mesh,
        in_specs=placed,
        out_specs=(P("member", "tile", None), P("tile", "member")),
        check_vma=False,
    )
```

```python
import jax
import jax.numpy as jnp
import numpy as np
from jax import lax
from jax.experimental import pallas as pl
from jax.experimental.pallas import tpu as pltpu
from jax.sharding import PartitionSpec as P

RATIO = 4
KSM = 3
DIFFUSION = 0.45
NTILE = 16
NMEMBER = 8
NCORE = 2
NY = NMEMBER // NCORE
MEMBERS_HERE = 16
ROWS = 4
FINE_ROWS = 16
COARSE_COLS = 1280
WIDTH = 320
CHUNK = NCORE * WIDTH
SLOTS = 8
BATCHES = 128
ROOM = 12 << 20
FLOAT, HALF = jnp.float32, jnp.bfloat16


def refine_matrix():
    table = np.zeros((FINE_ROWS, ROWS + 2))
    for row in range(ROWS):
        for offset in range(RATIO):
            shift = (offset + 0.5) / RATIO - 0.5
            fine = RATIO * row + offset
            if shift < 0:
                table[fine, row + 1] += 1.0 + shift
                table[fine, row] -= shift
            else:
                table[fine, row + 1] += 1.0 - shift
                table[fine, row + 2] += shift
    return table


def member_matrix():
    return np.einsum("fr,kl->kfrl", refine_matrix(), np.eye(MEMBERS_HERE)).reshape(
        MEMBERS_HERE * FINE_ROWS, (ROWS + 2) * MEMBERS_HERE
    )


def turn(values, step, axis):
    count = lax.axis_size(axis)
    return lax.ppermute(values, axis, [(i, (i + step) % count) for i in range(count)])


def swap_near(values):
    return lax.ppermute(values, "tile", [(i, i ^ 1) for i in range(NTILE)])


def swap_far(values):
    pairs = [(0, 0), (NTILE - 1, NTILE - 1)]
    for i in range(1, NTILE - 1, 2):
        pairs += [(i, i + 1), (i + 1, i)]
    return lax.ppermute(values, "tile", pairs)


def swap_both(near_values, far_values):
    near_rows = swap_near(near_values)
    far_rows = swap_far(far_values)
    return near_rows, far_rows


def swap_core(values):
    return lax.ppermute(values, "member", [(i, i ^ 1) for i in range(NMEMBER)])


NEAR = pl.BlockSpec(memory_space=pltpu.VMEM)
FAR = pl.BlockSpec(memory_space=pltpu.HBM)
SCALAR = pl.BlockSpec(memory_space=pltpu.SMEM)


def near(values):
    return pltpu.with_memory_space_constraint(values, pltpu.VMEM)


def distant(values):
    return pltpu.with_memory_space_constraint(values, pltpu.HBM)


def call(kernel, out_shapes, arguments, far=(), scratch=(), far_out=(), scalar=()):
    specs = [
        SCALAR if i in scalar else FAR if i in far else NEAR for i in range(len(arguments))
    ]
    arguments = tuple(
        x if i in scalar else distant(x) if i in far else near(x)
        for i, x in enumerate(arguments)
    )
    return pl.pallas_call(
        kernel,
        out_shape=tuple(
            jax.ShapeDtypeStruct(shape, kind) if i in far_out else pltpu.VMEM(shape, kind)
            for i, (shape, kind) in enumerate(out_shapes)
        ),
        in_specs=specs,
        out_specs=tuple(NEAR for _ in out_shapes),
        scratch_shapes=list(scratch),
        compiler_params=pltpu.CompilerParams(vmem_limit_bytes=ROOM),
        cost_estimate=pl.CostEstimate(flops=10**9, transcendentals=0, bytes_accessed=8 << 20),
    )(*arguments)


def place():
    member_pos = lax.axis_index("member")
    return lax.axis_index("tile"), lax.rem(member_pos, NCORE), lax.div(member_pos, NCORE)


def edges():
    tile_pos = lax.axis_index("tile")
    return jnp.where(tile_pos > 0, 1.0, 0.0), jnp.where(tile_pos < NTILE - 1, 1.0, 0.0)


def swept(rows, masks):
    for _ in range(KSM):
        rows = [v if m is None else v * m for v, m in zip(rows, masks)]
        rows = [
            rows[i] + DIFFUSION * (rows[i - 1] + rows[i + 1] - 2.0 * rows[i])
            for i in range(1, len(rows) - 1)
        ]
        masks = masks[1:-1]
    return [v if m is None else v * m for v, m in zip(rows, masks)]


def row_slice(row):
    return pl.ds(row * MEMBERS_HERE, MEMBERS_HERE)


def is_even():
    return lax.rem(lax.axis_index("tile"), 2) == 0


def sides(a_ref, b_ref, cols, even):
    first = [a_ref[row_slice(r), cols].astype(FLOAT) for r in range(4)]
    second = [b_ref[row_slice(r), cols].astype(FLOAT) for r in range(4)]
    low = [jnp.where(even, v, u) for u, v in zip(first, second)]
    high = [jnp.where(even, u, v) for u, v in zip(first, second)]
    return low, high


def streamed_kernel(
    a_ref, own_ref, b_ref, refine_hbm, perturb_hbm, map_hbm, after_ref,
    mine_ref, other_ref, refine_ref, perturb_ref, map_ref, smooth_ref, sem,
):
    copies = [(pltpu.make_async_copy(refine_hbm, refine_ref, sem.at[0, NY]),)]
    for y in range(NY):
        cols = pl.ds(y * CHUNK, CHUNK)
        copies.append(
            (
                pltpu.make_async_copy(map_hbm.at[:, cols], map_ref.at[:, cols], sem.at[0, y]),
                pltpu.make_async_copy(
                    perturb_hbm.at[:, :, cols], perturb_ref.at[:, :, cols], sem.at[1, y]
                ),
            )
        )
    for group in copies[1:2] + copies[:1] + copies[2:]:
        for copy in group:
            copy.start()

    def arrived(y):
        for copy in copies[y + 1] + (copies[0] if y == 0 else ()):
            copy.wait()

    forward_kernel(
        a_ref, own_ref, b_ref, refine_ref, perturb_ref, map_ref, mine_ref, other_ref, smooth_ref,
        arrived=arrived,
    )


def forward_kernel(
    a_ref, own_ref, b_ref, refine_ref, perturb_ref, map_ref, mine_ref, other_ref, smooth_ref,
    arrived=None,
):
    _, core_pos, _ = place()
    even = is_even()
    below, above = edges()
    masks = [below] * 4 + [None] * 4 + [above] * 4
    for start in range(0, COARSE_COLS, 128):
        cols = pl.ds(start, 128)
        low, high = sides(a_ref, b_ref, cols, even)
        rows = low + [own_ref[row_slice(r), cols] for r in range(4)] + high
        for r, value in enumerate(swept(rows, masks)):
            smooth_ref[row_slice(r), cols] = value.astype(HALF)
    smooth = smooth_ref[...]
    for y in range(NY):
        cols = pl.ds(y * CHUNK, CHUNK)
        if arrived is not None:
            arrived(y)
        mapped = jnp.dot(smooth, map_ref[:, cols], preferred_element_type=FLOAT)
        high = mapped.astype(HALF)
        low = (mapped - high.astype(FLOAT)).astype(HALF)
        fine = jnp.dot(
            refine_ref[...], jnp.concatenate([high, low], axis=0), preferred_element_type=FLOAT
        )
        total = None
        for k in range(MEMBERS_HERE):
            term = fine[k * FINE_ROWS : (k + 1) * FINE_ROWS] * perturb_ref[k, :, cols].astype(FLOAT)
            total = term if total is None else total + term
        first, second = total[:, :WIDTH], total[:, WIDTH:]
        mine_ref[y] = jnp.where(core_pos == 0, first, second)
        other_ref[y] = jnp.where(core_pos == 0, second, first)


REGIONS = ((NY, FINE_ROWS, WIDTH), FLOAT)


SMOOTH = pltpu.VMEM(((ROWS + 2) * MEMBERS_HERE, COARSE_COLS), HALF)


def first_forward(first, own, second, perturb, column_map, after):
    matrix = member_matrix()
    matrix = jnp.asarray(np.concatenate([matrix, matrix], axis=1), HALF)
    operators = (matrix, perturb, column_map)
    return call(
        streamed_kernel,
        (REGIONS, REGIONS) + tuple((x.shape, x.dtype) for x in operators),
        (first, own, second) + operators + (after,),
        far=(3, 4, 5),
        scratch=[SMOOTH, pltpu.SemaphoreType.DMA((2, NY + 1))],
    )


def later_forward(first, own, second, *operators):
    return call(
        forward_kernel, (REGIONS, REGIONS), (first, own, second) + operators, scratch=[SMOOTH]
    )


def adjoint_kernel(
    mine_ref, other_ref, back_ref, perturb_ref, map_ref,
    part_ref, a_ref, b_ref,
):
    _, core_pos, _ = place()
    even = is_even()
    total = None
    for y in range(NY):
        cols = pl.ds(y * CHUNK, CHUNK)
        mine, other = mine_ref[y], other_ref[y]
        first = jnp.where(core_pos == 0, mine, other)
        second = jnp.where(core_pos == 0, other, mine)
        spread = jnp.concatenate([first, second], axis=1)
        highs, lows = [], []
        for k in range(MEMBERS_HERE):
            term = perturb_ref[k, :, cols].astype(FLOAT) * spread
            high = term.astype(HALF)
            highs.append(high)
            lows.append((term - high.astype(FLOAT)).astype(HALF))
        pulled = jnp.dot(
            back_ref[...], jnp.concatenate(highs + lows, axis=0), preferred_element_type=FLOAT
        )
        part = lax.dot_general(
            pulled.astype(HALF),
            map_ref[:, cols],
            (((1,), (1,)), ((), ())),
            preferred_element_type=FLOAT,
        )
        total = part if total is None else total + part
    part_ref[...] = total
    up = total[2 * MEMBERS_HERE :].astype(HALF)
    down = total[: 4 * MEMBERS_HERE].astype(HALF)
    a_ref[...] = jnp.where(even, up, down)
    b_ref[...] = jnp.where(even, down, up)


def partial_adjoint(mine, other, perturb, column_map):
    matrix = member_matrix().T
    matrix = jnp.asarray(np.concatenate([matrix, matrix], axis=1), HALF)
    rim = ((4 * MEMBERS_HERE, COARSE_COLS), HALF)
    return call(
        adjoint_kernel,
        ((((ROWS + 2) * MEMBERS_HERE, COARSE_COLS), FLOAT), rim, rim),
        (mine, other, matrix, perturb, column_map),
    )


def gradient_kernel(a_ref, part_ref, b_ref, own_ref, grad_ref, half_ref, square_ref):
    below, above = edges()
    masks = [below] * 3 + [None] * 4 + [above] * 3
    even = is_even()
    square = None
    for start in range(0, COARSE_COLS, 128):
        cols = pl.ds(start, 128)
        low, high = sides(a_ref, b_ref, cols, even)
        part = [part_ref[row_slice(r), cols] for r in range(6)]
        rows = [low[0], low[1], low[2] + part[0], low[3] * below + part[1], part[2], part[3]]
        rows += [part[4] + high[0] * above, part[5] + high[1], high[2], high[3]]
        for r, value in enumerate(swept(rows, masks)):
            gradient = own_ref[row_slice(r), cols] + value
            grad_ref[row_slice(r), cols] = gradient
            half_ref[row_slice(r), cols] = gradient.astype(HALF)
            term = gradient * gradient
            square = term if square is None else square + term
    square_ref[...] = square[:8] + square[8:]


def gradient_of(low, part, high, own):
    shape = (ROWS * MEMBERS_HERE, COARSE_COLS)
    return call(
        gradient_kernel,
        ((shape, FLOAT), (shape, HALF), ((8, 128), FLOAT)),
        (low, part, high, own),
    )


def send_kernel(value_hbm, error_hbm, gain_ref, sent_ref, value_ref, error_ref, sem):
    copies = [
        pltpu.make_async_copy(value_hbm, value_ref, sem.at[0]),
        pltpu.make_async_copy(error_hbm, error_ref, sem.at[1]),
    ]
    for copy in copies:
        copy.start()
    for copy in copies:
        copy.wait()
    lanes = lax.broadcasted_iota(jnp.int32, (SLOTS, BATCHES), 1)
    block = lanes // (NCORE * NTILE)
    rows = []
    for ref in (value_ref, error_ref):
        values = ref[...]
        turned = [values] + [
            pltpu.roll(values, NCORE * NTILE * i, 1) for i in range(1, NY)
        ]
        for y in range(NY):
            out = turned[0]
            for j in range(NY):
                out = jnp.where(block == j, turned[(j - y) % NY], out)
            rows.append(out)
    gain = jnp.full((2 * NY * SLOTS, BATCHES), gain_ref[0], FLOAT)
    sent_ref[...] = jnp.transpose(jnp.concatenate(rows + [gain], axis=0))


def add_kernel(a_ref, b_ref, base_ref, out_ref):
    _, _, y_pos = place()
    for y in range(NY):
        out_ref[y] = a_ref[y] + b_ref[y]
    out_ref[y_pos] += base_ref[...]


def pick_kernel(a_ref, b_ref, *out_refs):
    _, _, y_pos = place()
    for step, ref in enumerate(out_refs):
        y = lax.rem(y_pos + step, NY)
        ref[...] = a_ref[y] + b_ref[y]


def column_picks(column):
    ids = lax.broadcasted_iota(jnp.int32, (WIDTH, BATCHES), 0)
    return jnp.concatenate(
        [(ids == column[s : s + 1]).astype(FLOAT).astype(HALF) for s in range(SLOTS)], axis=1
    )


def row_factors(row, fraction):
    ids = lax.broadcasted_iota(jnp.int32, (FINE_ROWS, BATCHES), 0)
    return jnp.concatenate(
        [
            jnp.where(ids == row[s : s + 1], 1.0 - fraction[s : s + 1], 0.0)
            + jnp.where(ids == row[s : s + 1] + 1, fraction[s : s + 1], 0.0)
            for s in range(SLOTS)
        ],
        axis=1,
    )


def on_lanes(values):
    return jnp.concatenate([values[s : s + 1] for s in range(SLOTS)], axis=1)


def on_slots(values):
    return jnp.concatenate(
        [values[:, s * BATCHES : (s + 1) * BATCHES] for s in range(SLOTS)], axis=0
    )


def halves(values):
    high = values.astype(HALF)
    return jnp.concatenate([high, (values - high.astype(FLOAT)).astype(HALF)], axis=0)


def interpolated(field, picks, factors, fraction):
    shifted = jnp.concatenate([field[:, 1:], field[:, :1]], axis=1)
    got = jnp.dot(
        halves(jnp.concatenate([field, shifted], axis=0)), picks, preferred_element_type=FLOAT
    )
    got = got[: 2 * FINE_ROWS] + got[2 * FINE_ROWS :]
    left, right = got[:FINE_ROWS], got[FINE_ROWS:]
    mixed = left * (1.0 - fraction) + right * fraction
    return on_slots(jnp.sum(mixed * factors, axis=0, keepdims=True))


def located(index):
    row = index // WIDTH
    return row, index - row * WIDTH


def obs_kernel(
    a_ref, b_ref, c_ref, d_ref, index_ref, row_ref, column_ref, length_ref, data_ref,
    spread_ref, weight_ref, full_ref,
):
    _, core_pos, y_pos = place()
    data = jnp.transpose(data_ref[...])
    gain = data[2 * NY * SLOTS : 2 * NY * SLOTS + SLOTS]
    slots = lax.broadcasted_iota(jnp.int32, (SLOTS, BATCHES), 0)
    for y in range(NY):
        field = a_ref[y] + b_ref[y] + c_ref[y] + d_ref[y]
        group = NCORE * y + core_pos
        row, column = located(index_ref[group])
        picks = column_picks(column)
        factors = row_factors(row, row_ref[group])
        fraction = on_lanes(column_ref[group])
        live = jnp.where(slots < length_ref[pl.ds(group, 1)], 1.0, 0.0)
        state = interpolated(field, picks, factors, fraction)
        value = data[y * SLOTS : (y + 1) * SLOTS]
        error = data[(NY + y) * SLOTS : (NY + y + 1) * SLOTS]
        bounded = jnp.tanh(state)
        derivative = 1.0 + gain * (1.0 - bounded * bounded)
        misfit = state + gain * bounded - value
        precision = live / (error * error)
        residual = derivative * misfit * precision

        @pl.when(y == y_pos)
        def _():
            weight_ref[...] = derivative * derivative * precision
            full_ref[...] = field

        weighted = factors * on_lanes(residual)
        both = jnp.concatenate([weighted * (1.0 - fraction), weighted * fraction], axis=0)
        got = lax.dot_general(
            halves(both), picks, (((1,), (1,)), ((), ())), preferred_element_type=FLOAT
        )
        got = got[: 2 * FINE_ROWS] + got[2 * FINE_ROWS :]
        left, right = got[:FINE_ROWS], got[FINE_ROWS:]
        spread_ref[y] = left + jnp.concatenate([right[:, -1:], right[:, :-1]], axis=1)


def curve_kernel(
    a_ref, b_ref, c_ref, d_ref, index_ref, row_ref, column_ref, weight_ref, square_ref,
    field_ref, sent_ref,
):
    _, core_pos, y_pos = place()
    own = NCORE * y_pos + core_pos
    field = a_ref[...] + b_ref[...] + c_ref[...] + d_ref[...]
    field_ref[...] = field
    row, column = located(index_ref[own])
    observed = interpolated(
        field, column_picks(column), row_factors(row, row_ref[own]), on_lanes(column_ref[own])
    )
    curvature = jnp.sum(weight_ref[...] * observed * observed, keepdims=True)
    square = jnp.sum(square_ref[...], keepdims=True)
    lanes = lax.broadcasted_iota(jnp.int32, (BATCHES, 128), 1)
    sent_ref[...] = jnp.where(lanes < 64, square, curvature)


def step_kernel(
    shared_ref, own_ref, grad_ref, full_ref, base_ref, image_ref, coarse_ref, increment_ref
):
    totals = jnp.sum(shared_ref[...], axis=0, keepdims=True)
    lanes = lax.broadcasted_iota(jnp.int32, (1, 128), 1)
    square = jnp.sum(jnp.where(lanes == 0, totals, 0.0), keepdims=True)
    curvature = jnp.sum(jnp.where(lanes == 127, totals, 0.0), keepdims=True)
    step = square / (square + curvature)
    for r in range(ROWS):
        coarse_ref[:, r, :] = own_ref[row_slice(r)] - step * grad_ref[row_slice(r)]
    increment_ref[...] = full_ref[...] - base_ref[...] - step * image_ref[...]


def shards(
    perturb,
    weights,
    column_map,
    background,
    stencil_index,
    row_fraction,
    column_fraction,
    block_lengths,
    obs_value,
    obs_error,
    instrument_gain,
):
    flat = (ROWS * MEMBERS_HERE, COARSE_COLS)
    own = jnp.transpose(weights, (1, 0, 2)).reshape(flat)
    half = own.astype(HALF)
    near_rows, far_rows = swap_both(half, half)

    (sent,) = call(
        send_kernel,
        (((BATCHES, BATCHES), FLOAT),),
        (obs_value[0].T, obs_error[0].T, instrument_gain),
        far=(0, 1),
        scalar=(2,),
        scratch=[pltpu.VMEM((SLOTS, BATCHES), FLOAT)] * 2 + [pltpu.SemaphoreType.DMA((2,))],
    )
    data = lax.all_to_all(sent, ("member", "tile"), split_axis=0, concat_axis=0, tiled=True)

    index = jnp.transpose(stencil_index[0], (1, 2, 0))
    row_frac = jnp.transpose(row_fraction[0], (1, 2, 0))
    column_frac = jnp.transpose(column_fraction[0], (1, 2, 0))
    lengths = block_lengths[0].T

    mine, other, matrix, perturb, column_map = first_forward(
        near_rows, own, far_rows, perturb, column_map, data
    )
    (mine,) = call(add_kernel, (REGIONS,), (mine, swap_core(other), background))
    pieces = [mine] + [turn(mine, NCORE * i, "member") for i in range(1, NY)]
    region = ((FINE_ROWS, WIDTH), FLOAT)
    spread, weight, full = call(
        obs_kernel,
        (REGIONS, ((SLOTS, BATCHES), FLOAT), region),
        (*pieces, index, row_frac, column_frac, lengths, data),
    )
    part, up, down = partial_adjoint(spread, swap_core(spread), perturb, column_map)
    near_rows, far_rows = swap_both(up, down)
    gradient, half, square = gradient_of(near_rows, part, far_rows, own)
    near_rows, far_rows = swap_both(half, half)
    mine, other = later_forward(near_rows, gradient, far_rows, matrix, perturb, column_map)
    pieces = call(pick_kernel, (region,) * NY, (mine, swap_core(other)))
    pieces = [pieces[0]] + [turn(pieces[i], NCORE * i, "member") for i in range(1, NY)]
    image, sent = call(
        curve_kernel,
        (region, ((BATCHES, 128), FLOAT)),
        (*pieces, index, row_frac, column_frac, weight, square),
    )
    shared = lax.all_to_all(sent, ("member", "tile"), split_axis=0, concat_axis=0, tiled=True)
    return call(
        step_kernel,
        (((MEMBERS_HERE, ROWS, COARSE_COLS), FLOAT), region),
        (shared, own, gradient, full, background, image),
        far_out=(0, 1),
    )


def solution(mesh):
    placed = (
        P("member", "tile", None),
        P("member", "tile", None),
        P(),
        P("tile", "member"),
        P("tile", None, None, None),
        P("tile", None, None, None),
        P("tile", None, None, None),
        P("tile", None, None),
        P(("member", "tile"), None, None),
        P(("member", "tile"), None, None),
        P(("member", "tile")),
    )
    return jax.shard_map(
        shards,
        mesh=mesh,
        in_specs=placed,
        out_specs=(P("member", "tile", None), P("tile", "member")),
        check_vma=False,
    )
```

```python
import jax
import jax.numpy as jnp
import numpy as np
from jax import lax
from jax.experimental import pallas as pl
from jax.experimental.pallas import tpu as pltpu
from jax.sharding import PartitionSpec as P

RATIO = 4
KSM = 3
DIFFUSION = 0.45
NTILE = 16
NMEMBER = 8
NCORE = 2
NY = NMEMBER // NCORE
MEMBERS_HERE = 16
ROWS = 4
FINE_ROWS = 16
COARSE_COLS = 1280
WIDTH = 320
CHUNK = NCORE * WIDTH
SLOTS = 8
BATCHES = 128
ROOM = 12 << 20
EVEN, ODD = pl.ds(0, NTILE, stride=2), pl.ds(1, NTILE, stride=2)
FLOAT, HALF = jnp.float32, jnp.bfloat16


def refine_matrix():
    table = np.zeros((FINE_ROWS, ROWS + 2))
    for row in range(ROWS):
        for offset in range(RATIO):
            shift = (offset + 0.5) / RATIO - 0.5
            fine = RATIO * row + offset
            if shift < 0:
                table[fine, row + 1] += 1.0 + shift
                table[fine, row] -= shift
            else:
                table[fine, row + 1] += 1.0 - shift
                table[fine, row + 2] += shift
    return table


def member_matrix():
    return np.einsum("fr,kl->kfrl", refine_matrix(), np.eye(MEMBERS_HERE)).reshape(
        MEMBERS_HERE * FINE_ROWS, (ROWS + 2) * MEMBERS_HERE
    )


def turn(values, step, axis):
    count = lax.axis_size(axis)
    return lax.ppermute(values, axis, [(i, (i + step) % count) for i in range(count)])


def swap_near(values):
    return lax.ppermute(values, "tile", [(i, i ^ 1) for i in range(NTILE)])


def swap_far(values):
    pairs = [(0, 0), (NTILE - 1, NTILE - 1)]
    for i in range(1, NTILE - 1, 2):
        pairs += [(i, i + 1), (i + 1, i)]
    return lax.ppermute(values, "tile", pairs)


def swap_both(near_values, far_values):
    near_rows = swap_near(near_values)
    far_rows = swap_far(far_values)
    return near_rows, far_rows


def swap_core(values):
    return lax.ppermute(values, "member", [(i, i ^ 1) for i in range(NMEMBER)])


NEAR = pl.BlockSpec(memory_space=pltpu.VMEM)
FAR = pl.BlockSpec(memory_space=pltpu.HBM)
SCALAR = pl.BlockSpec(memory_space=pltpu.SMEM)


def near(values):
    return pltpu.with_memory_space_constraint(values, pltpu.VMEM)


def distant(values):
    return pltpu.with_memory_space_constraint(values, pltpu.HBM)


def call(kernel, out_shapes, arguments, far=(), scratch=(), far_out=(), scalar=()):
    specs = [
        SCALAR if i in scalar else FAR if i in far else NEAR for i in range(len(arguments))
    ]
    arguments = tuple(
        x if i in scalar else distant(x) if i in far else near(x)
        for i, x in enumerate(arguments)
    )
    return pl.pallas_call(
        kernel,
        out_shape=tuple(
            jax.ShapeDtypeStruct(shape, kind) if i in far_out else pltpu.VMEM(shape, kind)
            for i, (shape, kind) in enumerate(out_shapes)
        ),
        in_specs=specs,
        out_specs=tuple(NEAR for _ in out_shapes),
        scratch_shapes=list(scratch),
        compiler_params=pltpu.CompilerParams(vmem_limit_bytes=ROOM),
        cost_estimate=pl.CostEstimate(flops=10**9, transcendentals=0, bytes_accessed=8 << 20),
    )(*arguments)


def place():
    member_pos = lax.axis_index("member")
    return lax.axis_index("tile"), lax.rem(member_pos, NCORE), lax.div(member_pos, NCORE)


def edges():
    tile_pos = lax.axis_index("tile")
    return jnp.where(tile_pos > 0, 1.0, 0.0), jnp.where(tile_pos < NTILE - 1, 1.0, 0.0)


def swept(rows, masks):
    for _ in range(KSM):
        rows = [v if m is None else v * m for v, m in zip(rows, masks)]
        rows = [
            rows[i] + DIFFUSION * (rows[i - 1] + rows[i + 1] - 2.0 * rows[i])
            for i in range(1, len(rows) - 1)
        ]
        masks = masks[1:-1]
    return [v if m is None else v * m for v, m in zip(rows, masks)]


def row_slice(row):
    return pl.ds(row * MEMBERS_HERE, MEMBERS_HERE)


def is_even():
    return lax.rem(lax.axis_index("tile"), 2) == 0


def sides(a_ref, b_ref, cols, even):
    first = [a_ref[row_slice(r), cols].astype(FLOAT) for r in range(4)]
    second = [b_ref[row_slice(r), cols].astype(FLOAT) for r in range(4)]
    low = [jnp.where(even, v, u) for u, v in zip(first, second)]
    high = [jnp.where(even, u, v) for u, v in zip(first, second)]
    return low, high


def streamed_kernel(
    a_ref, own_ref, b_ref, refine_hbm, perturb_hbm, map_hbm, data_ref,
    mine_ref, other_ref, refine_ref, perturb_ref, map_ref, smooth_ref, sem,
):
    copies = [(pltpu.make_async_copy(refine_hbm, refine_ref, sem.at[0, NY]),)]
    for y in range(NY):
        cols = pl.ds(y * CHUNK, CHUNK)
        copies.append(
            (
                pltpu.make_async_copy(map_hbm.at[:, cols], map_ref.at[:, cols], sem.at[0, y]),
                pltpu.make_async_copy(
                    perturb_hbm.at[:, :, cols], perturb_ref.at[:, :, cols], sem.at[1, y]
                ),
            )
        )
    for group in copies[1:2] + copies[:1] + copies[2:]:
        for copy in group:
            copy.start()

    _, core_pos, _ = place()
    data, gain = data_ref[EVEN], data_ref[ODD]
    lanes = lax.broadcasted_iota(jnp.int32, data.shape, 1)
    home = RIDE + 2 * NTILE * core_pos
    for y in range(NY):
        for ref, parity in ((mine_ref, core_pos), (other_ref, 1 - core_pos)):
            shift = lax.rem(home + BATCHES - NTILE * (NCORE * y + parity), BATCHES)
            moved = jnp.where(lanes == home + 2 * SLOTS, gain, pltpu.roll(data, shift, 1))
            kept = (lanes >= home) & (lanes <= home + 2 * SLOTS)
            ref[y, :, 256:] = jnp.where(kept, moved, 0.0)

    def arrived(y):
        for copy in copies[y + 1] + (copies[0] if y == 0 else ()):
            copy.wait()

    forward_kernel(
        a_ref, own_ref, b_ref, refine_ref, perturb_ref, map_ref, mine_ref, other_ref, smooth_ref,
        arrived=arrived,
    )


def forward_kernel(
    a_ref, own_ref, b_ref, refine_ref, perturb_ref, map_ref, mine_ref, other_ref, smooth_ref,
    arrived=None,
):
    _, core_pos, _ = place()
    even = is_even()
    below, above = edges()
    masks = [below] * 4 + [None] * 4 + [above] * 4
    for start in range(0, COARSE_COLS, 128):
        cols = pl.ds(start, 128)
        low, high = sides(a_ref, b_ref, cols, even)
        rows = low + [own_ref[row_slice(r), cols] for r in range(4)] + high
        for r, value in enumerate(swept(rows, masks)):
            smooth_ref[row_slice(r), cols] = value.astype(HALF)
    smooth = smooth_ref[...]
    for y in range(NY):
        cols = pl.ds(y * CHUNK, CHUNK)
        if arrived is not None:
            arrived(y)
        mapped = jnp.dot(smooth, map_ref[:, cols], preferred_element_type=FLOAT)
        high = mapped.astype(HALF)
        low = (mapped - high.astype(FLOAT)).astype(HALF)
        fine = jnp.dot(
            refine_ref[...], jnp.concatenate([high, low], axis=0), preferred_element_type=FLOAT
        )
        total = None
        for k in range(MEMBERS_HERE):
            term = fine[k * FINE_ROWS : (k + 1) * FINE_ROWS] * perturb_ref[k, :, cols].astype(FLOAT)
            total = term if total is None else total + term
        first, second = total[:, :WIDTH], total[:, WIDTH:]
        mine_ref[y, :, :WIDTH] = jnp.where(core_pos == 0, first, second)
        other_ref[y, :, :WIDTH] = jnp.where(core_pos == 0, second, first)


REGIONS = ((NY, FINE_ROWS, WIDTH), FLOAT)
LADEN = ((NY, FINE_ROWS, 384), FLOAT)
RIDE = 64


SMOOTH = pltpu.VMEM(((ROWS + 2) * MEMBERS_HERE, COARSE_COLS), HALF)


def first_forward(first, own, second, perturb, column_map, data):
    matrix = member_matrix()
    matrix = jnp.asarray(np.concatenate([matrix, matrix], axis=1), HALF)
    operators = (matrix, perturb, column_map)
    return call(
        streamed_kernel,
        (LADEN, LADEN) + tuple((x.shape, x.dtype) for x in operators),
        (first, own, second) + operators + (data,),
        far=(3, 4, 5),
        scratch=[SMOOTH, pltpu.SemaphoreType.DMA((2, NY + 1))],
    )


def later_forward(first, own, second, *operators):
    return call(
        forward_kernel, (REGIONS, REGIONS), (first, own, second) + operators, scratch=[SMOOTH]
    )


def adjoint_kernel(
    mine_ref, other_ref, back_ref, perturb_ref, map_ref,
    part_ref, a_ref, b_ref,
):
    _, core_pos, _ = place()
    even = is_even()
    total = None
    for y in range(NY):
        cols = pl.ds(y * CHUNK, CHUNK)
        mine, other = mine_ref[y], other_ref[y]
        first = jnp.where(core_pos == 0, mine, other)
        second = jnp.where(core_pos == 0, other, mine)
        spread = jnp.concatenate([first, second], axis=1)
        highs, lows = [], []
        for k in range(MEMBERS_HERE):
            term = perturb_ref[k, :, cols].astype(FLOAT) * spread
            high = term.astype(HALF)
            highs.append(high)
            lows.append((term - high.astype(FLOAT)).astype(HALF))
        pulled = jnp.dot(
            back_ref[...], jnp.concatenate(highs + lows, axis=0), preferred_element_type=FLOAT
        )
        part = lax.dot_general(
            pulled.astype(HALF),
            map_ref[:, cols],
            (((1,), (1,)), ((), ())),
            preferred_element_type=FLOAT,
        )
        total = part if total is None else total + part
    part_ref[...] = total
    up = total[2 * MEMBERS_HERE :].astype(HALF)
    down = total[: 4 * MEMBERS_HERE].astype(HALF)
    a_ref[...] = jnp.where(even, up, down)
    b_ref[...] = jnp.where(even, down, up)


def partial_adjoint(mine, other, perturb, column_map):
    matrix = member_matrix().T
    matrix = jnp.asarray(np.concatenate([matrix, matrix], axis=1), HALF)
    rim = ((4 * MEMBERS_HERE, COARSE_COLS), HALF)
    return call(
        adjoint_kernel,
        ((((ROWS + 2) * MEMBERS_HERE, COARSE_COLS), FLOAT), rim, rim),
        (mine, other, matrix, perturb, column_map),
    )


def gradient_kernel(a_ref, part_ref, b_ref, own_ref, grad_ref, half_ref, square_ref):
    below, above = edges()
    masks = [below] * 3 + [None] * 4 + [above] * 3
    even = is_even()
    square = None
    for start in range(0, COARSE_COLS, 128):
        cols = pl.ds(start, 128)
        low, high = sides(a_ref, b_ref, cols, even)
        part = [part_ref[row_slice(r), cols] for r in range(6)]
        rows = [low[0], low[1], low[2] + part[0], low[3] * below + part[1], part[2], part[3]]
        rows += [part[4] + high[0] * above, part[5] + high[1], high[2], high[3]]
        for r, value in enumerate(swept(rows, masks)):
            gradient = own_ref[row_slice(r), cols] + value
            grad_ref[row_slice(r), cols] = gradient
            half_ref[row_slice(r), cols] = gradient.astype(HALF)
            term = gradient * gradient
            square = term if square is None else square + term
    square_ref[...] = square[:8] + square[8:]


def gradient_of(low, part, high, own):
    shape = (ROWS * MEMBERS_HERE, COARSE_COLS)
    return call(
        gradient_kernel,
        ((shape, FLOAT), (shape, HALF), ((8, 128), FLOAT)),
        (low, part, high, own),
    )


def send_kernel(value_hbm, error_hbm, gain_ref, sent_ref, value_ref, error_ref, sem):
    copies = [
        pltpu.make_async_copy(value_hbm, value_ref, sem.at[0]),
        pltpu.make_async_copy(error_hbm, error_ref, sem.at[1]),
    ]
    for copy in copies:
        copy.start()
    for copy in copies:
        copy.wait()
    rows = []
    for group in range(NMEMBER):
        for ref in (value_ref, error_ref):
            rows.append(pltpu.roll(ref[...], (BATCHES - NTILE * group) % BATCHES, 1))
    sent_ref[EVEN] = jnp.transpose(jnp.concatenate(rows, axis=0))[:NTILE]
    sent_ref[ODD] = jnp.full((NTILE, 128), gain_ref[0], FLOAT)


def add_kernel(a_ref, b_ref, base_ref, out_ref):
    _, _, y_pos = place()
    for y in range(NY):
        out_ref[y] = a_ref[y] + b_ref[y]
    out_ref[y_pos, :, :WIDTH] += base_ref[...]


def pick_kernel(a_ref, b_ref, *out_refs):
    _, _, y_pos = place()
    for step, ref in enumerate(out_refs):
        y = lax.rem(y_pos + step, NY)
        ref[...] = a_ref[y] + b_ref[y]


def column_picks(column):
    ids = lax.broadcasted_iota(jnp.int32, (WIDTH, BATCHES), 0)
    return jnp.concatenate(
        [(ids == column[s : s + 1]).astype(FLOAT).astype(HALF) for s in range(SLOTS)], axis=1
    )


def row_factors(row, fraction):
    ids = lax.broadcasted_iota(jnp.int32, (FINE_ROWS, BATCHES), 0)
    return jnp.concatenate(
        [
            jnp.where(ids == row[s : s + 1], 1.0 - fraction[s : s + 1], 0.0)
            + jnp.where(ids == row[s : s + 1] + 1, fraction[s : s + 1], 0.0)
            for s in range(SLOTS)
        ],
        axis=1,
    )


def on_lanes(values):
    return jnp.concatenate([values[s : s + 1] for s in range(SLOTS)], axis=1)


def on_slots(values):
    return jnp.concatenate(
        [values[:, s * BATCHES : (s + 1) * BATCHES] for s in range(SLOTS)], axis=0
    )


def halves(values):
    high = values.astype(HALF)
    return jnp.concatenate([high, (values - high.astype(FLOAT)).astype(HALF)], axis=0)


def interpolated(field, picks, factors, fraction):
    shifted = jnp.concatenate([field[:, 1:], field[:, :1]], axis=1)
    got = jnp.dot(
        halves(jnp.concatenate([field, shifted], axis=0)), picks, preferred_element_type=FLOAT
    )
    got = got[: 2 * FINE_ROWS] + got[2 * FINE_ROWS :]
    left, right = got[:FINE_ROWS], got[FINE_ROWS:]
    mixed = left * (1.0 - fraction) + right * fraction
    return on_slots(jnp.sum(mixed * factors, axis=0, keepdims=True))


def located(index):
    row = index // WIDTH
    return row, index - row * WIDTH


def obs_kernel(
    a_ref, b_ref, c_ref, d_ref, index_ref, row_ref, column_ref, length_ref,
    spread_ref, weight_ref, full_ref, data_ref,
):
    _, core_pos, y_pos = place()
    slots = lax.broadcasted_iota(jnp.int32, (SLOTS, BATCHES), 0)
    for y in range(NY):
        field = sum(ref[y, :, :WIDTH] for ref in (b_ref, c_ref, d_ref)) + a_ref[y, :, :WIDTH]
        for step, ref in enumerate((a_ref, b_ref, c_ref, d_ref)):
            source = lax.rem(y_pos + NY - step, NY) * (NCORE * NTILE)
            load = ref[y, :, 256:]
            for core in range(NCORE):
                start = pl.multiple_of(source + core * NTILE, NTILE)
                data_ref[y, pl.ds(start, NTILE)] = pltpu.roll(
                    load, (BATCHES - RIDE - 2 * NTILE * core) % BATCHES, 1
                )
        data = jnp.transpose(data_ref[y])
        value, error = data[:SLOTS], data[SLOTS : 2 * SLOTS]
        gain = data[2 * SLOTS : 2 * SLOTS + 1]
        group = NCORE * y + core_pos
        row, column = located(index_ref[group])
        picks = column_picks(column)
        factors = row_factors(row, row_ref[group])
        fraction = on_lanes(column_ref[group])
        live = jnp.where(slots < length_ref[pl.ds(group, 1)], 1.0, 0.0)
        state = interpolated(field, picks, factors, fraction)
        bounded = jnp.tanh(state)
        derivative = 1.0 + gain * (1.0 - bounded * bounded)
        misfit = state + gain * bounded - value
        precision = live / (error * error)
        residual = derivative * misfit * precision

        @pl.when(y == y_pos)
        def _():
            weight_ref[...] = derivative * derivative * precision
            full_ref[...] = field

        weighted = factors * on_lanes(residual)
        both = jnp.concatenate([weighted * (1.0 - fraction), weighted * fraction], axis=0)
        got = lax.dot_general(
            halves(both), picks, (((1,), (1,)), ((), ())), preferred_element_type=FLOAT
        )
        got = got[: 2 * FINE_ROWS] + got[2 * FINE_ROWS :]
        left, right = got[:FINE_ROWS], got[FINE_ROWS:]
        spread_ref[y] = left + jnp.concatenate([right[:, -1:], right[:, :-1]], axis=1)


def curve_kernel(
    a_ref, b_ref, c_ref, d_ref, index_ref, row_ref, column_ref, weight_ref, square_ref,
    field_ref, sent_ref,
):
    _, core_pos, y_pos = place()
    own = NCORE * y_pos + core_pos
    field = a_ref[...] + b_ref[...] + c_ref[...] + d_ref[...]
    field_ref[...] = field
    row, column = located(index_ref[own])
    observed = interpolated(
        field, column_picks(column), row_factors(row, row_ref[own]), on_lanes(column_ref[own])
    )
    curvature = jnp.sum(weight_ref[...] * observed * observed, keepdims=True)
    square = jnp.sum(square_ref[...], keepdims=True)
    lanes = lax.broadcasted_iota(jnp.int32, (BATCHES, 128), 1)
    sent_ref[...] = jnp.where(lanes < 64, square, curvature)


def step_kernel(
    shared_ref, own_ref, grad_ref, full_ref, base_ref, image_ref, coarse_ref, increment_ref
):
    totals = jnp.sum(shared_ref[...], axis=0, keepdims=True)
    lanes = lax.broadcasted_iota(jnp.int32, (1, 128), 1)
    square = jnp.sum(jnp.where(lanes == 0, totals, 0.0), keepdims=True)
    curvature = jnp.sum(jnp.where(lanes == 127, totals, 0.0), keepdims=True)
    step = square / (square + curvature)
    for r in range(ROWS):
        coarse_ref[:, r, :] = own_ref[row_slice(r)] - step * grad_ref[row_slice(r)]
    increment_ref[...] = full_ref[...] - base_ref[...] - step * image_ref[...]


def shards(
    perturb,
    weights,
    column_map,
    background,
    stencil_index,
    row_fraction,
    column_fraction,
    block_lengths,
    obs_value,
    obs_error,
    instrument_gain,
):
    flat = (ROWS * MEMBERS_HERE, COARSE_COLS)
    own = jnp.transpose(weights, (1, 0, 2)).reshape(flat)
    half = own.astype(HALF)
    near_rows, far_rows = swap_both(half, half)

    (sent,) = call(
        send_kernel,
        (((2 * NTILE, 128), FLOAT),),
        (obs_value[0].T, obs_error[0].T, instrument_gain),
        far=(0, 1),
        scalar=(2,),
        scratch=[pltpu.VMEM((SLOTS, BATCHES), FLOAT)] * 2 + [pltpu.SemaphoreType.DMA((2,))],
    )
    data = lax.all_to_all(sent, "tile", split_axis=0, concat_axis=0, tiled=True)

    index = jnp.transpose(stencil_index[0], (1, 2, 0))
    row_frac = jnp.transpose(row_fraction[0], (1, 2, 0))
    column_frac = jnp.transpose(column_fraction[0], (1, 2, 0))
    lengths = block_lengths[0].T

    mine, other, matrix, perturb, column_map = first_forward(
        near_rows, own, far_rows, perturb, column_map, data
    )
    (mine,) = call(add_kernel, (LADEN,), (mine, swap_core(other), background))
    pieces = [mine] + [turn(mine, NCORE * i, "member") for i in range(1, NY)]
    region = ((FINE_ROWS, WIDTH), FLOAT)
    spread, weight, full = call(
        obs_kernel,
        (REGIONS, ((SLOTS, BATCHES), FLOAT), region),
        (*pieces, index, row_frac, column_frac, lengths),
        scratch=[pltpu.VMEM((NY, BATCHES, 128), FLOAT)],
    )
    part, up, down = partial_adjoint(spread, swap_core(spread), perturb, column_map)
    near_rows, far_rows = swap_both(up, down)
    gradient, half, square = gradient_of(near_rows, part, far_rows, own)
    near_rows, far_rows = swap_both(half, half)
    mine, other = later_forward(near_rows, gradient, far_rows, matrix, perturb, column_map)
    pieces = call(pick_kernel, (region,) * NY, (mine, swap_core(other)))
    pieces = [pieces[0]] + [turn(pieces[i], NCORE * i, "member") for i in range(1, NY)]
    image, sent = call(
        curve_kernel,
        (region, ((BATCHES, 128), FLOAT)),
        (*pieces, index, row_frac, column_frac, weight, square),
    )
    shared = lax.all_to_all(sent, ("member", "tile"), split_axis=0, concat_axis=0, tiled=True)
    return call(
        step_kernel,
        (((MEMBERS_HERE, ROWS, COARSE_COLS), FLOAT), region),
        (shared, own, gradient, full, background, image),
        far_out=(0, 1),
    )


def solution(mesh):
    placed = (
        P("member", "tile", None),
        P("member", "tile", None),
        P(),
        P("tile", "member"),
        P("tile", None, None, None),
        P("tile", None, None, None),
        P("tile", None, None, None),
        P("tile", None, None),
        P(("member", "tile"), None, None),
        P(("member", "tile"), None, None),
        P(("member", "tile")),
    )
    return jax.shard_map(
        shards,
        mesh=mesh,
        in_specs=placed,
        out_specs=(P("member", "tile", None), P("tile", "member")),
        check_vma=False,
    )
```

```python
import jax
import jax.numpy as jnp
import numpy as np
from jax import lax
from jax.experimental import pallas as pl
from jax.experimental.pallas import tpu as pltpu
from jax.sharding import PartitionSpec as P

RATIO = 4
KSM = 3
DIFFUSION = 0.45
NTILE = 16
NMEMBER = 8
NCORE = 2
NY = NMEMBER // NCORE
MEMBERS_HERE = 16
ROWS = 4
FINE_ROWS = 16
COARSE_COLS = 1280
WIDTH = 320
CHUNK = NCORE * WIDTH
SLOTS = 8
BATCHES = 128
ROOM = 12 << 20
WORK = 2 * 10**10
EVEN, ODD = pl.ds(0, NTILE, stride=2), pl.ds(1, NTILE, stride=2)
FLOAT, HALF = jnp.float32, jnp.bfloat16


def refine_matrix():
    table = np.zeros((FINE_ROWS, ROWS + 2))
    for row in range(ROWS):
        for offset in range(RATIO):
            shift = (offset + 0.5) / RATIO - 0.5
            fine = RATIO * row + offset
            if shift < 0:
                table[fine, row + 1] += 1.0 + shift
                table[fine, row] -= shift
            else:
                table[fine, row + 1] += 1.0 - shift
                table[fine, row + 2] += shift
    return table


def member_matrix():
    return np.einsum("fr,kl->kfrl", refine_matrix(), np.eye(MEMBERS_HERE)).reshape(
        MEMBERS_HERE * FINE_ROWS, (ROWS + 2) * MEMBERS_HERE
    )


def turn(values, step, axis):
    count = lax.axis_size(axis)
    return lax.ppermute(values, axis, [(i, (i + step) % count) for i in range(count)])


def swap_near(values):
    return lax.ppermute(values, "tile", [(i, i ^ 1) for i in range(NTILE)])


def swap_far(values):
    pairs = [(0, 0), (NTILE - 1, NTILE - 1)]
    for i in range(1, NTILE - 1, 2):
        pairs += [(i, i + 1), (i + 1, i)]
    return lax.ppermute(values, "tile", pairs)


def swap_both(near_values, far_values):
    near_rows = swap_near(near_values)
    far_rows = swap_far(far_values)
    return near_rows, far_rows


def swap_core(values):
    return lax.ppermute(values, "member", [(i, i ^ 1) for i in range(NMEMBER)])


NEAR = pl.BlockSpec(memory_space=pltpu.VMEM)
FAR = pl.BlockSpec(memory_space=pltpu.HBM)
SCALAR = pl.BlockSpec(memory_space=pltpu.SMEM)


def near(values):
    return pltpu.with_memory_space_constraint(values, pltpu.VMEM)


def distant(values):
    return pltpu.with_memory_space_constraint(values, pltpu.HBM)


def call(kernel, out_shapes, arguments, far=(), scratch=(), far_out=(), scalar=(), work=10**9):
    specs = [
        SCALAR if i in scalar else FAR if i in far else NEAR for i in range(len(arguments))
    ]
    arguments = tuple(
        x if i in scalar else distant(x) if i in far else near(x)
        for i, x in enumerate(arguments)
    )
    return pl.pallas_call(
        kernel,
        out_shape=tuple(
            jax.ShapeDtypeStruct(shape, kind) if i in far_out else pltpu.VMEM(shape, kind)
            for i, (shape, kind) in enumerate(out_shapes)
        ),
        in_specs=specs,
        out_specs=tuple(NEAR for _ in out_shapes),
        scratch_shapes=list(scratch),
        compiler_params=pltpu.CompilerParams(vmem_limit_bytes=ROOM),
        cost_estimate=pl.CostEstimate(flops=work, transcendentals=0, bytes_accessed=work >> 7),
    )(*arguments)


def place():
    member_pos = lax.axis_index("member")
    return lax.axis_index("tile"), lax.rem(member_pos, NCORE), lax.div(member_pos, NCORE)


def edges():
    tile_pos = lax.axis_index("tile")
    return jnp.where(tile_pos > 0, 1.0, 0.0), jnp.where(tile_pos < NTILE - 1, 1.0, 0.0)


def swept(rows, masks):
    for _ in range(KSM):
        rows = [v if m is None else v * m for v, m in zip(rows, masks)]
        rows = [
            rows[i] + DIFFUSION * (rows[i - 1] + rows[i + 1] - 2.0 * rows[i])
            for i in range(1, len(rows) - 1)
        ]
        masks = masks[1:-1]
    return [v if m is None else v * m for v, m in zip(rows, masks)]


def row_slice(row):
    return pl.ds(row * MEMBERS_HERE, MEMBERS_HERE)


def is_even():
    return lax.rem(lax.axis_index("tile"), 2) == 0


def sides(a_ref, b_ref, cols, even):
    first = [a_ref[row_slice(r), cols].astype(FLOAT) for r in range(4)]
    second = [b_ref[row_slice(r), cols].astype(FLOAT) for r in range(4)]
    low = [jnp.where(even, v, u) for u, v in zip(first, second)]
    high = [jnp.where(even, u, v) for u, v in zip(first, second)]
    return low, high


def laden_kernel(
    a_ref, own_ref, b_ref, refine_ref, perturb_ref, map_ref, data_ref, mine_ref, other_ref, smooth_ref
):
    _, core_pos, _ = place()
    data, gain = data_ref[EVEN], data_ref[ODD]
    lanes = lax.broadcasted_iota(jnp.int32, data.shape, 1)
    home = RIDE + 2 * NTILE * core_pos
    for y in range(NY):
        for ref, parity in ((mine_ref, core_pos), (other_ref, 1 - core_pos)):
            shift = lax.rem(home + BATCHES - NTILE * (NCORE * y + parity), BATCHES)
            moved = jnp.where(lanes == home + 2 * SLOTS, gain, pltpu.roll(data, shift, 1))
            kept = (lanes >= home) & (lanes <= home + 2 * SLOTS)
            ref[y, :, 256:] = jnp.where(kept, moved, 0.0)
    forward_kernel(
        a_ref, own_ref, b_ref, refine_ref, perturb_ref, map_ref, mine_ref, other_ref, smooth_ref
    )


def forward_kernel(
    a_ref, own_ref, b_ref, refine_ref, perturb_ref, map_ref, mine_ref, other_ref, smooth_ref
):
    _, core_pos, _ = place()
    even = is_even()
    below, above = edges()
    masks = [below] * 4 + [None] * 4 + [above] * 4
    for start in range(0, COARSE_COLS, 128):
        cols = pl.ds(start, 128)
        low, high = sides(a_ref, b_ref, cols, even)
        rows = low + [own_ref[row_slice(r), cols] for r in range(4)] + high
        for r, value in enumerate(swept(rows, masks)):
            smooth_ref[row_slice(r), cols] = value.astype(HALF)
    smooth = smooth_ref[...]
    for y in range(NY):
        cols = pl.ds(y * CHUNK, CHUNK)
        mapped = jnp.dot(smooth, map_ref[:, cols], preferred_element_type=FLOAT)
        high = mapped.astype(HALF)
        low = (mapped - high.astype(FLOAT)).astype(HALF)
        fine = jnp.dot(
            refine_ref[...], jnp.concatenate([high, low], axis=0), preferred_element_type=FLOAT
        )
        total = None
        for k in range(MEMBERS_HERE):
            term = fine[k * FINE_ROWS : (k + 1) * FINE_ROWS] * perturb_ref[k, :, cols].astype(FLOAT)
            total = term if total is None else total + term
        first, second = total[:, :WIDTH], total[:, WIDTH:]
        mine_ref[y, :, :WIDTH] = jnp.where(core_pos == 0, first, second)
        other_ref[y, :, :WIDTH] = jnp.where(core_pos == 0, second, first)


REGIONS = ((NY, FINE_ROWS, WIDTH), FLOAT)
LADEN = ((NY, FINE_ROWS, 384), FLOAT)
RIDE = 64


SMOOTH = pltpu.VMEM(((ROWS + 2) * MEMBERS_HERE, COARSE_COLS), HALF)


def partial_forward(kernel, shape, *arguments):
    return call(kernel, (shape, shape), arguments, scratch=[SMOOTH])


def adjoint_kernel(
    mine_ref, other_ref, back_ref, perturb_ref, map_ref,
    part_ref, a_ref, b_ref,
):
    _, core_pos, _ = place()
    even = is_even()
    total = None
    for y in range(NY):
        cols = pl.ds(y * CHUNK, CHUNK)
        mine, other = mine_ref[y], other_ref[y]
        first = jnp.where(core_pos == 0, mine, other)
        second = jnp.where(core_pos == 0, other, mine)
        spread = jnp.concatenate([first, second], axis=1)
        highs, lows = [], []
        for k in range(MEMBERS_HERE):
            term = perturb_ref[k, :, cols].astype(FLOAT) * spread
            high = term.astype(HALF)
            highs.append(high)
            lows.append((term - high.astype(FLOAT)).astype(HALF))
        pulled = jnp.dot(
            back_ref[...], jnp.concatenate(highs + lows, axis=0), preferred_element_type=FLOAT
        )
        part = lax.dot_general(
            pulled.astype(HALF),
            map_ref[:, cols],
            (((1,), (1,)), ((), ())),
            preferred_element_type=FLOAT,
        )
        total = part if total is None else total + part
    part_ref[...] = total
    up = total[2 * MEMBERS_HERE :].astype(HALF)
    down = total[: 4 * MEMBERS_HERE].astype(HALF)
    a_ref[...] = jnp.where(even, up, down)
    b_ref[...] = jnp.where(even, down, up)


def partial_adjoint(mine, other, perturb, column_map):
    matrix = member_matrix().T
    matrix = jnp.asarray(np.concatenate([matrix, matrix], axis=1), HALF)
    rim = ((4 * MEMBERS_HERE, COARSE_COLS), HALF)
    return call(
        adjoint_kernel,
        ((((ROWS + 2) * MEMBERS_HERE, COARSE_COLS), FLOAT), rim, rim),
        (mine, other, matrix, perturb, column_map),
    )


def gradient_kernel(a_ref, part_ref, b_ref, own_ref, grad_ref, half_ref, square_ref):
    below, above = edges()
    masks = [below] * 3 + [None] * 4 + [above] * 3
    even = is_even()
    square = None
    for start in range(0, COARSE_COLS, 128):
        cols = pl.ds(start, 128)
        low, high = sides(a_ref, b_ref, cols, even)
        part = [part_ref[row_slice(r), cols] for r in range(6)]
        rows = [low[0], low[1], low[2] + part[0], low[3] * below + part[1], part[2], part[3]]
        rows += [part[4] + high[0] * above, part[5] + high[1], high[2], high[3]]
        for r, value in enumerate(swept(rows, masks)):
            gradient = own_ref[row_slice(r), cols] + value
            grad_ref[row_slice(r), cols] = gradient
            half_ref[row_slice(r), cols] = gradient.astype(HALF)
            term = gradient * gradient
            square = term if square is None else square + term
    square_ref[...] = square[:8] + square[8:]


def gradient_of(low, part, high, own):
    shape = (ROWS * MEMBERS_HERE, COARSE_COLS)
    return call(
        gradient_kernel,
        ((shape, FLOAT), (shape, HALF), ((8, 128), FLOAT)),
        (low, part, high, own),
    )


def send_kernel(value_hbm, error_hbm, gain_ref, sent_ref, value_ref, error_ref, sem):
    copies = [
        pltpu.make_async_copy(value_hbm, value_ref, sem.at[0]),
        pltpu.make_async_copy(error_hbm, error_ref, sem.at[1]),
    ]
    for copy in copies:
        copy.start()
    for copy in copies:
        copy.wait()
    rows = []
    for group in range(NMEMBER):
        for ref in (value_ref, error_ref):
            rows.append(pltpu.roll(ref[...], (BATCHES - NTILE * group) % BATCHES, 1))
    sent_ref[EVEN] = jnp.transpose(jnp.concatenate(rows, axis=0))[:NTILE]
    sent_ref[ODD] = jnp.full((NTILE, 128), gain_ref[0], FLOAT)


def add_kernel(a_ref, b_ref, base_ref, out_ref):
    _, _, y_pos = place()
    for y in range(NY):
        out_ref[y] = a_ref[y] + b_ref[y]
    out_ref[y_pos, :, :WIDTH] += base_ref[...]


def pick_kernel(a_ref, b_ref, *out_refs):
    _, _, y_pos = place()
    for step, ref in enumerate(out_refs):
        y = lax.rem(y_pos + step, NY)
        ref[...] = a_ref[y] + b_ref[y]


def column_picks(column):
    ids = lax.broadcasted_iota(jnp.int32, (WIDTH, BATCHES), 0)
    return jnp.concatenate(
        [(ids == column[s : s + 1]).astype(FLOAT).astype(HALF) for s in range(SLOTS)], axis=1
    )


def row_factors(row, fraction):
    ids = lax.broadcasted_iota(jnp.int32, (FINE_ROWS, BATCHES), 0)
    return jnp.concatenate(
        [
            jnp.where(ids == row[s : s + 1], 1.0 - fraction[s : s + 1], 0.0)
            + jnp.where(ids == row[s : s + 1] + 1, fraction[s : s + 1], 0.0)
            for s in range(SLOTS)
        ],
        axis=1,
    )


def on_lanes(values):
    return jnp.concatenate([values[s : s + 1] for s in range(SLOTS)], axis=1)


def on_slots(values):
    return jnp.concatenate(
        [values[:, s * BATCHES : (s + 1) * BATCHES] for s in range(SLOTS)], axis=0
    )


def halves(values):
    high = values.astype(HALF)
    return jnp.concatenate([high, (values - high.astype(FLOAT)).astype(HALF)], axis=0)


def interpolated(field, picks, factors, fraction):
    shifted = jnp.concatenate([field[:, 1:], field[:, :1]], axis=1)
    got = jnp.dot(
        halves(jnp.concatenate([field, shifted], axis=0)), picks, preferred_element_type=FLOAT
    )
    got = got[: 2 * FINE_ROWS] + got[2 * FINE_ROWS :]
    left, right = got[:FINE_ROWS], got[FINE_ROWS:]
    mixed = left * (1.0 - fraction) + right * fraction
    return on_slots(jnp.sum(mixed * factors, axis=0, keepdims=True))


def located(index):
    row = index // WIDTH
    return row, index - row * WIDTH


def obs_kernel(
    a_ref, b_ref, c_ref, d_ref, index_ref, row_ref, column_ref, length_ref,
    spread_ref, weight_ref, full_ref, data_ref,
):
    _, core_pos, y_pos = place()
    slots = lax.broadcasted_iota(jnp.int32, (SLOTS, BATCHES), 0)
    for y in range(NY):
        field = sum(ref[y, :, :WIDTH] for ref in (b_ref, c_ref, d_ref)) + a_ref[y, :, :WIDTH]
        for step, ref in enumerate((a_ref, b_ref, c_ref, d_ref)):
            source = lax.rem(y_pos + NY - step, NY) * (NCORE * NTILE)
            load = ref[y, :, 256:]
            for core in range(NCORE):
                start = pl.multiple_of(source + core * NTILE, NTILE)
                data_ref[y, pl.ds(start, NTILE)] = pltpu.roll(
                    load, (BATCHES - RIDE - 2 * NTILE * core) % BATCHES, 1
                )
        data = jnp.transpose(data_ref[y])
        value, error = data[:SLOTS], data[SLOTS : 2 * SLOTS]
        gain = data[2 * SLOTS : 2 * SLOTS + 1]
        group = NCORE * y + core_pos
        row, column = located(index_ref[group])
        picks = column_picks(column)
        factors = row_factors(row, row_ref[group])
        fraction = on_lanes(column_ref[group])
        live = jnp.where(slots < length_ref[pl.ds(group, 1)], 1.0, 0.0)
        state = interpolated(field, picks, factors, fraction)
        bounded = jnp.tanh(state)
        derivative = 1.0 + gain * (1.0 - bounded * bounded)
        misfit = state + gain * bounded - value
        precision = live / (error * error)
        residual = derivative * misfit * precision

        @pl.when(y == y_pos)
        def _():
            weight_ref[...] = derivative * derivative * precision
            full_ref[...] = field

        weighted = factors * on_lanes(residual)
        both = jnp.concatenate([weighted * (1.0 - fraction), weighted * fraction], axis=0)
        got = lax.dot_general(
            halves(both), picks, (((1,), (1,)), ((), ())), preferred_element_type=FLOAT
        )
        got = got[: 2 * FINE_ROWS] + got[2 * FINE_ROWS :]
        left, right = got[:FINE_ROWS], got[FINE_ROWS:]
        spread_ref[y] = left + jnp.concatenate([right[:, -1:], right[:, :-1]], axis=1)


def curve_kernel(
    a_ref, b_ref, c_ref, d_ref, index_ref, row_ref, column_ref, weight_ref, square_ref,
    field_ref, sent_ref,
):
    _, core_pos, y_pos = place()
    own = NCORE * y_pos + core_pos
    field = a_ref[...] + b_ref[...] + c_ref[...] + d_ref[...]
    field_ref[...] = field
    row, column = located(index_ref[own])
    observed = interpolated(
        field, column_picks(column), row_factors(row, row_ref[own]), on_lanes(column_ref[own])
    )
    curvature = jnp.sum(weight_ref[...] * observed * observed, keepdims=True)
    square = jnp.sum(square_ref[...], keepdims=True)
    lanes = lax.broadcasted_iota(jnp.int32, (BATCHES, 128), 1)
    sent_ref[...] = jnp.where(lanes < 64, square, curvature)


def step_kernel(
    shared_ref, own_ref, grad_ref, full_ref, base_ref, image_ref, coarse_ref, increment_ref
):
    totals = jnp.sum(shared_ref[...], axis=0, keepdims=True)
    lanes = lax.broadcasted_iota(jnp.int32, (1, 128), 1)
    square = jnp.sum(jnp.where(lanes == 0, totals, 0.0), keepdims=True)
    curvature = jnp.sum(jnp.where(lanes == 127, totals, 0.0), keepdims=True)
    step = square / (square + curvature)
    for r in range(ROWS):
        coarse_ref[:, r, :] = own_ref[row_slice(r)] - step * grad_ref[row_slice(r)]
    increment_ref[...] = full_ref[...] - base_ref[...] - step * image_ref[...]


def shards(
    perturb,
    weights,
    column_map,
    background,
    stencil_index,
    row_fraction,
    column_fraction,
    block_lengths,
    obs_value,
    obs_error,
    instrument_gain,
):
    perturb, column_map = near(perturb), near(column_map)
    matrix = member_matrix()
    matrix = near(jnp.asarray(np.concatenate([matrix, matrix], axis=1), HALF))
    flat = (ROWS * MEMBERS_HERE, COARSE_COLS)
    own = jnp.transpose(weights, (1, 0, 2)).reshape(flat)
    half = own.astype(HALF)
    near_rows, far_rows = swap_both(half, half)

    (sent,) = call(
        send_kernel,
        (((2 * NTILE, 128), FLOAT),),
        (obs_value[0].T, obs_error[0].T, instrument_gain),
        far=(0, 1),
        scalar=(2,),
        work=WORK,
        scratch=[pltpu.VMEM((SLOTS, BATCHES), FLOAT)] * 2 + [pltpu.SemaphoreType.DMA((2,))],
    )
    data = lax.all_to_all(sent, "tile", split_axis=0, concat_axis=0, tiled=True)

    index = jnp.transpose(stencil_index[0], (1, 2, 0))
    row_frac = jnp.transpose(row_fraction[0], (1, 2, 0))
    column_frac = jnp.transpose(column_fraction[0], (1, 2, 0))
    lengths = block_lengths[0].T

    mine, other = partial_forward(
        laden_kernel, LADEN, near_rows, own, far_rows, matrix, perturb, column_map, data
    )
    (mine,) = call(add_kernel, (LADEN,), (mine, swap_core(other), background))
    pieces = [mine] + [turn(mine, NCORE * i, "member") for i in range(1, NY)]
    region = ((FINE_ROWS, WIDTH), FLOAT)
    spread, weight, full = call(
        obs_kernel,
        (REGIONS, ((SLOTS, BATCHES), FLOAT), region),
        (*pieces, index, row_frac, column_frac, lengths),
        scratch=[pltpu.VMEM((NY, BATCHES, 128), FLOAT)],
    )
    part, up, down = partial_adjoint(spread, swap_core(spread), perturb, column_map)
    near_rows, far_rows = swap_both(up, down)
    gradient, half, square = gradient_of(near_rows, part, far_rows, own)
    near_rows, far_rows = swap_both(half, half)
    mine, other = partial_forward(
        forward_kernel, REGIONS, near_rows, gradient, far_rows, matrix, perturb, column_map
    )
    pieces = call(pick_kernel, (region,) * NY, (mine, swap_core(other)))
    pieces = [pieces[0]] + [turn(pieces[i], NCORE * i, "member") for i in range(1, NY)]
    image, sent = call(
        curve_kernel,
        (region, ((BATCHES, 128), FLOAT)),
        (*pieces, index, row_frac, column_frac, weight, square),
    )
    shared = lax.all_to_all(sent, ("member", "tile"), split_axis=0, concat_axis=0, tiled=True)
    return call(
        step_kernel,
        (((MEMBERS_HERE, ROWS, COARSE_COLS), FLOAT), region),
        (shared, own, gradient, full, background, image),
        far_out=(0, 1),
    )


def solution(mesh):
    placed = (
        P("member", "tile", None),
        P("member", "tile", None),
        P(),
        P("tile", "member"),
        P("tile", None, None, None),
        P("tile", None, None, None),
        P("tile", None, None, None),
        P("tile", None, None),
        P(("member", "tile"), None, None),
        P(("member", "tile"), None, None),
        P(("member", "tile")),
    )
    return jax.shard_map(
        shards,
        mesh=mesh,
        in_specs=placed,
        out_specs=(P("member", "tile", None), P("tile", "member")),
        check_vma=False,
    )
```

```python
import jax
import jax.numpy as jnp
import numpy as np
from jax import lax
from jax.experimental import pallas as pl
from jax.experimental.pallas import tpu as pltpu
from jax.sharding import PartitionSpec as P

RATIO = 4
KSM = 3
DIFFUSION = 0.45
NTILE = 16
NMEMBER = 8
NCORE = 2
NY = NMEMBER // NCORE
MEMBERS_HERE = 16
ROWS = 4
FINE_ROWS = 16
COARSE_COLS = 1280
WIDTH = 320
CHUNK = NCORE * WIDTH
SLOTS = 8
BATCHES = 128
ROOM = 12 << 20
WORK = 2 * 10**10
EVEN, ODD = pl.ds(0, NTILE, stride=2), pl.ds(1, NTILE, stride=2)
FLOAT, HALF = jnp.float32, jnp.bfloat16


def refine_matrix():
    table = np.zeros((FINE_ROWS, ROWS + 2))
    for row in range(ROWS):
        for offset in range(RATIO):
            shift = (offset + 0.5) / RATIO - 0.5
            fine = RATIO * row + offset
            if shift < 0:
                table[fine, row + 1] += 1.0 + shift
                table[fine, row] -= shift
            else:
                table[fine, row + 1] += 1.0 - shift
                table[fine, row + 2] += shift
    return table


def member_matrix():
    return np.einsum("fr,kl->kfrl", refine_matrix(), np.eye(MEMBERS_HERE)).reshape(
        MEMBERS_HERE * FINE_ROWS, (ROWS + 2) * MEMBERS_HERE
    )


def ring():
    step = []
    for member in range(NMEMBER):
        core, here, there = member % NCORE, member * NTILE, (member ^ 1) * NTILE
        for tile in range(NTILE):
            onward = tile + 1 - 2 * core
            inside = 0 <= onward < NTILE
            step.append((here + tile, here + onward if inside else there + tile))
    return step


def swap_both(first_values, second_values):
    first = lax.ppermute(first_values, ("member", "tile"), ring())
    back = [(target, source) for source, target in ring()]
    second = lax.ppermute(second_values, ("member", "tile"), back)
    return first, second


def across(values, step):
    pairs = [(i, i ^ (NCORE * step)) for i in range(NMEMBER)]
    return lax.ppermute(values, "member", pairs)


def swap_core(values):
    return lax.ppermute(values, "member", [(i, i ^ 1) for i in range(NMEMBER)])


NEAR = pl.BlockSpec(memory_space=pltpu.VMEM)
FAR = pl.BlockSpec(memory_space=pltpu.HBM)
SCALAR = pl.BlockSpec(memory_space=pltpu.SMEM)


def near(values):
    return pltpu.with_memory_space_constraint(values, pltpu.VMEM)


def distant(values):
    return pltpu.with_memory_space_constraint(values, pltpu.HBM)


def call(kernel, out_shapes, arguments, far=(), scratch=(), far_out=(), scalar=(), work=10**9):
    specs = [
        SCALAR if i in scalar else FAR if i in far else NEAR for i in range(len(arguments))
    ]
    arguments = tuple(
        x if i in scalar else distant(x) if i in far else near(x)
        for i, x in enumerate(arguments)
    )
    return pl.pallas_call(
        kernel,
        out_shape=tuple(
            jax.ShapeDtypeStruct(shape, kind) if i in far_out else pltpu.VMEM(shape, kind)
            for i, (shape, kind) in enumerate(out_shapes)
        ),
        in_specs=specs,
        out_specs=tuple(NEAR for _ in out_shapes),
        scratch_shapes=list(scratch),
        compiler_params=pltpu.CompilerParams(vmem_limit_bytes=ROOM),
        cost_estimate=pl.CostEstimate(flops=work, transcendentals=0, bytes_accessed=work >> 7),
    )(*arguments)


def place():
    member_pos = lax.axis_index("member")
    return lax.axis_index("tile"), lax.rem(member_pos, NCORE), lax.div(member_pos, NCORE)


def edges():
    tile_pos = lax.axis_index("tile")
    return jnp.where(tile_pos > 0, 1.0, 0.0), jnp.where(tile_pos < NTILE - 1, 1.0, 0.0)


def swept(rows, masks):
    for _ in range(KSM):
        rows = [v if m is None else v * m for v, m in zip(rows, masks)]
        rows = [
            rows[i] + DIFFUSION * (rows[i - 1] + rows[i + 1] - 2.0 * rows[i])
            for i in range(1, len(rows) - 1)
        ]
        masks = masks[1:-1]
    return [v if m is None else v * m for v, m in zip(rows, masks)]


def row_slice(row):
    return pl.ds(row * MEMBERS_HERE, MEMBERS_HERE)


def downward():
    return lax.rem(lax.axis_index("member"), NCORE) == 1


def sides(a_ref, b_ref, cols, down_first):
    first = [a_ref[row_slice(r), cols].astype(FLOAT) for r in range(4)]
    second = [b_ref[row_slice(r), cols].astype(FLOAT) for r in range(4)]
    low = [jnp.where(down_first, v, u) for u, v in zip(first, second)]
    high = [jnp.where(down_first, u, v) for u, v in zip(first, second)]
    return low, high


def laden_kernel(
    a_ref, own_ref, b_ref, refine_ref, perturb_ref, map_ref, data_ref, mine_ref, other_ref, smooth_ref
):
    _, core_pos, _ = place()
    data, gain = data_ref[EVEN], data_ref[ODD]
    lanes = lax.broadcasted_iota(jnp.int32, data.shape, 1)
    home = RIDE + 2 * NTILE * core_pos
    for y in range(NY):
        for ref, parity in ((mine_ref, core_pos), (other_ref, 1 - core_pos)):
            shift = lax.rem(home + BATCHES - NTILE * (NCORE * y + parity), BATCHES)
            moved = jnp.where(lanes == home + 2 * SLOTS, gain, pltpu.roll(data, shift, 1))
            kept = (lanes >= home) & (lanes <= home + 2 * SLOTS)
            ref[y, :, 256:] = jnp.where(kept, moved, 0.0)
    forward_kernel(
        a_ref, own_ref, b_ref, refine_ref, perturb_ref, map_ref, mine_ref, other_ref, smooth_ref
    )


def forward_kernel(
    a_ref, own_ref, b_ref, refine_ref, perturb_ref, map_ref, mine_ref, other_ref, smooth_ref
):
    _, core_pos, _ = place()
    down_first = downward()
    below, above = edges()
    masks = [below] * 4 + [None] * 4 + [above] * 4
    for start in range(0, COARSE_COLS, 128):
        cols = pl.ds(start, 128)
        low, high = sides(a_ref, b_ref, cols, down_first)
        rows = low + [own_ref[row_slice(r), cols] for r in range(4)] + high
        for r, value in enumerate(swept(rows, masks)):
            smooth_ref[row_slice(r), cols] = value.astype(HALF)
    smooth = smooth_ref[...]
    for y in range(NY):
        cols = pl.ds(y * CHUNK, CHUNK)
        mapped = jnp.dot(smooth, map_ref[:, cols], preferred_element_type=FLOAT)
        high = mapped.astype(HALF)
        low = (mapped - high.astype(FLOAT)).astype(HALF)
        fine = jnp.dot(
            refine_ref[...], jnp.concatenate([high, low], axis=0), preferred_element_type=FLOAT
        )
        total = None
        for k in range(MEMBERS_HERE):
            term = fine[k * FINE_ROWS : (k + 1) * FINE_ROWS] * perturb_ref[k, :, cols].astype(FLOAT)
            total = term if total is None else total + term
        first, second = total[:, :WIDTH], total[:, WIDTH:]
        mine_ref[y, :, :WIDTH] = jnp.where(core_pos == 0, first, second)
        other_ref[y, :, :WIDTH] = jnp.where(core_pos == 0, second, first)


REGIONS = ((NY, FINE_ROWS, WIDTH), FLOAT)
LADEN = ((NY, FINE_ROWS, 384), FLOAT)
RIDE = 64


SMOOTH = pltpu.VMEM(((ROWS + 2) * MEMBERS_HERE, COARSE_COLS), HALF)


def partial_forward(kernel, shape, *arguments):
    return call(kernel, (shape, shape), arguments, scratch=[SMOOTH])


def adjoint_kernel(
    mine_ref, other_ref, back_ref, perturb_ref, map_ref,
    part_ref, a_ref, b_ref,
):
    _, core_pos, _ = place()
    down_first = downward()
    total = None
    for y in range(NY):
        cols = pl.ds(y * CHUNK, CHUNK)
        mine, other = mine_ref[y], other_ref[y]
        first = jnp.where(core_pos == 0, mine, other)
        second = jnp.where(core_pos == 0, other, mine)
        spread = jnp.concatenate([first, second], axis=1)
        highs, lows = [], []
        for k in range(MEMBERS_HERE):
            term = perturb_ref[k, :, cols].astype(FLOAT) * spread
            high = term.astype(HALF)
            highs.append(high)
            lows.append((term - high.astype(FLOAT)).astype(HALF))
        pulled = jnp.dot(
            back_ref[...], jnp.concatenate(highs + lows, axis=0), preferred_element_type=FLOAT
        )
        part = lax.dot_general(
            pulled.astype(HALF),
            map_ref[:, cols],
            (((1,), (1,)), ((), ())),
            preferred_element_type=FLOAT,
        )
        total = part if total is None else total + part
    part_ref[...] = total
    up = total[2 * MEMBERS_HERE :].astype(HALF)
    down = total[: 4 * MEMBERS_HERE].astype(HALF)
    a_ref[...] = jnp.where(down_first, down, up)
    b_ref[...] = jnp.where(down_first, up, down)


def partial_adjoint(mine, other, perturb, column_map):
    matrix = member_matrix().T
    matrix = jnp.asarray(np.concatenate([matrix, matrix], axis=1), HALF)
    rim = ((4 * MEMBERS_HERE, COARSE_COLS), HALF)
    return call(
        adjoint_kernel,
        ((((ROWS + 2) * MEMBERS_HERE, COARSE_COLS), FLOAT), rim, rim),
        (mine, other, matrix, perturb, column_map),
    )


def gradient_kernel(a_ref, part_ref, b_ref, own_ref, grad_ref, half_ref, square_ref):
    below, above = edges()
    masks = [below] * 3 + [None] * 4 + [above] * 3
    down_first = downward()
    square = None
    for start in range(0, COARSE_COLS, 128):
        cols = pl.ds(start, 128)
        low, high = sides(a_ref, b_ref, cols, down_first)
        part = [part_ref[row_slice(r), cols] for r in range(6)]
        rows = [low[0], low[1], low[2] + part[0], low[3] * below + part[1], part[2], part[3]]
        rows += [part[4] + high[0] * above, part[5] + high[1], high[2], high[3]]
        for r, value in enumerate(swept(rows, masks)):
            gradient = own_ref[row_slice(r), cols] + value
            grad_ref[row_slice(r), cols] = gradient
            half_ref[row_slice(r), cols] = gradient.astype(HALF)
            term = gradient * gradient
            square = term if square is None else square + term
    square_ref[...] = square[:8] + square[8:]


def gradient_of(low, part, high, own):
    shape = (ROWS * MEMBERS_HERE, COARSE_COLS)
    return call(
        gradient_kernel,
        ((shape, FLOAT), (shape, HALF), ((8, 128), FLOAT)),
        (low, part, high, own),
    )


def send_kernel(value_hbm, error_hbm, gain_ref, sent_ref, value_ref, error_ref, sem):
    copies = [
        pltpu.make_async_copy(value_hbm, value_ref, sem.at[0]),
        pltpu.make_async_copy(error_hbm, error_ref, sem.at[1]),
    ]
    for copy in copies:
        copy.start()
    for copy in copies:
        copy.wait()
    rows = []
    for group in range(NMEMBER):
        for ref in (value_ref, error_ref):
            rows.append(pltpu.roll(ref[...], (BATCHES - NTILE * group) % BATCHES, 1))
    sent_ref[EVEN] = jnp.transpose(jnp.concatenate(rows, axis=0))[:NTILE]
    sent_ref[ODD] = jnp.full((NTILE, 128), gain_ref[0], FLOAT)


def add_kernel(a_ref, b_ref, base_ref, out_ref):
    _, _, y_pos = place()
    for y in range(NY):
        out_ref[y] = a_ref[y] + b_ref[y]
    out_ref[y_pos, :, :WIDTH] += base_ref[...]


def pick_kernel(a_ref, b_ref, *out_refs):
    _, _, y_pos = place()
    for step, ref in enumerate(out_refs):
        y = lax.bitwise_xor(y_pos, step)
        ref[...] = a_ref[y] + b_ref[y]


def column_picks(column):
    ids = lax.broadcasted_iota(jnp.int32, (WIDTH, BATCHES), 0)
    return jnp.concatenate(
        [(ids == column[s : s + 1]).astype(FLOAT).astype(HALF) for s in range(SLOTS)], axis=1
    )


def row_factors(row, fraction):
    ids = lax.broadcasted_iota(jnp.int32, (FINE_ROWS, BATCHES), 0)
    return jnp.concatenate(
        [
            jnp.where(ids == row[s : s + 1], 1.0 - fraction[s : s + 1], 0.0)
            + jnp.where(ids == row[s : s + 1] + 1, fraction[s : s + 1], 0.0)
            for s in range(SLOTS)
        ],
        axis=1,
    )


def on_lanes(values):
    return jnp.concatenate([values[s : s + 1] for s in range(SLOTS)], axis=1)


def on_slots(values):
    return jnp.concatenate(
        [values[:, s * BATCHES : (s + 1) * BATCHES] for s in range(SLOTS)], axis=0
    )


def halves(values):
    high = values.astype(HALF)
    return jnp.concatenate([high, (values - high.astype(FLOAT)).astype(HALF)], axis=0)


def interpolated(field, picks, factors, fraction):
    shifted = jnp.concatenate([field[:, 1:], field[:, :1]], axis=1)
    got = jnp.dot(
        halves(jnp.concatenate([field, shifted], axis=0)), picks, preferred_element_type=FLOAT
    )
    got = got[: 2 * FINE_ROWS] + got[2 * FINE_ROWS :]
    left, right = got[:FINE_ROWS], got[FINE_ROWS:]
    mixed = left * (1.0 - fraction) + right * fraction
    return on_slots(jnp.sum(mixed * factors, axis=0, keepdims=True))


def located(index):
    row = index // WIDTH
    return row, index - row * WIDTH


def obs_kernel(
    a_ref, b_ref, c_ref, d_ref, index_ref, row_ref, column_ref, length_ref,
    spread_ref, weight_ref, full_ref, data_ref,
):
    _, core_pos, y_pos = place()
    slots = lax.broadcasted_iota(jnp.int32, (SLOTS, BATCHES), 0)
    for y in range(NY):
        field = sum(ref[y, :, :WIDTH] for ref in (b_ref, c_ref, d_ref)) + a_ref[y, :, :WIDTH]
        for step, ref in enumerate((a_ref, b_ref, c_ref, d_ref)):
            source = lax.bitwise_xor(y_pos, step) * (NCORE * NTILE)
            load = ref[y, :, 256:]
            for core in range(NCORE):
                start = pl.multiple_of(source + core * NTILE, NTILE)
                data_ref[y, pl.ds(start, NTILE)] = pltpu.roll(
                    load, (BATCHES - RIDE - 2 * NTILE * core) % BATCHES, 1
                )
        data = jnp.transpose(data_ref[y])
        value, error = data[:SLOTS], data[SLOTS : 2 * SLOTS]
        gain = data[2 * SLOTS : 2 * SLOTS + 1]
        group = NCORE * y + core_pos
        row, column = located(index_ref[group])
        picks = column_picks(column)
        factors = row_factors(row, row_ref[group])
        fraction = on_lanes(column_ref[group])
        live = jnp.where(slots < length_ref[pl.ds(group, 1)], 1.0, 0.0)
        state = interpolated(field, picks, factors, fraction)
        bounded = jnp.tanh(state)
        derivative = 1.0 + gain * (1.0 - bounded * bounded)
        misfit = state + gain * bounded - value
        precision = live / (error * error)
        residual = derivative * misfit * precision

        @pl.when(y == y_pos)
        def _():
            weight_ref[...] = derivative * derivative * precision
            full_ref[...] = field

        weighted = factors * on_lanes(residual)
        both = jnp.concatenate([weighted * (1.0 - fraction), weighted * fraction], axis=0)
        got = lax.dot_general(
            halves(both), picks, (((1,), (1,)), ((), ())), preferred_element_type=FLOAT
        )
        got = got[: 2 * FINE_ROWS] + got[2 * FINE_ROWS :]
        left, right = got[:FINE_ROWS], got[FINE_ROWS:]
        spread_ref[y] = left + jnp.concatenate([right[:, -1:], right[:, :-1]], axis=1)


def curve_kernel(
    a_ref, b_ref, c_ref, d_ref, index_ref, row_ref, column_ref, weight_ref, square_ref,
    field_ref, sent_ref,
):
    _, core_pos, y_pos = place()
    own = NCORE * y_pos + core_pos
    field = a_ref[...] + b_ref[...] + c_ref[...] + d_ref[...]
    field_ref[...] = field
    row, column = located(index_ref[own])
    observed = interpolated(
        field, column_picks(column), row_factors(row, row_ref[own]), on_lanes(column_ref[own])
    )
    curvature = jnp.sum(weight_ref[...] * observed * observed, keepdims=True)
    square = jnp.sum(square_ref[...], keepdims=True)
    lanes = lax.broadcasted_iota(jnp.int32, (BATCHES, 128), 1)
    sent_ref[...] = jnp.where(lanes < 64, square, curvature)


def step_kernel(
    shared_ref, own_ref, grad_ref, full_ref, base_ref, image_ref, coarse_ref, increment_ref
):
    totals = jnp.sum(shared_ref[...], axis=0, keepdims=True)
    lanes = lax.broadcasted_iota(jnp.int32, (1, 128), 1)
    square = jnp.sum(jnp.where(lanes == 0, totals, 0.0), keepdims=True)
    curvature = jnp.sum(jnp.where(lanes == 127, totals, 0.0), keepdims=True)
    step = square / (square + curvature)
    for r in range(ROWS):
        coarse_ref[:, r, :] = own_ref[row_slice(r)] - step * grad_ref[row_slice(r)]
    increment_ref[...] = full_ref[...] - base_ref[...] - step * image_ref[...]


def shards(
    perturb,
    weights,
    column_map,
    background,
    stencil_index,
    row_fraction,
    column_fraction,
    block_lengths,
    obs_value,
    obs_error,
    instrument_gain,
):
    perturb, column_map = near(perturb), near(column_map)
    matrix = member_matrix()
    matrix = near(jnp.asarray(np.concatenate([matrix, matrix], axis=1), HALF))
    flat = (ROWS * MEMBERS_HERE, COARSE_COLS)
    own = jnp.transpose(weights, (1, 0, 2)).reshape(flat)
    half = own.astype(HALF)
    near_rows, far_rows = swap_both(half, half)

    (sent,) = call(
        send_kernel,
        (((2 * NTILE, 128), FLOAT),),
        (obs_value[0].T, obs_error[0].T, instrument_gain),
        far=(0, 1),
        scalar=(2,),
        work=WORK,
        scratch=[pltpu.VMEM((SLOTS, BATCHES), FLOAT)] * 2 + [pltpu.SemaphoreType.DMA((2,))],
    )
    data = lax.all_to_all(sent, "tile", split_axis=0, concat_axis=0, tiled=True)

    index = jnp.transpose(stencil_index[0], (1, 2, 0))
    row_frac = jnp.transpose(row_fraction[0], (1, 2, 0))
    column_frac = jnp.transpose(column_fraction[0], (1, 2, 0))
    lengths = block_lengths[0].T

    mine, other = partial_forward(
        laden_kernel, LADEN, near_rows, own, far_rows, matrix, perturb, column_map, data
    )
    (mine,) = call(add_kernel, (LADEN,), (mine, swap_core(other), background))
    pieces = [mine] + [across(mine, i) for i in range(1, NY)]
    region = ((FINE_ROWS, WIDTH), FLOAT)
    spread, weight, full = call(
        obs_kernel,
        (REGIONS, ((SLOTS, BATCHES), FLOAT), region),
        (*pieces, index, row_frac, column_frac, lengths),
        scratch=[pltpu.VMEM((NY, BATCHES, 128), FLOAT)],
    )
    part, up, down = partial_adjoint(spread, swap_core(spread), perturb, column_map)
    near_rows, far_rows = swap_both(up, down)
    gradient, half, square = gradient_of(near_rows, part, far_rows, own)
    near_rows, far_rows = swap_both(half, half)
    mine, other = partial_forward(
        forward_kernel, REGIONS, near_rows, gradient, far_rows, matrix, perturb, column_map
    )
    pieces = call(pick_kernel, (region,) * NY, (mine, swap_core(other)))
    pieces = [pieces[0]] + [across(pieces[i], i) for i in range(1, NY)]
    image, sent = call(
        curve_kernel,
        (region, ((BATCHES, 128), FLOAT)),
        (*pieces, index, row_frac, column_frac, weight, square),
    )
    shared = lax.all_to_all(sent, ("member", "tile"), split_axis=0, concat_axis=0, tiled=True)
    return call(
        step_kernel,
        (((MEMBERS_HERE, ROWS, COARSE_COLS), FLOAT), region),
        (shared, own, gradient, full, background, image),
        far_out=(0, 1),
    )


def solution(mesh):
    placed = (
        P("member", "tile", None),
        P("member", "tile", None),
        P(),
        P("tile", "member"),
        P("tile", None, None, None),
        P("tile", None, None, None),
        P("tile", None, None, None),
        P("tile", None, None),
        P(("member", "tile"), None, None),
        P(("member", "tile"), None, None),
        P(("member", "tile")),
    )
    return jax.shard_map(
        shards,
        mesh=mesh,
        in_specs=placed,
        out_specs=(P("member", "tile", None), P("tile", "member")),
        check_vma=False,
    )
```

```python
import jax
import jax.numpy as jnp
import numpy as np
from jax import lax
from jax.experimental import pallas as pl
from jax.experimental.pallas import tpu as pltpu
from jax.sharding import PartitionSpec as P

RATIO = 4
KSM = 3
DIFFUSION = 0.45
NTILE = 16
NMEMBER = 8
NCORE = 2
NY = NMEMBER // NCORE
MEMBERS_HERE = 16
ROWS = 4
FINE_ROWS = 16
COARSE_COLS = 1280
WIDTH = 320
CHUNK = NCORE * WIDTH
SLOTS = 8
BATCHES = 128
ROOM = 12 << 20
WORK = 2 * 10**10
EVEN, ODD = pl.ds(0, NTILE, stride=2), pl.ds(1, NTILE, stride=2)
FLOAT, HALF = jnp.float32, jnp.bfloat16


def refine_matrix():
    table = np.zeros((FINE_ROWS, ROWS + 2))
    for row in range(ROWS):
        for offset in range(RATIO):
            shift = (offset + 0.5) / RATIO - 0.5
            fine = RATIO * row + offset
            if shift < 0:
                table[fine, row + 1] += 1.0 + shift
                table[fine, row] -= shift
            else:
                table[fine, row + 1] += 1.0 - shift
                table[fine, row + 2] += shift
    return table


def member_matrix():
    return np.einsum("fr,kl->kfrl", refine_matrix(), np.eye(MEMBERS_HERE)).reshape(
        MEMBERS_HERE * FINE_ROWS, (ROWS + 2) * MEMBERS_HERE
    )


def ring():
    step = []
    for member in range(NMEMBER):
        core, here, there = member % NCORE, member * NTILE, (member ^ 1) * NTILE
        for tile in range(NTILE):
            onward = tile + 1 - 2 * core
            inside = 0 <= onward < NTILE
            step.append((here + tile, here + onward if inside else there + tile))
    return step


def swap_both(first_values, second_values):
    first = lax.ppermute(first_values, ("member", "tile"), ring())
    back = [(target, source) for source, target in ring()]
    second = lax.ppermute(second_values, ("member", "tile"), back)
    return first, second


def across(values, step):
    pairs = [(i, i ^ (NCORE * step)) for i in range(NMEMBER)]
    return lax.ppermute(values, "member", pairs)


def swap_core(values):
    return lax.ppermute(values, "member", [(i, i ^ 1) for i in range(NMEMBER)])


NEAR = pl.BlockSpec(memory_space=pltpu.VMEM)
FAR = pl.BlockSpec(memory_space=pltpu.HBM)
SCALAR = pl.BlockSpec(memory_space=pltpu.SMEM)


def near(values):
    return pltpu.with_memory_space_constraint(values, pltpu.VMEM)


def distant(values):
    return pltpu.with_memory_space_constraint(values, pltpu.HBM)


def call(kernel, out_shapes, arguments, far=(), scratch=(), far_out=(), scalar=(), work=10**9):
    specs = [
        SCALAR if i in scalar else FAR if i in far else NEAR for i in range(len(arguments))
    ]
    arguments = tuple(
        x if i in scalar else distant(x) if i in far else near(x)
        for i, x in enumerate(arguments)
    )
    return pl.pallas_call(
        kernel,
        out_shape=tuple(
            jax.ShapeDtypeStruct(shape, kind) if i in far_out else pltpu.VMEM(shape, kind)
            for i, (shape, kind) in enumerate(out_shapes)
        ),
        in_specs=specs,
        out_specs=tuple(NEAR for _ in out_shapes),
        scratch_shapes=list(scratch),
        compiler_params=pltpu.CompilerParams(vmem_limit_bytes=ROOM),
        cost_estimate=pl.CostEstimate(flops=work, transcendentals=0, bytes_accessed=work >> 7),
    )(*arguments)


def place():
    member_pos = lax.axis_index("member")
    return lax.axis_index("tile"), lax.rem(member_pos, NCORE), lax.div(member_pos, NCORE)


def edges():
    tile_pos = lax.axis_index("tile")
    return jnp.where(tile_pos > 0, 1.0, 0.0), jnp.where(tile_pos < NTILE - 1, 1.0, 0.0)


def swept(rows, masks):
    for _ in range(KSM):
        rows = [v if m is None else v * m for v, m in zip(rows, masks)]
        rows = [
            rows[i] + DIFFUSION * (rows[i - 1] + rows[i + 1] - 2.0 * rows[i])
            for i in range(1, len(rows) - 1)
        ]
        masks = masks[1:-1]
    return [v if m is None else v * m for v, m in zip(rows, masks)]


def row_slice(row):
    return pl.ds(row * MEMBERS_HERE, MEMBERS_HERE)


def downward():
    return lax.rem(lax.axis_index("member"), NCORE) == 1


def sides(a_ref, b_ref, cols, down_first):
    first = [a_ref[row_slice(r), cols].astype(FLOAT) for r in range(4)]
    second = [b_ref[row_slice(r), cols].astype(FLOAT) for r in range(4)]
    low = [jnp.where(down_first, v, u) for u, v in zip(first, second)]
    high = [jnp.where(down_first, u, v) for u, v in zip(first, second)]
    return low, high


def laden_kernel(
    a_ref, own_ref, b_ref, refine_ref, perturb_ref, map_ref, data_ref, mine_ref, other_ref, smooth_ref
):
    _, core_pos, _ = place()
    data, gain = data_ref[EVEN], data_ref[ODD]
    lanes = lax.broadcasted_iota(jnp.int32, data.shape, 1)
    home = RIDE + 2 * NTILE * core_pos
    for y in range(NY):
        for ref, parity in ((mine_ref, core_pos), (other_ref, 1 - core_pos)):
            shift = lax.rem(home + BATCHES - NTILE * (NCORE * y + parity), BATCHES)
            moved = jnp.where(lanes == home + 2 * SLOTS, gain, pltpu.roll(data, shift, 1))
            kept = (lanes >= home) & (lanes <= home + 2 * SLOTS)
            ref[y, :, 256:] = jnp.where(kept, moved, 0.0)
    forward_kernel(
        a_ref, own_ref, b_ref, refine_ref, perturb_ref, map_ref, mine_ref, other_ref, smooth_ref
    )


def forward_kernel(
    a_ref, own_ref, b_ref, refine_ref, perturb_ref, map_ref, mine_ref, other_ref, smooth_ref
):
    _, core_pos, _ = place()
    down_first = downward()
    below, above = edges()
    masks = [below] * 4 + [None] * 4 + [above] * 4
    for start in range(0, COARSE_COLS, 128):
        cols = pl.ds(start, 128)
        low, high = sides(a_ref, b_ref, cols, down_first)
        rows = low + [own_ref[row_slice(r), cols] for r in range(4)] + high
        for r, value in enumerate(swept(rows, masks)):
            smooth_ref[row_slice(r), cols] = value.astype(HALF)
    smooth = smooth_ref[...]
    for y in range(NY):
        cols = pl.ds(y * CHUNK, CHUNK)
        mapped = jnp.dot(smooth, map_ref[:, cols], preferred_element_type=FLOAT)
        high = mapped.astype(HALF)
        low = (mapped - high.astype(FLOAT)).astype(HALF)
        fine = jnp.dot(
            refine_ref[...], jnp.concatenate([high, low], axis=0), preferred_element_type=FLOAT
        )
        total = None
        for k in range(MEMBERS_HERE):
            term = fine[k * FINE_ROWS : (k + 1) * FINE_ROWS] * perturb_ref[k, :, cols].astype(FLOAT)
            total = term if total is None else total + term
        first, second = total[:, :WIDTH], total[:, WIDTH:]
        mine_ref[y, :, :WIDTH] = jnp.where(core_pos == 0, first, second)
        other_ref[y, :, :WIDTH] = jnp.where(core_pos == 0, second, first)


REGIONS = ((NY, FINE_ROWS, WIDTH), FLOAT)
LADEN = ((NY, FINE_ROWS, 384), FLOAT)
RIDE = 64


SMOOTH = pltpu.VMEM(((ROWS + 2) * MEMBERS_HERE, COARSE_COLS), HALF)


def partial_forward(kernel, shape, *arguments):
    return call(kernel, (shape, shape), arguments, scratch=[SMOOTH])


def adjoint_kernel(
    mine_ref, other_ref, back_ref, perturb_ref, map_ref,
    part_ref, a_ref, b_ref,
):
    _, core_pos, _ = place()
    down_first = downward()
    total = None
    for y in range(NY):
        cols = pl.ds(y * CHUNK, CHUNK)
        mine, other = mine_ref[y], other_ref[y]
        first = jnp.where(core_pos == 0, mine, other)
        second = jnp.where(core_pos == 0, other, mine)
        spread = jnp.concatenate([first, second], axis=1)
        highs, lows = [], []
        for k in range(MEMBERS_HERE):
            term = perturb_ref[k, :, cols].astype(FLOAT) * spread
            high = term.astype(HALF)
            highs.append(high)
            lows.append((term - high.astype(FLOAT)).astype(HALF))
        pulled = jnp.dot(
            back_ref[...], jnp.concatenate(highs + lows, axis=0), preferred_element_type=FLOAT
        )
        part = lax.dot_general(
            pulled.astype(HALF),
            map_ref[:, cols],
            (((1,), (1,)), ((), ())),
            preferred_element_type=FLOAT,
        )
        total = part if total is None else total + part
    part_ref[...] = total
    up = total[2 * MEMBERS_HERE :].astype(HALF)
    down = total[: 4 * MEMBERS_HERE].astype(HALF)
    a_ref[...] = jnp.where(down_first, down, up)
    b_ref[...] = jnp.where(down_first, up, down)


def partial_adjoint(mine, other, perturb, column_map):
    matrix = member_matrix().T
    matrix = jnp.asarray(np.concatenate([matrix, matrix], axis=1), HALF)
    rim = ((4 * MEMBERS_HERE, COARSE_COLS), HALF)
    return call(
        adjoint_kernel,
        ((((ROWS + 2) * MEMBERS_HERE, COARSE_COLS), FLOAT), rim, rim),
        (mine, other, matrix, perturb, column_map),
    )


def gradient_kernel(a_ref, part_ref, b_ref, own_ref, grad_ref, half_ref, square_ref):
    below, above = edges()
    masks = [below] * 3 + [None] * 4 + [above] * 3
    down_first = downward()
    square = None
    for start in range(0, COARSE_COLS, 128):
        cols = pl.ds(start, 128)
        low, high = sides(a_ref, b_ref, cols, down_first)
        part = [part_ref[row_slice(r), cols] for r in range(6)]
        rows = [low[0], low[1], low[2] + part[0], low[3] * below + part[1], part[2], part[3]]
        rows += [part[4] + high[0] * above, part[5] + high[1], high[2], high[3]]
        for r, value in enumerate(swept(rows, masks)):
            gradient = own_ref[row_slice(r), cols] + value
            grad_ref[row_slice(r), cols] = gradient
            half_ref[row_slice(r), cols] = gradient.astype(HALF)
            term = gradient * gradient
            square = term if square is None else square + term
    square_ref[...] = square[:8] + square[8:]


def gradient_of(low, part, high, own):
    shape = (ROWS * MEMBERS_HERE, COARSE_COLS)
    return call(
        gradient_kernel,
        ((shape, FLOAT), (shape, HALF), ((8, 128), FLOAT)),
        (low, part, high, own),
    )


def start_kernel(
    value_hbm, error_hbm, gain_ref, weights_hbm,
    sent_ref, own_ref, half_ref, value_ref, error_ref, weights_ref, sem,
):
    copies = [
        pltpu.make_async_copy(value_hbm, value_ref, sem.at[0]),
        pltpu.make_async_copy(error_hbm, error_ref, sem.at[1]),
        pltpu.make_async_copy(weights_hbm, weights_ref, sem.at[2]),
    ]
    for copy in copies:
        copy.start()
    for copy in copies:
        copy.wait()
    for r in range(ROWS):
        values = weights_ref[:, r, :]
        own_ref[row_slice(r)] = values
        half_ref[row_slice(r)] = values.astype(HALF)
    rows = []
    for group in range(NMEMBER):
        for ref in (value_ref, error_ref):
            rows.append(pltpu.roll(ref[...], (BATCHES - NTILE * group) % BATCHES, 1))
    sent_ref[EVEN] = jnp.transpose(jnp.concatenate(rows, axis=0))[:NTILE]
    sent_ref[ODD] = jnp.full((NTILE, 128), gain_ref[0], FLOAT)


def add_kernel(a_ref, b_ref, base_ref, out_ref):
    _, _, y_pos = place()
    for y in range(NY):
        out_ref[y] = a_ref[y] + b_ref[y]
    out_ref[y_pos, :, :WIDTH] += base_ref[...]


def pick_kernel(a_ref, b_ref, *out_refs):
    _, _, y_pos = place()
    for step, ref in enumerate(out_refs):
        y = lax.bitwise_xor(y_pos, step)
        ref[...] = a_ref[y] + b_ref[y]


def column_picks(column):
    ids = lax.broadcasted_iota(jnp.int32, (WIDTH, BATCHES), 0)
    return jnp.concatenate(
        [(ids == column[s : s + 1]).astype(FLOAT).astype(HALF) for s in range(SLOTS)], axis=1
    )


def row_factors(row, fraction):
    ids = lax.broadcasted_iota(jnp.int32, (FINE_ROWS, BATCHES), 0)
    return jnp.concatenate(
        [
            jnp.where(ids == row[s : s + 1], 1.0 - fraction[s : s + 1], 0.0)
            + jnp.where(ids == row[s : s + 1] + 1, fraction[s : s + 1], 0.0)
            for s in range(SLOTS)
        ],
        axis=1,
    )


def on_lanes(values):
    return jnp.concatenate([values[s : s + 1] for s in range(SLOTS)], axis=1)


def on_slots(values):
    return jnp.concatenate(
        [values[:, s * BATCHES : (s + 1) * BATCHES] for s in range(SLOTS)], axis=0
    )


def halves(values):
    high = values.astype(HALF)
    return jnp.concatenate([high, (values - high.astype(FLOAT)).astype(HALF)], axis=0)


def located(index):
    row = index // WIDTH
    return row, index - row * WIDTH


def prepare_kernel(index_ref, row_ref, column_ref, picks_ref, both_ref):
    _, core_pos, _ = place()
    for y in range(NY):
        group = NCORE * y + core_pos
        row, column = located(index_ref[group])
        picks_ref[y] = column_picks(column)
        factors = row_factors(row, row_ref[group])
        fraction = on_lanes(column_ref[group])
        both_ref[y, :FINE_ROWS] = factors * (1.0 - fraction)
        both_ref[y, FINE_ROWS:] = factors * fraction


def interpolated(field, picks, both):
    shifted = jnp.concatenate([field[:, 1:], field[:, :1]], axis=1)
    got = jnp.dot(
        halves(jnp.concatenate([field, shifted], axis=0)), picks, preferred_element_type=FLOAT
    )
    got = (got[: 2 * FINE_ROWS] + got[2 * FINE_ROWS :]) * both
    return on_slots(jnp.sum(got, axis=0, keepdims=True))


def obs_kernel(
    a_ref, b_ref, c_ref, d_ref, picks_ref, both_ref, length_ref,
    spread_ref, weight_ref, full_ref, data_ref,
):
    _, core_pos, y_pos = place()
    slots = lax.broadcasted_iota(jnp.int32, (SLOTS, BATCHES), 0)
    for y in range(NY):
        field = sum(ref[y, :, :WIDTH] for ref in (b_ref, c_ref, d_ref)) + a_ref[y, :, :WIDTH]
        for step, ref in enumerate((a_ref, b_ref, c_ref, d_ref)):
            source = lax.bitwise_xor(y_pos, step) * (NCORE * NTILE)
            load = ref[y, :, 256:]
            for core in range(NCORE):
                start = pl.multiple_of(source + core * NTILE, NTILE)
                data_ref[y, pl.ds(start, NTILE)] = pltpu.roll(
                    load, (BATCHES - RIDE - 2 * NTILE * core) % BATCHES, 1
                )
        data = jnp.transpose(data_ref[y])
        value, error = data[:SLOTS], data[SLOTS : 2 * SLOTS]
        gain = data[2 * SLOTS : 2 * SLOTS + 1]
        group = NCORE * y + core_pos
        picks, both = picks_ref[y], both_ref[y]
        live = jnp.where(slots < length_ref[pl.ds(group, 1)], 1.0, 0.0)
        state = interpolated(field, picks, both)
        bounded = jnp.tanh(state)
        derivative = 1.0 + gain * (1.0 - bounded * bounded)
        misfit = state + gain * bounded - value
        precision = live / (error * error)
        residual = derivative * misfit * precision

        @pl.when(y == y_pos)
        def _():
            weight_ref[...] = derivative * derivative * precision
            full_ref[...] = field

        got = lax.dot_general(
            halves(both * on_lanes(residual)), picks, (((1,), (1,)), ((), ())), preferred_element_type=FLOAT
        )
        got = got[: 2 * FINE_ROWS] + got[2 * FINE_ROWS :]
        left, right = got[:FINE_ROWS], got[FINE_ROWS:]
        spread_ref[y] = left + jnp.concatenate([right[:, -1:], right[:, :-1]], axis=1)


def curve_kernel(
    a_ref, b_ref, c_ref, d_ref, picks_ref, both_ref, weight_ref, square_ref, field_ref, sent_ref
):
    _, _, y_pos = place()
    field = a_ref[...] + b_ref[...] + c_ref[...] + d_ref[...]
    field_ref[...] = field
    observed = interpolated(field, picks_ref[y_pos], both_ref[y_pos])
    curvature = jnp.sum(weight_ref[...] * observed * observed, keepdims=True)
    square = jnp.sum(square_ref[...], keepdims=True)
    lanes = lax.broadcasted_iota(jnp.int32, (BATCHES, 128), 1)
    sent_ref[...] = jnp.where(lanes < 64, square, curvature)


def step_kernel(
    shared_ref, own_ref, grad_ref, full_ref, base_ref, image_ref, coarse_ref, increment_ref
):
    totals = jnp.sum(shared_ref[...], axis=0, keepdims=True)
    lanes = lax.broadcasted_iota(jnp.int32, (1, 128), 1)
    square = jnp.sum(jnp.where(lanes == 0, totals, 0.0), keepdims=True)
    curvature = jnp.sum(jnp.where(lanes == 127, totals, 0.0), keepdims=True)
    step = square / (square + curvature)
    for r in range(ROWS):
        coarse_ref[:, r, :] = own_ref[row_slice(r)] - step * grad_ref[row_slice(r)]
    increment_ref[...] = full_ref[...] - base_ref[...] - step * image_ref[...]


def shards(
    perturb,
    weights,
    column_map,
    background,
    stencil_index,
    row_fraction,
    column_fraction,
    block_lengths,
    obs_value,
    obs_error,
    instrument_gain,
):
    perturb, column_map = near(perturb), near(column_map)
    matrix = member_matrix()
    matrix = near(jnp.asarray(np.concatenate([matrix, matrix], axis=1), HALF))
    flat = (ROWS * MEMBERS_HERE, COARSE_COLS)
    sent, own, half = call(
        start_kernel,
        (((2 * NTILE, 128), FLOAT), (flat, FLOAT), (flat, HALF)),
        (obs_value[0].T, obs_error[0].T, instrument_gain, weights),
        far=(0, 1, 3),
        scalar=(2,),
        work=WORK,
        scratch=[pltpu.VMEM((SLOTS, BATCHES), FLOAT)] * 2
        + [pltpu.VMEM((MEMBERS_HERE, ROWS, COARSE_COLS), FLOAT), pltpu.SemaphoreType.DMA((3,))],
    )
    near_rows, far_rows = swap_both(half, half)

    data = lax.all_to_all(sent, "tile", split_axis=0, concat_axis=0, tiled=True)

    index = jnp.transpose(stencil_index[0], (1, 2, 0))
    row_frac = jnp.transpose(row_fraction[0], (1, 2, 0))
    column_frac = jnp.transpose(column_fraction[0], (1, 2, 0))
    lengths = block_lengths[0].T

    mine, other = partial_forward(
        laden_kernel, LADEN, near_rows, own, far_rows, matrix, perturb, column_map, data
    )
    (mine,) = call(add_kernel, (LADEN,), (mine, swap_core(other), background))
    pieces = [mine]
    for i in range(1, NY):
        pieces.append(across(mine, i))
    picks, both = call(
        prepare_kernel,
        (
            ((NY, WIDTH, SLOTS * BATCHES), HALF),
            ((NY, 2 * FINE_ROWS, SLOTS * BATCHES), FLOAT),
        ),
        (index, row_frac, column_frac),
    )
    region = ((FINE_ROWS, WIDTH), FLOAT)
    spread, weight, full = call(
        obs_kernel,
        (REGIONS, ((SLOTS, BATCHES), FLOAT), region),
        (*pieces, picks, both, lengths),
        scratch=[pltpu.VMEM((NY, BATCHES, 128), FLOAT)],
    )
    part, up, down = partial_adjoint(spread, swap_core(spread), perturb, column_map)
    near_rows, far_rows = swap_both(up, down)
    gradient, half, square = gradient_of(near_rows, part, far_rows, own)
    near_rows, far_rows = swap_both(half, half)
    mine, other = partial_forward(
        forward_kernel, REGIONS, near_rows, gradient, far_rows, matrix, perturb, column_map
    )
    pieces = call(pick_kernel, (region,) * NY, (mine, swap_core(other)))
    pieces = [pieces[0]] + [across(pieces[i], i) for i in range(1, NY)]
    image, sent = call(
        curve_kernel,
        (region, ((BATCHES, 128), FLOAT)),
        (*pieces, picks, both, weight, square),
    )
    shared = lax.all_to_all(sent, ("member", "tile"), split_axis=0, concat_axis=0, tiled=True)
    return call(
        step_kernel,
        (((MEMBERS_HERE, ROWS, COARSE_COLS), FLOAT), region),
        (shared, own, gradient, full, background, image),
        far_out=(0, 1),
    )


def solution(mesh):
    placed = (
        P("member", "tile", None),
        P("member", "tile", None),
        P(),
        P("tile", "member"),
        P("tile", None, None, None),
        P("tile", None, None, None),
        P("tile", None, None, None),
        P("tile", None, None),
        P(("member", "tile"), None, None),
        P(("member", "tile"), None, None),
        P(("member", "tile")),
    )
    return jax.shard_map(
        shards,
        mesh=mesh,
        in_specs=placed,
        out_specs=(P("member", "tile", None), P("tile", "member")),
        check_vma=False,
    )
```

```python
import jax
import jax.numpy as jnp
import numpy as np
from jax import lax
from jax.experimental import pallas as pl
from jax.experimental.pallas import tpu as pltpu
from jax.sharding import PartitionSpec as P

RATIO = 4
KSM = 3
DIFFUSION = 0.45
NTILE = 16
NMEMBER = 8
NCORE = 2
NY = NMEMBER // NCORE
MEMBERS_HERE = 16
ROWS = 4
FINE_ROWS = 16
COARSE_COLS = 1280
WIDTH = 320
CHUNK = NCORE * WIDTH
SLOTS = 8
BATCHES = 128
ROOM = 12 << 20
WORK = 2 * 10**10
EVEN, ODD = pl.ds(0, NTILE, stride=2), pl.ds(1, NTILE, stride=2)
FLOAT, HALF = jnp.float32, jnp.bfloat16


def refine_matrix():
    table = np.zeros((FINE_ROWS, ROWS + 2))
    for row in range(ROWS):
        for offset in range(RATIO):
            shift = (offset + 0.5) / RATIO - 0.5
            fine = RATIO * row + offset
            if shift < 0:
                table[fine, row + 1] += 1.0 + shift
                table[fine, row] -= shift
            else:
                table[fine, row + 1] += 1.0 - shift
                table[fine, row + 2] += shift
    return table


def member_matrix():
    return np.einsum("fr,kl->kfrl", refine_matrix(), np.eye(MEMBERS_HERE)).reshape(
        MEMBERS_HERE * FINE_ROWS, (ROWS + 2) * MEMBERS_HERE
    )


def ring():
    step = []
    for member in range(NMEMBER):
        core, here, there = member % NCORE, member * NTILE, (member ^ 1) * NTILE
        for tile in range(NTILE):
            onward = tile + 1 - 2 * core
            inside = 0 <= onward < NTILE
            step.append((here + tile, here + onward if inside else there + tile))
    return step


def swap_both(first_values, second_values):
    first = lax.ppermute(first_values, ("member", "tile"), ring())
    back = [(target, source) for source, target in ring()]
    second = lax.ppermute(second_values, ("member", "tile"), back)
    return first, second


def across(values, step):
    pairs = [(i, i ^ (NCORE * step)) for i in range(NMEMBER)]
    return lax.ppermute(values, "member", pairs)


def swap_core(values):
    return lax.ppermute(values, "member", [(i, i ^ 1) for i in range(NMEMBER)])


NEAR = pl.BlockSpec(memory_space=pltpu.VMEM)
FAR = pl.BlockSpec(memory_space=pltpu.HBM)
SCALAR = pl.BlockSpec(memory_space=pltpu.SMEM)


def near(values):
    return pltpu.with_memory_space_constraint(values, pltpu.VMEM)


def distant(values):
    return pltpu.with_memory_space_constraint(values, pltpu.HBM)


def call(kernel, out_shapes, arguments, far=(), scratch=(), far_out=(), scalar=(), work=10**9):
    specs = [
        SCALAR if i in scalar else FAR if i in far else NEAR for i in range(len(arguments))
    ]
    arguments = tuple(
        x if i in scalar else distant(x) if i in far else near(x)
        for i, x in enumerate(arguments)
    )
    return pl.pallas_call(
        kernel,
        out_shape=tuple(
            jax.ShapeDtypeStruct(shape, kind) if i in far_out else pltpu.VMEM(shape, kind)
            for i, (shape, kind) in enumerate(out_shapes)
        ),
        in_specs=specs,
        out_specs=tuple(NEAR for _ in out_shapes),
        scratch_shapes=list(scratch),
        compiler_params=pltpu.CompilerParams(vmem_limit_bytes=ROOM),
        cost_estimate=pl.CostEstimate(flops=work, transcendentals=0, bytes_accessed=work >> 7),
    )(*arguments)


def place():
    member_pos = lax.axis_index("member")
    return lax.axis_index("tile"), lax.rem(member_pos, NCORE), lax.div(member_pos, NCORE)


def edges():
    tile_pos = lax.axis_index("tile")
    return jnp.where(tile_pos > 0, 1.0, 0.0), jnp.where(tile_pos < NTILE - 1, 1.0, 0.0)


def swept(rows, masks):
    for _ in range(KSM):
        rows = [v if m is None else v * m for v, m in zip(rows, masks)]
        rows = [
            rows[i] + DIFFUSION * (rows[i - 1] + rows[i + 1] - 2.0 * rows[i])
            for i in range(1, len(rows) - 1)
        ]
        masks = masks[1:-1]
    return [v if m is None else v * m for v, m in zip(rows, masks)]


def row_slice(row):
    return pl.ds(row * MEMBERS_HERE, MEMBERS_HERE)


def downward():
    return lax.rem(lax.axis_index("member"), NCORE) == 1


def sides(a_ref, b_ref, cols, down_first):
    first = [a_ref[row_slice(r), cols].astype(FLOAT) for r in range(4)]
    second = [b_ref[row_slice(r), cols].astype(FLOAT) for r in range(4)]
    low = [jnp.where(down_first, v, u) for u, v in zip(first, second)]
    high = [jnp.where(down_first, u, v) for u, v in zip(first, second)]
    return low, high


def window(parity, y):
    return pl.ds(pl.multiple_of(y * CHUNK + 256 * parity, 128), 384)


def load(data_ref, ref, parity, core_pos):
    data, gain = data_ref[EVEN], data_ref[ODD]
    lanes = lax.broadcasted_iota(jnp.int32, data.shape, 1)
    home = RIDE + 2 * NTILE * core_pos
    for y in range(NY):
        shift = lax.rem(home + BATCHES - NTILE * (NCORE * y + parity), BATCHES)
        moved = jnp.where(lanes == home + 2 * SLOTS, gain, pltpu.roll(data, shift, 1))
        kept = (lanes >= home) & (lanes <= home + 2 * SLOTS)
        ref[y, :, 256:] = jnp.where(kept, moved, 0.0)


def regions_of(smooth_ref, refine_ref, perturb_ref, map_ref, parity, out_ref):
    smooth = smooth_ref[...]
    for y in range(NY):
        cols = window(parity, y)
        mapped = jnp.dot(smooth, map_ref[:, cols], preferred_element_type=FLOAT)
        high = mapped.astype(HALF)
        low = (mapped - high.astype(FLOAT)).astype(HALF)
        fine = jnp.dot(
            refine_ref[...], jnp.concatenate([high, low], axis=0), preferred_element_type=FLOAT
        )
        total = None
        for k in range(MEMBERS_HERE):
            term = fine[k * FINE_ROWS : (k + 1) * FINE_ROWS] * perturb_ref[k, :, cols].astype(FLOAT)
            total = term if total is None else total + term
        out_ref[y, :, :WIDTH] = jnp.where(parity == 0, total[:, :WIDTH], total[:, 384 - WIDTH :])


def other_kernel(a_ref, own_ref, b_ref, refine_ref, perturb_ref, map_ref, *refs):
    other_ref, smooth_ref = refs[-2:]
    _, core_pos, _ = place()
    down_first = downward()
    below, above = edges()
    masks = [below] * 4 + [None] * 4 + [above] * 4
    for start in range(0, COARSE_COLS, 128):
        cols = pl.ds(start, 128)
        low, high = sides(a_ref, b_ref, cols, down_first)
        rows = low + [own_ref[row_slice(r), cols] for r in range(4)] + high
        for r, value in enumerate(swept(rows, masks)):
            smooth_ref[row_slice(r), cols] = value.astype(HALF)
    if len(refs) > 2:
        load(refs[0], other_ref, 1 - core_pos, core_pos)
    regions_of(smooth_ref, refine_ref, perturb_ref, map_ref, 1 - core_pos, other_ref)


def mine_kernel(smooth_ref, refine_ref, perturb_ref, map_ref, *refs):
    _, core_pos, _ = place()
    if len(refs) > 1:
        load(refs[0], refs[-1], core_pos, core_pos)
    regions_of(smooth_ref, refine_ref, perturb_ref, map_ref, core_pos, refs[-1])


REGIONS = ((NY, FINE_ROWS, WIDTH), FLOAT)
LADEN = ((NY, FINE_ROWS, 384), FLOAT)
RIDE = 64


SMOOTH = (((ROWS + 2) * MEMBERS_HERE, COARSE_COLS), HALF)


def partial_forward(shape, first, own, second, operators, data=()):
    other, smooth = call(other_kernel, (shape, SMOOTH), (first, own, second) + operators + data)
    there = swap_core(other)
    (mine,) = call(mine_kernel, (shape,), (smooth,) + operators + data)
    return mine, there


PART = (((ROWS + 2) * MEMBERS_HERE, COARSE_COLS), FLOAT)


def pulled_part(values_ref, back_ref, perturb_ref, map_ref, parity):
    total = None
    for y in range(NY):
        cols = window(parity, y)
        values = values_ref[y]
        rest = jnp.zeros((FINE_ROWS, 384 - WIDTH), FLOAT)
        spread = jnp.where(
            parity == 0,
            jnp.concatenate([values, rest], axis=1),
            jnp.concatenate([rest, values], axis=1),
        )
        highs, lows = [], []
        for k in range(MEMBERS_HERE):
            term = perturb_ref[k, :, cols].astype(FLOAT) * spread
            high = term.astype(HALF)
            highs.append(high)
            lows.append((term - high.astype(FLOAT)).astype(HALF))
        pulled = jnp.dot(
            back_ref[...], jnp.concatenate(highs + lows, axis=0), preferred_element_type=FLOAT
        )
        part = lax.dot_general(
            pulled.astype(HALF),
            map_ref[:, cols],
            (((1,), (1,)), ((), ())),
            preferred_element_type=FLOAT,
        )
        total = part if total is None else total + part
    return total


def pull_mine_kernel(mine_ref, back_ref, perturb_ref, map_ref, part_ref):
    _, core_pos, _ = place()
    part_ref[...] = pulled_part(mine_ref, back_ref, perturb_ref, map_ref, core_pos)


def pull_other_kernel(
    mine_ref, other_ref, back_ref, perturb_ref, map_ref, part_ref, a_ref, b_ref
):
    _, core_pos, _ = place()
    down_first = downward()
    total = mine_ref[...] + pulled_part(other_ref, back_ref, perturb_ref, map_ref, 1 - core_pos)
    part_ref[...] = total
    up = total[2 * MEMBERS_HERE :].astype(HALF)
    down = total[: 4 * MEMBERS_HERE].astype(HALF)
    a_ref[...] = jnp.where(down_first, down, up)
    b_ref[...] = jnp.where(down_first, up, down)


def partial_adjoint(spread, perturb, column_map):
    matrix = member_matrix().T
    matrix = jnp.asarray(np.concatenate([matrix, matrix], axis=1), HALF)
    operators = (matrix, perturb, column_map)
    there = swap_core(spread)
    (mine,) = call(pull_mine_kernel, (PART,), (spread,) + operators)
    rim = ((4 * MEMBERS_HERE, COARSE_COLS), HALF)
    return call(pull_other_kernel, (PART, rim, rim), (mine, there) + operators)


def gradient_kernel(a_ref, part_ref, b_ref, own_ref, grad_ref, half_ref, square_ref):
    below, above = edges()
    masks = [below] * 3 + [None] * 4 + [above] * 3
    down_first = downward()
    square = None
    for start in range(0, COARSE_COLS, 128):
        cols = pl.ds(start, 128)
        low, high = sides(a_ref, b_ref, cols, down_first)
        part = [part_ref[row_slice(r), cols] for r in range(6)]
        rows = [low[0], low[1], low[2] + part[0], low[3] * below + part[1], part[2], part[3]]
        rows += [part[4] + high[0] * above, part[5] + high[1], high[2], high[3]]
        for r, value in enumerate(swept(rows, masks)):
            gradient = own_ref[row_slice(r), cols] + value
            grad_ref[row_slice(r), cols] = gradient
            half_ref[row_slice(r), cols] = gradient.astype(HALF)
            term = gradient * gradient
            square = term if square is None else square + term
    square_ref[...] = square[:8] + square[8:]


def gradient_of(low, part, high, own):
    shape = (ROWS * MEMBERS_HERE, COARSE_COLS)
    return call(
        gradient_kernel,
        ((shape, FLOAT), (shape, HALF), ((8, 128), FLOAT)),
        (low, part, high, own),
    )


def start_kernel(
    value_hbm, error_hbm, gain_ref, weights_hbm,
    sent_ref, own_ref, half_ref, value_ref, error_ref, weights_ref, sem,
):
    copies = [
        pltpu.make_async_copy(value_hbm, value_ref, sem.at[0]),
        pltpu.make_async_copy(error_hbm, error_ref, sem.at[1]),
        pltpu.make_async_copy(weights_hbm, weights_ref, sem.at[2]),
    ]
    for copy in copies:
        copy.start()
    for copy in copies:
        copy.wait()
    for r in range(ROWS):
        values = weights_ref[:, r, :]
        own_ref[row_slice(r)] = values
        half_ref[row_slice(r)] = values.astype(HALF)
    rows = []
    for group in range(NMEMBER):
        for ref in (value_ref, error_ref):
            rows.append(pltpu.roll(ref[...], (BATCHES - NTILE * group) % BATCHES, 1))
    sent_ref[EVEN] = jnp.transpose(jnp.concatenate(rows, axis=0))[:NTILE]
    sent_ref[ODD] = jnp.full((NTILE, 128), gain_ref[0], FLOAT)


def add_kernel(a_ref, b_ref, base_ref, out_ref):
    _, _, y_pos = place()
    for y in range(NY):
        out_ref[y] = a_ref[y] + b_ref[y]
    out_ref[y_pos, :, :WIDTH] += base_ref[...]


def pick_kernel(a_ref, b_ref, *out_refs):
    _, _, y_pos = place()
    for step, ref in enumerate(out_refs):
        y = lax.bitwise_xor(y_pos, step)
        ref[...] = a_ref[y] + b_ref[y]


def column_picks(column):
    ids = lax.broadcasted_iota(jnp.int32, (WIDTH, BATCHES), 0)
    return jnp.concatenate(
        [(ids == column[s : s + 1]).astype(FLOAT).astype(HALF) for s in range(SLOTS)], axis=1
    )


def row_factors(row, fraction):
    ids = lax.broadcasted_iota(jnp.int32, (FINE_ROWS, BATCHES), 0)
    return jnp.concatenate(
        [
            jnp.where(ids == row[s : s + 1], 1.0 - fraction[s : s + 1], 0.0)
            + jnp.where(ids == row[s : s + 1] + 1, fraction[s : s + 1], 0.0)
            for s in range(SLOTS)
        ],
        axis=1,
    )


def on_lanes(values):
    return jnp.concatenate([values[s : s + 1] for s in range(SLOTS)], axis=1)


def on_slots(values):
    return jnp.concatenate(
        [values[:, s * BATCHES : (s + 1) * BATCHES] for s in range(SLOTS)], axis=0
    )


def halves(values):
    high = values.astype(HALF)
    return jnp.concatenate([high, (values - high.astype(FLOAT)).astype(HALF)], axis=0)


def located(index):
    row = index // WIDTH
    return row, index - row * WIDTH


def prepare_kernel(index_ref, row_ref, column_ref, picks_ref, both_ref):
    _, core_pos, _ = place()
    for y in range(NY):
        group = NCORE * y + core_pos
        row, column = located(index_ref[group])
        picks_ref[y] = column_picks(column)
        factors = row_factors(row, row_ref[group])
        fraction = on_lanes(column_ref[group])
        both_ref[y, :FINE_ROWS] = factors * (1.0 - fraction)
        both_ref[y, FINE_ROWS:] = factors * fraction


def interpolated(field, picks, both):
    shifted = jnp.concatenate([field[:, 1:], field[:, :1]], axis=1)
    got = jnp.dot(
        halves(jnp.concatenate([field, shifted], axis=0)), picks, preferred_element_type=FLOAT
    )
    got = (got[: 2 * FINE_ROWS] + got[2 * FINE_ROWS :]) * both
    return on_slots(jnp.sum(got, axis=0, keepdims=True))


def obs_kernel(
    a_ref, b_ref, c_ref, d_ref, picks_ref, both_ref, length_ref,
    spread_ref, weight_ref, full_ref, data_ref,
):
    _, core_pos, y_pos = place()
    slots = lax.broadcasted_iota(jnp.int32, (SLOTS, BATCHES), 0)
    for y in range(NY):
        field = sum(ref[y, :, :WIDTH] for ref in (b_ref, c_ref, d_ref)) + a_ref[y, :, :WIDTH]
        for step, ref in enumerate((a_ref, b_ref, c_ref, d_ref)):
            source = lax.bitwise_xor(y_pos, step) * (NCORE * NTILE)
            load = ref[y, :, 256:]
            for core in range(NCORE):
                start = pl.multiple_of(source + core * NTILE, NTILE)
                data_ref[y, pl.ds(start, NTILE)] = pltpu.roll(
                    load, (BATCHES - RIDE - 2 * NTILE * core) % BATCHES, 1
                )
        data = jnp.transpose(data_ref[y])
        value, error = data[:SLOTS], data[SLOTS : 2 * SLOTS]
        gain = data[2 * SLOTS : 2 * SLOTS + 1]
        group = NCORE * y + core_pos
        picks, both = picks_ref[y], both_ref[y]
        live = jnp.where(slots < length_ref[pl.ds(group, 1)], 1.0, 0.0)
        state = interpolated(field, picks, both)
        bounded = jnp.tanh(state)
        derivative = 1.0 + gain * (1.0 - bounded * bounded)
        misfit = state + gain * bounded - value
        precision = live / (error * error)
        residual = derivative * misfit * precision

        @pl.when(y == y_pos)
        def _():
            weight_ref[...] = derivative * derivative * precision
            full_ref[...] = field

        got = lax.dot_general(
            halves(both * on_lanes(residual)), picks, (((1,), (1,)), ((), ())), preferred_element_type=FLOAT
        )
        got = got[: 2 * FINE_ROWS] + got[2 * FINE_ROWS :]
        left, right = got[:FINE_ROWS], got[FINE_ROWS:]
        spread_ref[y] = left + jnp.concatenate([right[:, -1:], right[:, :-1]], axis=1)


def curve_kernel(
    a_ref, b_ref, c_ref, d_ref, picks_ref, both_ref, weight_ref, square_ref, field_ref, sent_ref
):
    _, _, y_pos = place()
    field = a_ref[...] + b_ref[...] + c_ref[...] + d_ref[...]
    field_ref[...] = field
    observed = interpolated(field, picks_ref[y_pos], both_ref[y_pos])
    curvature = jnp.sum(weight_ref[...] * observed * observed, keepdims=True)
    square = jnp.sum(square_ref[...], keepdims=True)
    lanes = lax.broadcasted_iota(jnp.int32, (BATCHES, 128), 1)
    sent_ref[...] = jnp.where(lanes < 64, square, curvature)


def step_kernel(
    shared_ref, own_ref, grad_ref, full_ref, base_ref, image_ref, coarse_ref, increment_ref
):
    totals = jnp.sum(shared_ref[...], axis=0, keepdims=True)
    lanes = lax.broadcasted_iota(jnp.int32, (1, 128), 1)
    square = jnp.sum(jnp.where(lanes == 0, totals, 0.0), keepdims=True)
    curvature = jnp.sum(jnp.where(lanes == 127, totals, 0.0), keepdims=True)
    step = square / (square + curvature)
    for r in range(ROWS):
        coarse_ref[:, r, :] = own_ref[row_slice(r)] - step * grad_ref[row_slice(r)]
    increment_ref[...] = full_ref[...] - base_ref[...] - step * image_ref[...]


def shards(
    perturb,
    weights,
    column_map,
    background,
    stencil_index,
    row_fraction,
    column_fraction,
    block_lengths,
    obs_value,
    obs_error,
    instrument_gain,
):
    perturb, column_map = near(perturb), near(column_map)
    matrix = member_matrix()
    matrix = near(jnp.asarray(np.concatenate([matrix, matrix], axis=1), HALF))
    flat = (ROWS * MEMBERS_HERE, COARSE_COLS)
    sent, own, half = call(
        start_kernel,
        (((2 * NTILE, 128), FLOAT), (flat, FLOAT), (flat, HALF)),
        (obs_value[0].T, obs_error[0].T, instrument_gain, weights),
        far=(0, 1, 3),
        scalar=(2,),
        work=WORK,
        scratch=[pltpu.VMEM((SLOTS, BATCHES), FLOAT)] * 2
        + [pltpu.VMEM((MEMBERS_HERE, ROWS, COARSE_COLS), FLOAT), pltpu.SemaphoreType.DMA((3,))],
    )
    near_rows, far_rows = swap_both(half, half)

    data = lax.all_to_all(sent, "tile", split_axis=0, concat_axis=0, tiled=True)

    index = jnp.transpose(stencil_index[0], (1, 2, 0))
    row_frac = jnp.transpose(row_fraction[0], (1, 2, 0))
    column_frac = jnp.transpose(column_fraction[0], (1, 2, 0))
    lengths = block_lengths[0].T

    operators = (matrix, perturb, column_map)
    mine, there = partial_forward(LADEN, near_rows, own, far_rows, operators, (data,))
    (mine,) = call(add_kernel, (LADEN,), (mine, there, background))
    pieces = [mine]
    for i in range(1, NY):
        pieces.append(across(mine, i))
    picks, both = call(
        prepare_kernel,
        (
            ((NY, WIDTH, SLOTS * BATCHES), HALF),
            ((NY, 2 * FINE_ROWS, SLOTS * BATCHES), FLOAT),
        ),
        (index, row_frac, column_frac),
    )
    region = ((FINE_ROWS, WIDTH), FLOAT)
    spread, weight, full = call(
        obs_kernel,
        (REGIONS, ((SLOTS, BATCHES), FLOAT), region),
        (*pieces, picks, both, lengths),
        scratch=[pltpu.VMEM((NY, BATCHES, 128), FLOAT)],
    )
    part, up, down = partial_adjoint(spread, perturb, column_map)
    near_rows, far_rows = swap_both(up, down)
    gradient, half, square = gradient_of(near_rows, part, far_rows, own)
    near_rows, far_rows = swap_both(half, half)
    mine, there = partial_forward(REGIONS, near_rows, gradient, far_rows, operators)
    turned = call(pick_kernel, (region,) * NY, (mine, there))
    pieces = [turned[0]]
    for i in range(1, NY):
        pieces.append(across(turned[i], i))
    image, sent = call(
        curve_kernel,
        (region, ((BATCHES, 128), FLOAT)),
        (*pieces, picks, both, weight, square),
    )
    shared = lax.all_to_all(sent, ("member", "tile"), split_axis=0, concat_axis=0, tiled=True)
    return call(
        step_kernel,
        (((MEMBERS_HERE, ROWS, COARSE_COLS), FLOAT), region),
        (shared, own, gradient, full, background, image),
        far_out=(0, 1),
    )


def solution(mesh):
    placed = (
        P("member", "tile", None),
        P("member", "tile", None),
        P(),
        P("tile", "member"),
        P("tile", None, None, None),
        P("tile", None, None, None),
        P("tile", None, None, None),
        P("tile", None, None),
        P(("member", "tile"), None, None),
        P(("member", "tile"), None, None),
        P(("member", "tile")),
    )
    return jax.shard_map(
        shards,
        mesh=mesh,
        in_specs=placed,
        out_specs=(P("member", "tile", None), P("tile", "member")),
        check_vma=False,
    )
```

```python
import jax
import jax.numpy as jnp
import numpy as np
from jax import lax
from jax.experimental import pallas as pl
from jax.experimental.pallas import tpu as pltpu
from jax.sharding import PartitionSpec as P

RATIO = 4
KSM = 3
DIFFUSION = 0.45
NTILE = 16
NMEMBER = 8
NCORE = 2
NY = NMEMBER // NCORE
MEMBERS_HERE = 16
ROWS = 4
FINE_ROWS = 16
COARSE_COLS = 1280
WIDTH = 320
CHUNK = NCORE * WIDTH
SLOTS = 8
BATCHES = 128
ROOM = 16 << 20
WORK = 2 * 10**10
EVEN, ODD = pl.ds(0, NTILE, stride=2), pl.ds(1, NTILE, stride=2)
FLOAT, HALF = jnp.float32, jnp.bfloat16


def refine_matrix():
    table = np.zeros((FINE_ROWS, ROWS + 2))
    for row in range(ROWS):
        for offset in range(RATIO):
            shift = (offset + 0.5) / RATIO - 0.5
            fine = RATIO * row + offset
            if shift < 0:
                table[fine, row + 1] += 1.0 + shift
                table[fine, row] -= shift
            else:
                table[fine, row + 1] += 1.0 - shift
                table[fine, row + 2] += shift
    return table


def member_matrix():
    return np.einsum("fr,kl->kfrl", refine_matrix(), np.eye(MEMBERS_HERE)).reshape(
        MEMBERS_HERE * FINE_ROWS, (ROWS + 2) * MEMBERS_HERE
    )


def ring():
    step = []
    for member in range(NMEMBER):
        core, here, there = member % NCORE, member * NTILE, (member ^ 1) * NTILE
        for tile in range(NTILE):
            onward = tile + 1 - 2 * core
            inside = 0 <= onward < NTILE
            step.append((here + tile, here + onward if inside else there + tile))
    return step


def swap_both(first_values, second_values):
    first = lax.ppermute(first_values, ("member", "tile"), ring())
    back = [(target, source) for source, target in ring()]
    second = lax.ppermute(second_values, ("member", "tile"), back)
    return first, second


def across(values, step):
    pairs = [(i, i ^ (NCORE * step)) for i in range(NMEMBER)]
    return lax.ppermute(values, "member", pairs)


def swap_core(values):
    return lax.ppermute(values, "member", [(i, i ^ 1) for i in range(NMEMBER)])


NEAR = pl.BlockSpec(memory_space=pltpu.VMEM)
FAR = pl.BlockSpec(memory_space=pltpu.HBM)
SCALAR = pl.BlockSpec(memory_space=pltpu.SMEM)


def near(values):
    return pltpu.with_memory_space_constraint(values, pltpu.VMEM)


def distant(values):
    return pltpu.with_memory_space_constraint(values, pltpu.HBM)


def call(kernel, out_shapes, arguments, far=(), scratch=(), far_out=(), scalar=(), work=10**9):
    specs = [
        SCALAR if i in scalar else FAR if i in far else NEAR for i in range(len(arguments))
    ]
    arguments = tuple(
        x if i in scalar else distant(x) if i in far else near(x)
        for i, x in enumerate(arguments)
    )
    return pl.pallas_call(
        kernel,
        out_shape=tuple(
            jax.ShapeDtypeStruct(shape, kind) if i in far_out else pltpu.VMEM(shape, kind)
            for i, (shape, kind) in enumerate(out_shapes)
        ),
        in_specs=specs,
        out_specs=tuple(NEAR for _ in out_shapes),
        scratch_shapes=list(scratch),
        compiler_params=pltpu.CompilerParams(vmem_limit_bytes=ROOM),
        cost_estimate=pl.CostEstimate(flops=work, transcendentals=0, bytes_accessed=work >> 7),
    )(*arguments)


def place():
    member_pos = lax.axis_index("member")
    return lax.axis_index("tile"), lax.rem(member_pos, NCORE), lax.div(member_pos, NCORE)


def edges():
    tile_pos = lax.axis_index("tile")
    return jnp.where(tile_pos > 0, 1.0, 0.0), jnp.where(tile_pos < NTILE - 1, 1.0, 0.0)


def swept(rows, masks):
    for _ in range(KSM):
        rows = [v if m is None else v * m for v, m in zip(rows, masks)]
        rows = [
            rows[i] + DIFFUSION * (rows[i - 1] + rows[i + 1] - 2.0 * rows[i])
            for i in range(1, len(rows) - 1)
        ]
        masks = masks[1:-1]
    return [v if m is None else v * m for v, m in zip(rows, masks)]


def row_slice(row):
    return pl.ds(row * MEMBERS_HERE, MEMBERS_HERE)


def downward():
    return lax.rem(lax.axis_index("member"), NCORE) == 1


def sides(a_ref, b_ref, cols, down_first):
    first = [a_ref[row_slice(r), cols].astype(FLOAT) for r in range(4)]
    second = [b_ref[row_slice(r), cols].astype(FLOAT) for r in range(4)]
    low = [jnp.where(down_first, v, u) for u, v in zip(first, second)]
    high = [jnp.where(down_first, u, v) for u, v in zip(first, second)]
    return low, high


def laden_kernel(
    a_ref, own_ref, b_ref, refine_ref, perturb_ref, map_ref, data_ref, mine_ref, other_ref, smooth_ref
):
    _, core_pos, _ = place()
    data, gain = data_ref[EVEN], data_ref[ODD]
    lanes = lax.broadcasted_iota(jnp.int32, data.shape, 1)
    home = RIDE + 2 * NTILE * core_pos
    for y in range(NY):
        for ref, parity in ((mine_ref, core_pos), (other_ref, 1 - core_pos)):
            shift = lax.rem(home + BATCHES - NTILE * (NCORE * y + parity), BATCHES)
            moved = jnp.where(lanes == home + 2 * SLOTS, gain, pltpu.roll(data, shift, 1))
            kept = (lanes >= home) & (lanes <= home + 2 * SLOTS)
            ref[y, :, 256:] = jnp.where(kept, moved, 0.0)
    forward_kernel(
        a_ref, own_ref, b_ref, refine_ref, perturb_ref, map_ref, mine_ref, other_ref, smooth_ref
    )


def forward_kernel(
    a_ref, own_ref, b_ref, refine_ref, perturb_ref, map_ref, mine_ref, other_ref, smooth_ref
):
    _, core_pos, _ = place()
    down_first = downward()
    below, above = edges()
    masks = [below] * 4 + [None] * 4 + [above] * 4
    for start in range(0, COARSE_COLS, 128):
        cols = pl.ds(start, 128)
        low, high = sides(a_ref, b_ref, cols, down_first)
        rows = low + [own_ref[row_slice(r), cols] for r in range(4)] + high
        for r, value in enumerate(swept(rows, masks)):
            smooth_ref[row_slice(r), cols] = value.astype(HALF)
    smooth = smooth_ref[...]
    for pair in range(0, NY, 2):
        cols = pl.ds(pair * CHUNK, 2 * CHUNK)
        mapped = jnp.dot(smooth, map_ref[:, cols], preferred_element_type=FLOAT)
        high = mapped.astype(HALF)
        low = (mapped - high.astype(FLOAT)).astype(HALF)
        fine = jnp.dot(
            refine_ref[...], jnp.concatenate([high, low], axis=0), preferred_element_type=FLOAT
        )
        total = None
        for k in range(MEMBERS_HERE):
            term = fine[k * FINE_ROWS : (k + 1) * FINE_ROWS] * perturb_ref[k, :, cols].astype(FLOAT)
            total = term if total is None else total + term
        for y in range(pair, pair + 2):
            start = (y - pair) * CHUNK
            first = total[:, start : start + WIDTH]
            second = total[:, start + WIDTH : start + CHUNK]
            mine_ref[y, :, :WIDTH] = jnp.where(core_pos == 0, first, second)
            other_ref[y, :, :WIDTH] = jnp.where(core_pos == 0, second, first)


REGIONS = ((NY, FINE_ROWS, WIDTH), FLOAT)
LADEN = ((NY, FINE_ROWS, 384), FLOAT)
RIDE = 64


SMOOTH = pltpu.VMEM(((ROWS + 2) * MEMBERS_HERE, COARSE_COLS), HALF)


def partial_forward(kernel, shape, *arguments):
    return call(kernel, (shape, shape), arguments, scratch=[SMOOTH])


def adjoint_kernel(
    mine_ref, other_ref, back_ref, perturb_ref, map_ref,
    part_ref, a_ref, b_ref,
):
    _, core_pos, _ = place()
    down_first = downward()
    total = None
    for pair in range(0, NY, 2):
        cols = pl.ds(pair * CHUNK, 2 * CHUNK)
        regions = []
        for y in range(pair, pair + 2):
            mine, other = mine_ref[y], other_ref[y]
            regions.append(jnp.where(core_pos == 0, mine, other))
            regions.append(jnp.where(core_pos == 0, other, mine))
        spread = jnp.concatenate(regions, axis=1)
        highs, lows = [], []
        for k in range(MEMBERS_HERE):
            term = perturb_ref[k, :, cols].astype(FLOAT) * spread
            high = term.astype(HALF)
            highs.append(high)
            lows.append((term - high.astype(FLOAT)).astype(HALF))
        pulled = jnp.dot(
            back_ref[...], jnp.concatenate(highs + lows, axis=0), preferred_element_type=FLOAT
        )
        part = lax.dot_general(
            pulled.astype(HALF),
            map_ref[:, cols],
            (((1,), (1,)), ((), ())),
            preferred_element_type=FLOAT,
        )
        total = part if total is None else total + part
    part_ref[...] = total
    up = total[2 * MEMBERS_HERE :].astype(HALF)
    down = total[: 4 * MEMBERS_HERE].astype(HALF)
    a_ref[...] = jnp.where(down_first, down, up)
    b_ref[...] = jnp.where(down_first, up, down)


def partial_adjoint(mine, other, perturb, column_map):
    matrix = member_matrix().T
    matrix = jnp.asarray(np.concatenate([matrix, matrix], axis=1), HALF)
    rim = ((4 * MEMBERS_HERE, COARSE_COLS), HALF)
    return call(
        adjoint_kernel,
        ((((ROWS + 2) * MEMBERS_HERE, COARSE_COLS), FLOAT), rim, rim),
        (mine, other, matrix, perturb, column_map),
    )


def gradient_kernel(a_ref, part_ref, b_ref, own_ref, grad_ref, half_ref, square_ref):
    below, above = edges()
    masks = [below] * 3 + [None] * 4 + [above] * 3
    down_first = downward()
    square = None
    for start in range(0, COARSE_COLS, 128):
        cols = pl.ds(start, 128)
        low, high = sides(a_ref, b_ref, cols, down_first)
        part = [part_ref[row_slice(r), cols] for r in range(6)]
        rows = [low[0], low[1], low[2] + part[0], low[3] * below + part[1], part[2], part[3]]
        rows += [part[4] + high[0] * above, part[5] + high[1], high[2], high[3]]
        for r, value in enumerate(swept(rows, masks)):
            gradient = own_ref[row_slice(r), cols] + value
            grad_ref[row_slice(r), cols] = gradient
            half_ref[row_slice(r), cols] = gradient.astype(HALF)
            term = gradient * gradient
            square = term if square is None else square + term
    square_ref[...] = square[:8] + square[8:]


def gradient_of(low, part, high, own):
    shape = (ROWS * MEMBERS_HERE, COARSE_COLS)
    return call(
        gradient_kernel,
        ((shape, FLOAT), (shape, HALF), ((8, 128), FLOAT)),
        (low, part, high, own),
    )


def start_kernel(
    value_hbm, error_hbm, gain_ref, weights_hbm,
    sent_ref, own_ref, half_ref, value_ref, error_ref, weights_ref, sem,
):
    copies = [
        pltpu.make_async_copy(value_hbm, value_ref, sem.at[0]),
        pltpu.make_async_copy(error_hbm, error_ref, sem.at[1]),
        pltpu.make_async_copy(weights_hbm, weights_ref, sem.at[2]),
    ]
    for copy in copies:
        copy.start()
    for copy in copies:
        copy.wait()
    for r in range(ROWS):
        values = weights_ref[:, r, :]
        own_ref[row_slice(r)] = values
        half_ref[row_slice(r)] = values.astype(HALF)
    rows = []
    for group in range(NMEMBER):
        for ref in (value_ref, error_ref):
            rows.append(pltpu.roll(ref[...], (BATCHES - NTILE * group) % BATCHES, 1))
    sent_ref[EVEN] = jnp.transpose(jnp.concatenate(rows, axis=0))[:NTILE]
    sent_ref[ODD] = jnp.full((NTILE, 128), gain_ref[0], FLOAT)


def add_kernel(a_ref, b_ref, base_ref, out_ref):
    _, _, y_pos = place()
    for y in range(NY):
        out_ref[y] = a_ref[y] + b_ref[y]
    out_ref[y_pos, :, :WIDTH] += base_ref[...]


def pick_kernel(a_ref, b_ref, *out_refs):
    _, _, y_pos = place()
    for step, ref in enumerate(out_refs):
        y = lax.bitwise_xor(y_pos, step)
        ref[...] = a_ref[y] + b_ref[y]


def column_picks(column):
    ids = lax.broadcasted_iota(jnp.int32, (WIDTH, BATCHES), 0)
    return jnp.concatenate(
        [(ids == column[s : s + 1]).astype(FLOAT).astype(HALF) for s in range(SLOTS)], axis=1
    )


def row_factors(row, fraction):
    ids = lax.broadcasted_iota(jnp.int32, (FINE_ROWS, BATCHES), 0)
    return jnp.concatenate(
        [
            jnp.where(ids == row[s : s + 1], 1.0 - fraction[s : s + 1], 0.0)
            + jnp.where(ids == row[s : s + 1] + 1, fraction[s : s + 1], 0.0)
            for s in range(SLOTS)
        ],
        axis=1,
    )


def on_lanes(values):
    return jnp.concatenate([values[s : s + 1] for s in range(SLOTS)], axis=1)


def on_slots(values):
    return jnp.concatenate(
        [values[:, s * BATCHES : (s + 1) * BATCHES] for s in range(SLOTS)], axis=0
    )


def halves(values):
    high = values.astype(HALF)
    return jnp.concatenate([high, (values - high.astype(FLOAT)).astype(HALF)], axis=0)


def located(index):
    row = index // WIDTH
    return row, index - row * WIDTH


def prepare_kernel(index_ref, row_ref, column_ref, picks_ref, both_ref):
    _, core_pos, _ = place()
    for y in range(NY):
        group = NCORE * y + core_pos
        row, column = located(index_ref[group])
        picks_ref[y] = column_picks(column)
        factors = row_factors(row, row_ref[group])
        fraction = on_lanes(column_ref[group])
        both_ref[y, :FINE_ROWS] = factors * (1.0 - fraction)
        both_ref[y, FINE_ROWS:] = factors * fraction


def interpolated(field, picks, both):
    shifted = jnp.concatenate([field[:, 1:], field[:, :1]], axis=1)
    got = jnp.dot(
        halves(jnp.concatenate([field, shifted], axis=0)), picks, preferred_element_type=FLOAT
    )
    got = (got[: 2 * FINE_ROWS] + got[2 * FINE_ROWS :]) * both
    return on_slots(jnp.sum(got, axis=0, keepdims=True))


def obs_kernel(
    a_ref, b_ref, c_ref, d_ref, picks_ref, both_ref, length_ref,
    spread_ref, weight_ref, full_ref, data_ref,
):
    _, core_pos, y_pos = place()
    slots = lax.broadcasted_iota(jnp.int32, (SLOTS, BATCHES), 0)
    for y in range(NY):
        field = sum(ref[y, :, :WIDTH] for ref in (b_ref, c_ref, d_ref)) + a_ref[y, :, :WIDTH]
        for step, ref in enumerate((a_ref, b_ref, c_ref, d_ref)):
            source = lax.bitwise_xor(y_pos, step) * (NCORE * NTILE)
            load = ref[y, :, 256:]
            for core in range(NCORE):
                start = pl.multiple_of(source + core * NTILE, NTILE)
                data_ref[y, pl.ds(start, NTILE)] = pltpu.roll(
                    load, (BATCHES - RIDE - 2 * NTILE * core) % BATCHES, 1
                )
        data = jnp.transpose(data_ref[y])
        value, error = data[:SLOTS], data[SLOTS : 2 * SLOTS]
        gain = data[2 * SLOTS : 2 * SLOTS + 1]
        group = NCORE * y + core_pos
        picks, both = picks_ref[y], both_ref[y]
        live = jnp.where(slots < length_ref[pl.ds(group, 1)], 1.0, 0.0)
        state = interpolated(field, picks, both)
        bounded = jnp.tanh(state)
        derivative = 1.0 + gain * (1.0 - bounded * bounded)
        misfit = state + gain * bounded - value
        precision = live / (error * error)
        residual = derivative * misfit * precision

        @pl.when(y == y_pos)
        def _():
            weight_ref[...] = derivative * derivative * precision
            full_ref[...] = field

        got = lax.dot_general(
            halves(both * on_lanes(residual)), picks, (((1,), (1,)), ((), ())), preferred_element_type=FLOAT
        )
        got = got[: 2 * FINE_ROWS] + got[2 * FINE_ROWS :]
        left, right = got[:FINE_ROWS], got[FINE_ROWS:]
        spread_ref[y] = left + jnp.concatenate([right[:, -1:], right[:, :-1]], axis=1)


def curve_kernel(
    a_ref, b_ref, c_ref, d_ref, picks_ref, both_ref, weight_ref, square_ref, field_ref, sent_ref
):
    _, _, y_pos = place()
    field = a_ref[...] + b_ref[...] + c_ref[...] + d_ref[...]
    field_ref[...] = field
    observed = interpolated(field, picks_ref[y_pos], both_ref[y_pos])
    curvature = jnp.sum(weight_ref[...] * observed * observed, keepdims=True)
    square = jnp.sum(square_ref[...], keepdims=True)
    lanes = lax.broadcasted_iota(jnp.int32, (BATCHES, 128), 1)
    sent_ref[...] = jnp.where(lanes < 64, square, curvature)


def step_kernel(
    shared_ref, own_ref, grad_ref, full_ref, base_ref, image_ref, coarse_ref, increment_ref
):
    totals = jnp.sum(shared_ref[...], axis=0, keepdims=True)
    lanes = lax.broadcasted_iota(jnp.int32, (1, 128), 1)
    square = jnp.sum(jnp.where(lanes == 0, totals, 0.0), keepdims=True)
    curvature = jnp.sum(jnp.where(lanes == 127, totals, 0.0), keepdims=True)
    step = square / (square + curvature)
    for r in range(ROWS):
        coarse_ref[:, r, :] = own_ref[row_slice(r)] - step * grad_ref[row_slice(r)]
    increment_ref[...] = full_ref[...] - base_ref[...] - step * image_ref[...]


def shards(
    perturb,
    weights,
    column_map,
    background,
    stencil_index,
    row_fraction,
    column_fraction,
    block_lengths,
    obs_value,
    obs_error,
    instrument_gain,
):
    perturb, column_map = near(perturb), near(column_map)
    matrix = member_matrix()
    matrix = near(jnp.asarray(np.concatenate([matrix, matrix], axis=1), HALF))
    flat = (ROWS * MEMBERS_HERE, COARSE_COLS)
    sent, own, half = call(
        start_kernel,
        (((2 * NTILE, 128), FLOAT), (flat, FLOAT), (flat, HALF)),
        (obs_value[0].T, obs_error[0].T, instrument_gain, weights),
        far=(0, 1, 3),
        scalar=(2,),
        work=WORK,
        scratch=[pltpu.VMEM((SLOTS, BATCHES), FLOAT)] * 2
        + [pltpu.VMEM((MEMBERS_HERE, ROWS, COARSE_COLS), FLOAT), pltpu.SemaphoreType.DMA((3,))],
    )
    near_rows, far_rows = swap_both(half, half)

    data = lax.all_to_all(sent, "tile", split_axis=0, concat_axis=0, tiled=True)

    index = jnp.transpose(stencil_index[0], (1, 2, 0))
    row_frac = jnp.transpose(row_fraction[0], (1, 2, 0))
    column_frac = jnp.transpose(column_fraction[0], (1, 2, 0))
    lengths = block_lengths[0].T

    mine, other = partial_forward(
        laden_kernel, LADEN, near_rows, own, far_rows, matrix, perturb, column_map, data
    )
    (mine,) = call(add_kernel, (LADEN,), (mine, swap_core(other), background))
    pieces = [mine]
    for i in range(1, NY):
        pieces.append(across(mine, i))
    picks, both = call(
        prepare_kernel,
        (
            ((NY, WIDTH, SLOTS * BATCHES), HALF),
            ((NY, 2 * FINE_ROWS, SLOTS * BATCHES), FLOAT),
        ),
        (index, row_frac, column_frac),
    )
    region = ((FINE_ROWS, WIDTH), FLOAT)
    spread, weight, full = call(
        obs_kernel,
        (REGIONS, ((SLOTS, BATCHES), FLOAT), region),
        (*pieces, picks, both, lengths),
        scratch=[pltpu.VMEM((NY, BATCHES, 128), FLOAT)],
    )
    part, up, down = partial_adjoint(spread, swap_core(spread), perturb, column_map)
    near_rows, far_rows = swap_both(up, down)
    gradient, half, square = gradient_of(near_rows, part, far_rows, own)
    near_rows, far_rows = swap_both(half, half)
    mine, other = partial_forward(
        forward_kernel, REGIONS, near_rows, gradient, far_rows, matrix, perturb, column_map
    )
    pieces = call(pick_kernel, (region,) * NY, (mine, swap_core(other)))
    turned = pieces
    pieces = [turned[0]]
    for i in range(1, NY):
        pieces.append(across(turned[i], i))
    image, sent = call(
        curve_kernel,
        (region, ((BATCHES, 128), FLOAT)),
        (*pieces, picks, both, weight, square),
    )
    shared = lax.all_to_all(sent, ("member", "tile"), split_axis=0, concat_axis=0, tiled=True)
    return call(
        step_kernel,
        (((MEMBERS_HERE, ROWS, COARSE_COLS), FLOAT), region),
        (shared, own, gradient, full, background, image),
        far_out=(0, 1),
    )


def solution(mesh):
    placed = (
        P("member", "tile", None),
        P("member", "tile", None),
        P(),
        P("tile", "member"),
        P("tile", None, None, None),
        P("tile", None, None, None),
        P("tile", None, None, None),
        P("tile", None, None),
        P(("member", "tile"), None, None),
        P(("member", "tile"), None, None),
        P(("member", "tile")),
    )
    return jax.shard_map(
        shards,
        mesh=mesh,
        in_specs=placed,
        out_specs=(P("member", "tile", None), P("tile", "member")),
        check_vma=False,
    )
```

```python
import jax
import jax.numpy as jnp
import numpy as np
from jax import lax
from jax.experimental import pallas as pl
from jax.experimental.pallas import tpu as pltpu
from jax.sharding import PartitionSpec as P

RATIO = 4
KSM = 3
DIFFUSION = 0.45
NTILE = 16
NMEMBER = 8
NCORE = 2
NY = NMEMBER // NCORE
MEMBERS_HERE = 16
ROWS = 4
FINE_ROWS = 16
COARSE_COLS = 1280
WIDTH = 320
CHUNK = NCORE * WIDTH
SLOTS = 8
BATCHES = 128
ROOM = 16 << 20
WORK = 2 * 10**10
EVEN, ODD = pl.ds(0, NTILE, stride=2), pl.ds(1, NTILE, stride=2)
FLOAT, HALF = jnp.float32, jnp.bfloat16


def refine_matrix():
    table = np.zeros((FINE_ROWS, ROWS + 2))
    for row in range(ROWS):
        for offset in range(RATIO):
            shift = (offset + 0.5) / RATIO - 0.5
            fine = RATIO * row + offset
            if shift < 0:
                table[fine, row + 1] += 1.0 + shift
                table[fine, row] -= shift
            else:
                table[fine, row + 1] += 1.0 - shift
                table[fine, row + 2] += shift
    return table


def member_matrix():
    return np.einsum("fr,kl->kfrl", refine_matrix(), np.eye(MEMBERS_HERE)).reshape(
        MEMBERS_HERE * FINE_ROWS, (ROWS + 2) * MEMBERS_HERE
    )


def ring():
    step = []
    for member in range(NMEMBER):
        core, here, there = member % NCORE, member * NTILE, (member ^ 1) * NTILE
        for tile in range(NTILE):
            onward = tile + 1 - 2 * core
            inside = 0 <= onward < NTILE
            step.append((here + tile, here + onward if inside else there + tile))
    return step


def swap_both(first_values, second_values):
    first = lax.ppermute(first_values, ("member", "tile"), ring())
    back = [(target, source) for source, target in ring()]
    second = lax.ppermute(second_values, ("member", "tile"), back)
    return first, second


def across(values, step):
    pairs = [(i, i ^ (NCORE * step)) for i in range(NMEMBER)]
    return lax.ppermute(values, "member", pairs)


def swap_core(values):
    return lax.ppermute(values, "member", [(i, i ^ 1) for i in range(NMEMBER)])


NEAR = pl.BlockSpec(memory_space=pltpu.VMEM)
FAR = pl.BlockSpec(memory_space=pltpu.HBM)
SCALAR = pl.BlockSpec(memory_space=pltpu.SMEM)


def near(values):
    return pltpu.with_memory_space_constraint(values, pltpu.VMEM)


def distant(values):
    return pltpu.with_memory_space_constraint(values, pltpu.HBM)


def call(kernel, out_shapes, arguments, far=(), scratch=(), far_out=(), scalar=(), work=10**9):
    specs = [
        SCALAR if i in scalar else FAR if i in far else NEAR for i in range(len(arguments))
    ]
    arguments = tuple(
        x if i in scalar else distant(x) if i in far else near(x)
        for i, x in enumerate(arguments)
    )
    return pl.pallas_call(
        kernel,
        out_shape=tuple(
            jax.ShapeDtypeStruct(shape, kind) if i in far_out else pltpu.VMEM(shape, kind)
            for i, (shape, kind) in enumerate(out_shapes)
        ),
        in_specs=specs,
        out_specs=tuple(NEAR for _ in out_shapes),
        scratch_shapes=list(scratch),
        compiler_params=pltpu.CompilerParams(vmem_limit_bytes=ROOM),
        cost_estimate=pl.CostEstimate(flops=work, transcendentals=0, bytes_accessed=work >> 7),
    )(*arguments)


def place():
    member_pos = lax.axis_index("member")
    return lax.axis_index("tile"), lax.rem(member_pos, NCORE), lax.div(member_pos, NCORE)


def edges():
    tile_pos = lax.axis_index("tile")
    return jnp.where(tile_pos > 0, 1.0, 0.0), jnp.where(tile_pos < NTILE - 1, 1.0, 0.0)


def swept(rows, masks):
    for _ in range(KSM):
        rows = [v if m is None else v * m for v, m in zip(rows, masks)]
        rows = [
            rows[i] + DIFFUSION * (rows[i - 1] + rows[i + 1] - 2.0 * rows[i])
            for i in range(1, len(rows) - 1)
        ]
        masks = masks[1:-1]
    return [v if m is None else v * m for v, m in zip(rows, masks)]


def row_slice(row):
    return pl.ds(row * MEMBERS_HERE, MEMBERS_HERE)


def downward():
    return lax.rem(lax.axis_index("member"), NCORE) == 1


def sides(a_ref, b_ref, cols, down_first):
    first = [a_ref[row_slice(r), cols].astype(FLOAT) for r in range(4)]
    second = [b_ref[row_slice(r), cols].astype(FLOAT) for r in range(4)]
    low = [jnp.where(down_first, v, u) for u, v in zip(first, second)]
    high = [jnp.where(down_first, u, v) for u, v in zip(first, second)]
    return low, high


def window(parity, y):
    return pl.ds(pl.multiple_of(y * CHUNK + 256 * parity, 128), 384)


def load(data_ref, ref, parity, core_pos):
    data, gain = data_ref[EVEN], data_ref[ODD]
    lanes = lax.broadcasted_iota(jnp.int32, data.shape, 1)
    home = RIDE + 2 * NTILE * core_pos
    for y in range(NY):
        shift = lax.rem(home + BATCHES - NTILE * (NCORE * y + parity), BATCHES)
        moved = jnp.where(lanes == home + 2 * SLOTS, gain, pltpu.roll(data, shift, 1))
        kept = (lanes >= home) & (lanes <= home + 2 * SLOTS)
        ref[y, :, 256:] = jnp.where(kept, moved, 0.0)


def regions_of(smooth_ref, refine_ref, perturb_ref, map_ref, parity, out_ref):
    smooth = smooth_ref[...]
    for pair in range(0, NY, 2):
        windows = [window(parity, y) for y in (pair, pair + 1)]
        columns = jnp.concatenate([map_ref[:, cols] for cols in windows], axis=1)
        mapped = jnp.dot(smooth, columns, preferred_element_type=FLOAT)
        high = mapped.astype(HALF)
        low = (mapped - high.astype(FLOAT)).astype(HALF)
        fine = jnp.dot(
            refine_ref[...], jnp.concatenate([high, low], axis=0), preferred_element_type=FLOAT
        )
        for half, cols in enumerate(windows):
            total = None
            for k in range(MEMBERS_HERE):
                term = fine[k * FINE_ROWS : (k + 1) * FINE_ROWS, half * 384 : (half + 1) * 384]
                term = term * perturb_ref[k, :, cols].astype(FLOAT)
                total = term if total is None else total + term
            out_ref[pair + half, :, :WIDTH] = jnp.where(
                parity == 0, total[:, :WIDTH], total[:, 384 - WIDTH :]
            )


def other_kernel(a_ref, own_ref, b_ref, refine_ref, perturb_ref, map_ref, *refs):
    other_ref, smooth_ref = refs[-2:]
    _, core_pos, _ = place()
    down_first = downward()
    below, above = edges()
    masks = [below] * 4 + [None] * 4 + [above] * 4
    for start in range(0, COARSE_COLS, 128):
        cols = pl.ds(start, 128)
        low, high = sides(a_ref, b_ref, cols, down_first)
        rows = low + [own_ref[row_slice(r), cols] for r in range(4)] + high
        for r, value in enumerate(swept(rows, masks)):
            smooth_ref[row_slice(r), cols] = value.astype(HALF)
    if len(refs) > 2:
        load(refs[0], other_ref, 1 - core_pos, core_pos)
    regions_of(smooth_ref, refine_ref, perturb_ref, map_ref, 1 - core_pos, other_ref)


def mine_kernel(smooth_ref, refine_ref, perturb_ref, map_ref, *refs):
    _, core_pos, _ = place()
    if len(refs) > 1:
        load(refs[0], refs[-1], core_pos, core_pos)
    regions_of(smooth_ref, refine_ref, perturb_ref, map_ref, core_pos, refs[-1])


REGIONS = ((NY, FINE_ROWS, WIDTH), FLOAT)
LADEN = ((NY, FINE_ROWS, 384), FLOAT)
RIDE = 64


SMOOTH = (((ROWS + 2) * MEMBERS_HERE, COARSE_COLS), HALF)


def partial_forward(shape, first, own, second, operators, data=()):
    other, smooth = call(other_kernel, (shape, SMOOTH), (first, own, second) + operators + data)
    there = swap_core(other)
    (mine,) = call(mine_kernel, (shape,), (smooth,) + operators + data)
    return mine, there


PART = (((ROWS + 2) * MEMBERS_HERE, COARSE_COLS), FLOAT)


def pulled_part(values_ref, back_ref, perturb_ref, map_ref, parity):
    total = None
    for pair in range(0, NY, 2):
        windows = [window(parity, y) for y in (pair, pair + 1)]
        columns = jnp.concatenate([map_ref[:, cols] for cols in windows], axis=1)
        pulled = []
        for y, cols in zip((pair, pair + 1), windows):
            values = values_ref[y]
            rest = jnp.zeros((FINE_ROWS, 384 - WIDTH), FLOAT)
            spread = jnp.where(
                parity == 0,
                jnp.concatenate([values, rest], axis=1),
                jnp.concatenate([rest, values], axis=1),
            )
            highs, lows = [], []
            for k in range(MEMBERS_HERE):
                term = perturb_ref[k, :, cols].astype(FLOAT) * spread
                high = term.astype(HALF)
                highs.append(high)
                lows.append((term - high.astype(FLOAT)).astype(HALF))
            pulled.append(jnp.concatenate(highs + lows, axis=0))
        pulled = jnp.dot(
            back_ref[...], jnp.concatenate(pulled, axis=1), preferred_element_type=FLOAT
        )
        part = lax.dot_general(
            pulled.astype(HALF),
            columns,
            (((1,), (1,)), ((), ())),
            preferred_element_type=FLOAT,
        )
        total = part if total is None else total + part
    return total


def pull_mine_kernel(mine_ref, back_ref, perturb_ref, map_ref, part_ref):
    _, core_pos, _ = place()
    part_ref[...] = pulled_part(mine_ref, back_ref, perturb_ref, map_ref, core_pos)


def pull_other_kernel(
    mine_ref, other_ref, back_ref, perturb_ref, map_ref, part_ref, a_ref, b_ref
):
    _, core_pos, _ = place()
    down_first = downward()
    total = mine_ref[...] + pulled_part(other_ref, back_ref, perturb_ref, map_ref, 1 - core_pos)
    part_ref[...] = total
    up = total[2 * MEMBERS_HERE :].astype(HALF)
    down = total[: 4 * MEMBERS_HERE].astype(HALF)
    a_ref[...] = jnp.where(down_first, down, up)
    b_ref[...] = jnp.where(down_first, up, down)


def partial_adjoint(spread, perturb, column_map):
    matrix = member_matrix().T
    matrix = jnp.asarray(np.concatenate([matrix, matrix], axis=1), HALF)
    operators = (matrix, perturb, column_map)
    there = swap_core(spread)
    (mine,) = call(pull_mine_kernel, (PART,), (spread,) + operators)
    rim = ((4 * MEMBERS_HERE, COARSE_COLS), HALF)
    return call(pull_other_kernel, (PART, rim, rim), (mine, there) + operators)


def gradient_kernel(a_ref, part_ref, b_ref, own_ref, grad_ref, half_ref, square_ref):
    below, above = edges()
    masks = [below] * 3 + [None] * 4 + [above] * 3
    down_first = downward()
    square = None
    for start in range(0, COARSE_COLS, 128):
        cols = pl.ds(start, 128)
        low, high = sides(a_ref, b_ref, cols, down_first)
        part = [part_ref[row_slice(r), cols] for r in range(6)]
        rows = [low[0], low[1], low[2] + part[0], low[3] * below + part[1], part[2], part[3]]
        rows += [part[4] + high[0] * above, part[5] + high[1], high[2], high[3]]
        for r, value in enumerate(swept(rows, masks)):
            gradient = own_ref[row_slice(r), cols] + value
            grad_ref[row_slice(r), cols] = gradient
            half_ref[row_slice(r), cols] = gradient.astype(HALF)
            term = gradient * gradient
            square = term if square is None else square + term
    square_ref[...] = square[:8] + square[8:]


def gradient_of(low, part, high, own):
    shape = (ROWS * MEMBERS_HERE, COARSE_COLS)
    return call(
        gradient_kernel,
        ((shape, FLOAT), (shape, HALF), ((8, 128), FLOAT)),
        (low, part, high, own),
    )


def start_kernel(
    value_hbm, error_hbm, gain_ref, weights_hbm,
    sent_ref, own_ref, half_ref, value_ref, error_ref, weights_ref, sem,
):
    copies = [
        pltpu.make_async_copy(value_hbm, value_ref, sem.at[0]),
        pltpu.make_async_copy(error_hbm, error_ref, sem.at[1]),
        pltpu.make_async_copy(weights_hbm, weights_ref, sem.at[2]),
    ]
    for copy in copies:
        copy.start()
    for copy in copies:
        copy.wait()
    for r in range(ROWS):
        values = weights_ref[:, r, :]
        own_ref[row_slice(r)] = values
        half_ref[row_slice(r)] = values.astype(HALF)
    rows = []
    for group in range(NMEMBER):
        for ref in (value_ref, error_ref):
            rows.append(pltpu.roll(ref[...], (BATCHES - NTILE * group) % BATCHES, 1))
    sent_ref[EVEN] = jnp.transpose(jnp.concatenate(rows, axis=0))[:NTILE]
    sent_ref[ODD] = jnp.full((NTILE, 128), gain_ref[0], FLOAT)


def add_kernel(a_ref, b_ref, base_ref, out_ref):
    _, _, y_pos = place()
    for y in range(NY):
        out_ref[y] = a_ref[y] + b_ref[y]
    out_ref[y_pos, :, :WIDTH] += base_ref[...]


def pick_kernel(a_ref, b_ref, *out_refs):
    _, _, y_pos = place()
    for step, ref in enumerate(out_refs):
        y = lax.bitwise_xor(y_pos, step)
        ref[...] = a_ref[y] + b_ref[y]


def column_picks(column):
    ids = lax.broadcasted_iota(jnp.int32, (WIDTH, BATCHES), 0)
    return jnp.concatenate(
        [(ids == column[s : s + 1]).astype(FLOAT).astype(HALF) for s in range(SLOTS)], axis=1
    )


def row_factors(row, fraction):
    ids = lax.broadcasted_iota(jnp.int32, (FINE_ROWS, BATCHES), 0)
    return jnp.concatenate(
        [
            jnp.where(ids == row[s : s + 1], 1.0 - fraction[s : s + 1], 0.0)
            + jnp.where(ids == row[s : s + 1] + 1, fraction[s : s + 1], 0.0)
            for s in range(SLOTS)
        ],
        axis=1,
    )


def on_lanes(values):
    return jnp.concatenate([values[s : s + 1] for s in range(SLOTS)], axis=1)


def on_slots(values):
    return jnp.concatenate(
        [values[:, s * BATCHES : (s + 1) * BATCHES] for s in range(SLOTS)], axis=0
    )


def halves(values):
    high = values.astype(HALF)
    return jnp.concatenate([high, (values - high.astype(FLOAT)).astype(HALF)], axis=0)


def located(index):
    row = index // WIDTH
    return row, index - row * WIDTH


def prepare_kernel(index_ref, row_ref, column_ref, picks_ref, both_ref):
    _, core_pos, _ = place()
    for y in range(NY):
        group = NCORE * y + core_pos
        row, column = located(index_ref[group])
        picks_ref[y] = column_picks(column)
        factors = row_factors(row, row_ref[group])
        fraction = on_lanes(column_ref[group])
        both_ref[y, :FINE_ROWS] = factors * (1.0 - fraction)
        both_ref[y, FINE_ROWS:] = factors * fraction


def interpolated(field, picks, both):
    shifted = jnp.concatenate([field[:, 1:], field[:, :1]], axis=1)
    got = jnp.dot(
        halves(jnp.concatenate([field, shifted], axis=0)), picks, preferred_element_type=FLOAT
    )
    got = (got[: 2 * FINE_ROWS] + got[2 * FINE_ROWS :]) * both
    return on_slots(jnp.sum(got, axis=0, keepdims=True))


def obs_kernel(
    a_ref, b_ref, c_ref, d_ref, picks_ref, both_ref, length_ref,
    spread_ref, weight_ref, full_ref, data_ref,
):
    _, core_pos, y_pos = place()
    slots = lax.broadcasted_iota(jnp.int32, (SLOTS, BATCHES), 0)
    for y in range(NY):
        field = sum(ref[y, :, :WIDTH] for ref in (b_ref, c_ref, d_ref)) + a_ref[y, :, :WIDTH]
        for step, ref in enumerate((a_ref, b_ref, c_ref, d_ref)):
            source = lax.bitwise_xor(y_pos, step) * (NCORE * NTILE)
            load = ref[y, :, 256:]
            for core in range(NCORE):
                start = pl.multiple_of(source + core * NTILE, NTILE)
                data_ref[y, pl.ds(start, NTILE)] = pltpu.roll(
                    load, (BATCHES - RIDE - 2 * NTILE * core) % BATCHES, 1
                )
        data = jnp.transpose(data_ref[y])
        value, error = data[:SLOTS], data[SLOTS : 2 * SLOTS]
        gain = data[2 * SLOTS : 2 * SLOTS + 1]
        group = NCORE * y + core_pos
        picks, both = picks_ref[y], both_ref[y]
        live = jnp.where(slots < length_ref[pl.ds(group, 1)], 1.0, 0.0)
        state = interpolated(field, picks, both)
        bounded = jnp.tanh(state)
        derivative = 1.0 + gain * (1.0 - bounded * bounded)
        misfit = state + gain * bounded - value
        precision = live / (error * error)
        residual = derivative * misfit * precision

        @pl.when(y == y_pos)
        def _():
            weight_ref[...] = derivative * derivative * precision
            full_ref[...] = field

        got = lax.dot_general(
            halves(both * on_lanes(residual)), picks, (((1,), (1,)), ((), ())), preferred_element_type=FLOAT
        )
        got = got[: 2 * FINE_ROWS] + got[2 * FINE_ROWS :]
        left, right = got[:FINE_ROWS], got[FINE_ROWS:]
        spread_ref[y] = left + jnp.concatenate([right[:, -1:], right[:, :-1]], axis=1)


def curve_kernel(
    a_ref, b_ref, c_ref, d_ref, picks_ref, both_ref, weight_ref, square_ref, field_ref, sent_ref
):
    _, _, y_pos = place()
    field = a_ref[...] + b_ref[...] + c_ref[...] + d_ref[...]
    field_ref[...] = field
    observed = interpolated(field, picks_ref[y_pos], both_ref[y_pos])
    curvature = jnp.sum(weight_ref[...] * observed * observed, keepdims=True)
    square = jnp.sum(square_ref[...], keepdims=True)
    lanes = lax.broadcasted_iota(jnp.int32, (BATCHES, 128), 1)
    sent_ref[...] = jnp.where(lanes < 64, square, curvature)


def step_kernel(
    shared_ref, own_ref, grad_ref, full_ref, base_ref, image_ref, coarse_ref, increment_ref
):
    totals = jnp.sum(shared_ref[...], axis=0, keepdims=True)
    lanes = lax.broadcasted_iota(jnp.int32, (1, 128), 1)
    square = jnp.sum(jnp.where(lanes == 0, totals, 0.0), keepdims=True)
    curvature = jnp.sum(jnp.where(lanes == 127, totals, 0.0), keepdims=True)
    step = square / (square + curvature)
    for r in range(ROWS):
        coarse_ref[:, r, :] = own_ref[row_slice(r)] - step * grad_ref[row_slice(r)]
    increment_ref[...] = full_ref[...] - base_ref[...] - step * image_ref[...]


def shards(
    perturb,
    weights,
    column_map,
    background,
    stencil_index,
    row_fraction,
    column_fraction,
    block_lengths,
    obs_value,
    obs_error,
    instrument_gain,
):
    perturb, column_map = near(perturb), near(column_map)
    matrix = member_matrix()
    matrix = near(jnp.asarray(np.concatenate([matrix, matrix], axis=1), HALF))
    flat = (ROWS * MEMBERS_HERE, COARSE_COLS)
    sent, own, half = call(
        start_kernel,
        (((2 * NTILE, 128), FLOAT), (flat, FLOAT), (flat, HALF)),
        (obs_value[0].T, obs_error[0].T, instrument_gain, weights),
        far=(0, 1, 3),
        scalar=(2,),
        work=WORK,
        scratch=[pltpu.VMEM((SLOTS, BATCHES), FLOAT)] * 2
        + [pltpu.VMEM((MEMBERS_HERE, ROWS, COARSE_COLS), FLOAT), pltpu.SemaphoreType.DMA((3,))],
    )
    near_rows, far_rows = swap_both(half, half)

    data = lax.all_to_all(sent, "tile", split_axis=0, concat_axis=0, tiled=True)

    index = jnp.transpose(stencil_index[0], (1, 2, 0))
    row_frac = jnp.transpose(row_fraction[0], (1, 2, 0))
    column_frac = jnp.transpose(column_fraction[0], (1, 2, 0))
    lengths = block_lengths[0].T

    operators = (matrix, perturb, column_map)
    mine, there = partial_forward(LADEN, near_rows, own, far_rows, operators, (data,))
    (mine,) = call(add_kernel, (LADEN,), (mine, there, background))
    pieces = [mine]
    for i in range(1, NY):
        pieces.append(across(mine, i))
    picks, both = call(
        prepare_kernel,
        (
            ((NY, WIDTH, SLOTS * BATCHES), HALF),
            ((NY, 2 * FINE_ROWS, SLOTS * BATCHES), FLOAT),
        ),
        (index, row_frac, column_frac),
    )
    region = ((FINE_ROWS, WIDTH), FLOAT)
    spread, weight, full = call(
        obs_kernel,
        (REGIONS, ((SLOTS, BATCHES), FLOAT), region),
        (*pieces, picks, both, lengths),
        scratch=[pltpu.VMEM((NY, BATCHES, 128), FLOAT)],
    )
    part, up, down = partial_adjoint(spread, perturb, column_map)
    near_rows, far_rows = swap_both(up, down)
    gradient, half, square = gradient_of(near_rows, part, far_rows, own)
    near_rows, far_rows = swap_both(half, half)
    mine, there = partial_forward(REGIONS, near_rows, gradient, far_rows, operators)
    turned = call(pick_kernel, (region,) * NY, (mine, there))
    pieces = [turned[0]]
    for i in range(1, NY):
        pieces.append(across(turned[i], i))
    image, sent = call(
        curve_kernel,
        (region, ((BATCHES, 128), FLOAT)),
        (*pieces, picks, both, weight, square),
    )
    shared = lax.all_to_all(sent, ("member", "tile"), split_axis=0, concat_axis=0, tiled=True)
    return call(
        step_kernel,
        (((MEMBERS_HERE, ROWS, COARSE_COLS), FLOAT), region),
        (shared, own, gradient, full, background, image),
        far_out=(0, 1),
    )


def solution(mesh):
    placed = (
        P("member", "tile", None),
        P("member", "tile", None),
        P(),
        P("tile", "member"),
        P("tile", None, None, None),
        P("tile", None, None, None),
        P("tile", None, None, None),
        P("tile", None, None),
        P(("member", "tile"), None, None),
        P(("member", "tile"), None, None),
        P(("member", "tile")),
    )
    return jax.shard_map(
        shards,
        mesh=mesh,
        in_specs=placed,
        out_specs=(P("member", "tile", None), P("tile", "member")),
        check_vma=False,
    )
```

```python
import jax
import jax.numpy as jnp
import numpy as np
from jax import lax
from jax.experimental import pallas as pl
from jax.experimental.pallas import tpu as pltpu
from jax.sharding import PartitionSpec as P

RATIO = 4
KSM = 3
DIFFUSION = 0.45
NTILE = 16
NMEMBER = 8
NCORE = 2
NY = NMEMBER // NCORE
MEMBERS_HERE = 16
ROWS = 4
FINE_ROWS = 16
COARSE_COLS = 1280
WIDTH = 320
CHUNK = NCORE * WIDTH
SLOTS = 8
BATCHES = 128
ROOM = 24 << 20
TOGETHER, PULLED = 4, 4
WORK = 2 * 10**10
EVEN, ODD = pl.ds(0, NTILE, stride=2), pl.ds(1, NTILE, stride=2)
FLOAT, HALF = jnp.float32, jnp.bfloat16


def refine_matrix():
    table = np.zeros((FINE_ROWS, ROWS + 2))
    for row in range(ROWS):
        for offset in range(RATIO):
            shift = (offset + 0.5) / RATIO - 0.5
            fine = RATIO * row + offset
            if shift < 0:
                table[fine, row + 1] += 1.0 + shift
                table[fine, row] -= shift
            else:
                table[fine, row + 1] += 1.0 - shift
                table[fine, row + 2] += shift
    return table


def member_matrix():
    return np.einsum("fr,kl->kfrl", refine_matrix(), np.eye(MEMBERS_HERE)).reshape(
        MEMBERS_HERE * FINE_ROWS, (ROWS + 2) * MEMBERS_HERE
    )


def ring():
    step = []
    for member in range(NMEMBER):
        core, here, there = member % NCORE, member * NTILE, (member ^ 1) * NTILE
        for tile in range(NTILE):
            onward = tile + 1 - 2 * core
            inside = 0 <= onward < NTILE
            step.append((here + tile, here + onward if inside else there + tile))
    return step


def swap_both(first_values, second_values):
    first = lax.ppermute(first_values, ("member", "tile"), ring())
    back = [(target, source) for source, target in ring()]
    second = lax.ppermute(second_values, ("member", "tile"), back)
    return first, second


def across(values, step):
    pairs = [(i, i ^ (NCORE * step)) for i in range(NMEMBER)]
    return lax.ppermute(values, "member", pairs)


def swap_core(values):
    return lax.ppermute(values, "member", [(i, i ^ 1) for i in range(NMEMBER)])


NEAR = pl.BlockSpec(memory_space=pltpu.VMEM)
FAR = pl.BlockSpec(memory_space=pltpu.HBM)
SCALAR = pl.BlockSpec(memory_space=pltpu.SMEM)


def near(values):
    return pltpu.with_memory_space_constraint(values, pltpu.VMEM)


def distant(values):
    return pltpu.with_memory_space_constraint(values, pltpu.HBM)


def call(kernel, out_shapes, arguments, far=(), scratch=(), far_out=(), scalar=(), work=10**9):
    specs = [
        SCALAR if i in scalar else FAR if i in far else NEAR for i in range(len(arguments))
    ]
    arguments = tuple(
        x if i in scalar else distant(x) if i in far else near(x)
        for i, x in enumerate(arguments)
    )
    return pl.pallas_call(
        kernel,
        out_shape=tuple(
            jax.ShapeDtypeStruct(shape, kind) if i in far_out else pltpu.VMEM(shape, kind)
            for i, (shape, kind) in enumerate(out_shapes)
        ),
        in_specs=specs,
        out_specs=tuple(NEAR for _ in out_shapes),
        scratch_shapes=list(scratch),
        compiler_params=pltpu.CompilerParams(vmem_limit_bytes=ROOM),
        cost_estimate=pl.CostEstimate(flops=work, transcendentals=0, bytes_accessed=work >> 7),
    )(*arguments)


def place():
    member_pos = lax.axis_index("member")
    return lax.axis_index("tile"), lax.rem(member_pos, NCORE), lax.div(member_pos, NCORE)


def edges():
    tile_pos = lax.axis_index("tile")
    return jnp.where(tile_pos > 0, 1.0, 0.0), jnp.where(tile_pos < NTILE - 1, 1.0, 0.0)


def swept(rows, masks):
    for _ in range(KSM):
        rows = [v if m is None else v * m for v, m in zip(rows, masks)]
        rows = [
            rows[i] + DIFFUSION * (rows[i - 1] + rows[i + 1] - 2.0 * rows[i])
            for i in range(1, len(rows) - 1)
        ]
        masks = masks[1:-1]
    return [v if m is None else v * m for v, m in zip(rows, masks)]


def row_slice(row):
    return pl.ds(row * MEMBERS_HERE, MEMBERS_HERE)


def downward():
    return lax.rem(lax.axis_index("member"), NCORE) == 1


def sides(a_ref, b_ref, cols, down_first):
    first = [a_ref[row_slice(r), cols].astype(FLOAT) for r in range(4)]
    second = [b_ref[row_slice(r), cols].astype(FLOAT) for r in range(4)]
    low = [jnp.where(down_first, v, u) for u, v in zip(first, second)]
    high = [jnp.where(down_first, u, v) for u, v in zip(first, second)]
    return low, high


def window(parity, y):
    return pl.ds(pl.multiple_of(y * CHUNK + 256 * parity, 128), 384)


def load(data_ref, ref, parity, core_pos):
    data, gain = data_ref[EVEN], data_ref[ODD]
    lanes = lax.broadcasted_iota(jnp.int32, data.shape, 1)
    home = RIDE + 2 * NTILE * core_pos
    for y in range(NY):
        shift = lax.rem(home + BATCHES - NTILE * (NCORE * y + parity), BATCHES)
        moved = jnp.where(lanes == home + 2 * SLOTS, gain, pltpu.roll(data, shift, 1))
        kept = (lanes >= home) & (lanes <= home + 2 * SLOTS)
        ref[y, :, 256:] = jnp.where(kept, moved, 0.0)


def regions_of(smooth_ref, refine_ref, perturb_ref, map_ref, parity, out_ref):
    smooth = smooth_ref[...]
    for pair in range(0, NY, TOGETHER):
        windows = [window(parity, y) for y in range(pair, pair + TOGETHER)]
        columns = jnp.concatenate([map_ref[:, cols] for cols in windows], axis=1)
        mapped = jnp.dot(smooth, columns, preferred_element_type=FLOAT)
        high = mapped.astype(HALF)
        low = (mapped - high.astype(FLOAT)).astype(HALF)
        fine = jnp.dot(
            refine_ref[...], jnp.concatenate([high, low], axis=0), preferred_element_type=FLOAT
        )
        for half, cols in enumerate(windows):
            total = None
            for k in range(MEMBERS_HERE):
                term = fine[k * FINE_ROWS : (k + 1) * FINE_ROWS, half * 384 : (half + 1) * 384]
                term = term * perturb_ref[k, :, cols].astype(FLOAT)
                total = term if total is None else total + term
            out_ref[pair + half, :, :WIDTH] = jnp.where(
                parity == 0, total[:, :WIDTH], total[:, 384 - WIDTH :]
            )


def other_kernel(a_ref, own_ref, b_ref, refine_ref, perturb_ref, map_ref, *refs):
    other_ref, smooth_ref = refs[-2:]
    _, core_pos, _ = place()
    down_first = downward()
    below, above = edges()
    masks = [below] * 4 + [None] * 4 + [above] * 4
    for start in range(0, COARSE_COLS, 128):
        cols = pl.ds(start, 128)
        low, high = sides(a_ref, b_ref, cols, down_first)
        rows = low + [own_ref[row_slice(r), cols] for r in range(4)] + high
        for r, value in enumerate(swept(rows, masks)):
            smooth_ref[row_slice(r), cols] = value.astype(HALF)
    if len(refs) > 2:
        load(refs[0], other_ref, 1 - core_pos, core_pos)
    regions_of(smooth_ref, refine_ref, perturb_ref, map_ref, 1 - core_pos, other_ref)


def mine_kernel(smooth_ref, refine_ref, perturb_ref, map_ref, *refs):
    _, core_pos, _ = place()
    if len(refs) > 1:
        load(refs[0], refs[-1], core_pos, core_pos)
    regions_of(smooth_ref, refine_ref, perturb_ref, map_ref, core_pos, refs[-1])


REGIONS = ((NY, FINE_ROWS, WIDTH), FLOAT)
LADEN = ((NY, FINE_ROWS, 384), FLOAT)
RIDE = 64


SMOOTH = (((ROWS + 2) * MEMBERS_HERE, COARSE_COLS), HALF)


def partial_forward(shape, first, own, second, operators, data=()):
    other, smooth = call(other_kernel, (shape, SMOOTH), (first, own, second) + operators + data)
    there = swap_core(other)
    (mine,) = call(mine_kernel, (shape,), (smooth,) + operators + data)
    return mine, there


PART = (((ROWS + 2) * MEMBERS_HERE, COARSE_COLS), FLOAT)


def pulled_part(values_ref, back_ref, perturb_ref, map_ref, parity):
    total = None
    for pair in range(0, NY, PULLED):
        windows = [window(parity, y) for y in range(pair, pair + PULLED)]
        columns = jnp.concatenate([map_ref[:, cols] for cols in windows], axis=1)
        pulled = []
        for y, cols in zip(range(pair, pair + PULLED), windows):
            values = values_ref[y]
            rest = jnp.zeros((FINE_ROWS, 384 - WIDTH), FLOAT)
            spread = jnp.where(
                parity == 0,
                jnp.concatenate([values, rest], axis=1),
                jnp.concatenate([rest, values], axis=1),
            )
            highs, lows = [], []
            for k in range(MEMBERS_HERE):
                term = perturb_ref[k, :, cols].astype(FLOAT) * spread
                high = term.astype(HALF)
                highs.append(high)
                lows.append((term - high.astype(FLOAT)).astype(HALF))
            pulled.append(jnp.concatenate(highs + lows, axis=0))
        pulled = jnp.dot(
            back_ref[...], jnp.concatenate(pulled, axis=1), preferred_element_type=FLOAT
        )
        part = lax.dot_general(
            pulled.astype(HALF),
            columns,
            (((1,), (1,)), ((), ())),
            preferred_element_type=FLOAT,
        )
        total = part if total is None else total + part
    return total


def pull_mine_kernel(mine_ref, back_ref, perturb_ref, map_ref, part_ref):
    _, core_pos, _ = place()
    part_ref[...] = pulled_part(mine_ref, back_ref, perturb_ref, map_ref, core_pos)


def pull_other_kernel(
    mine_ref, other_ref, back_ref, perturb_ref, map_ref, part_ref, a_ref, b_ref
):
    _, core_pos, _ = place()
    down_first = downward()
    total = mine_ref[...] + pulled_part(other_ref, back_ref, perturb_ref, map_ref, 1 - core_pos)
    part_ref[...] = total
    up = total[2 * MEMBERS_HERE :].astype(HALF)
    down = total[: 4 * MEMBERS_HERE].astype(HALF)
    a_ref[...] = jnp.where(down_first, down, up)
    b_ref[...] = jnp.where(down_first, up, down)


def partial_adjoint(spread, perturb, column_map):
    matrix = member_matrix().T
    matrix = jnp.asarray(np.concatenate([matrix, matrix], axis=1), HALF)
    operators = (matrix, perturb, column_map)
    there = swap_core(spread)
    (mine,) = call(pull_mine_kernel, (PART,), (spread,) + operators)
    rim = ((4 * MEMBERS_HERE, COARSE_COLS), HALF)
    return call(pull_other_kernel, (PART, rim, rim), (mine, there) + operators)


def gradient_kernel(a_ref, part_ref, b_ref, own_ref, grad_ref, half_ref, square_ref):
    below, above = edges()
    masks = [below] * 3 + [None] * 4 + [above] * 3
    down_first = downward()
    square = None
    for start in range(0, COARSE_COLS, 128):
        cols = pl.ds(start, 128)
        low, high = sides(a_ref, b_ref, cols, down_first)
        part = [part_ref[row_slice(r), cols] for r in range(6)]
        rows = [low[0], low[1], low[2] + part[0], low[3] * below + part[1], part[2], part[3]]
        rows += [part[4] + high[0] * above, part[5] + high[1], high[2], high[3]]
        for r, value in enumerate(swept(rows, masks)):
            gradient = own_ref[row_slice(r), cols] + value
            grad_ref[row_slice(r), cols] = gradient
            half_ref[row_slice(r), cols] = gradient.astype(HALF)
            term = gradient * gradient
            square = term if square is None else square + term
    square_ref[...] = square[:8] + square[8:]


def gradient_of(low, part, high, own):
    shape = (ROWS * MEMBERS_HERE, COARSE_COLS)
    return call(
        gradient_kernel,
        ((shape, FLOAT), (shape, HALF), ((8, 128), FLOAT)),
        (low, part, high, own),
    )


def start_kernel(
    value_hbm, error_hbm, gain_ref, weights_hbm,
    sent_ref, own_ref, half_ref, value_ref, error_ref, weights_ref, sem,
):
    copies = [
        pltpu.make_async_copy(value_hbm, value_ref, sem.at[0]),
        pltpu.make_async_copy(error_hbm, error_ref, sem.at[1]),
        pltpu.make_async_copy(weights_hbm, weights_ref, sem.at[2]),
    ]
    for copy in copies:
        copy.start()
    for copy in copies:
        copy.wait()
    for r in range(ROWS):
        values = weights_ref[:, r, :]
        own_ref[row_slice(r)] = values
        half_ref[row_slice(r)] = values.astype(HALF)
    rows = []
    for group in range(NMEMBER):
        for ref in (value_ref, error_ref):
            rows.append(pltpu.roll(ref[...], (BATCHES - NTILE * group) % BATCHES, 1))
    sent_ref[EVEN] = jnp.transpose(jnp.concatenate(rows, axis=0))[:NTILE]
    sent_ref[ODD] = jnp.full((NTILE, 128), gain_ref[0], FLOAT)


def add_kernel(a_ref, b_ref, base_ref, out_ref):
    _, _, y_pos = place()
    for y in range(NY):
        out_ref[y] = a_ref[y] + b_ref[y]
    out_ref[y_pos, :, :WIDTH] += base_ref[...]


def pick_kernel(a_ref, b_ref, *out_refs):
    _, _, y_pos = place()
    for step, ref in enumerate(out_refs):
        y = lax.bitwise_xor(y_pos, step)
        ref[...] = a_ref[y] + b_ref[y]


def column_picks(column):
    ids = lax.broadcasted_iota(jnp.int32, (WIDTH, BATCHES), 0)
    return jnp.concatenate(
        [(ids == column[s : s + 1]).astype(FLOAT).astype(HALF) for s in range(SLOTS)], axis=1
    )


def row_factors(row, fraction):
    ids = lax.broadcasted_iota(jnp.int32, (FINE_ROWS, BATCHES), 0)
    return jnp.concatenate(
        [
            jnp.where(ids == row[s : s + 1], 1.0 - fraction[s : s + 1], 0.0)
            + jnp.where(ids == row[s : s + 1] + 1, fraction[s : s + 1], 0.0)
            for s in range(SLOTS)
        ],
        axis=1,
    )


def on_lanes(values):
    return jnp.concatenate([values[s : s + 1] for s in range(SLOTS)], axis=1)


def on_slots(values):
    return jnp.concatenate(
        [values[:, s * BATCHES : (s + 1) * BATCHES] for s in range(SLOTS)], axis=0
    )


def halves(values):
    high = values.astype(HALF)
    return jnp.concatenate([high, (values - high.astype(FLOAT)).astype(HALF)], axis=0)


def located(index):
    row = index // WIDTH
    return row, index - row * WIDTH


def prepare_kernel(index_ref, row_ref, column_ref, picks_ref, both_ref):
    _, core_pos, _ = place()
    for y in range(NY):
        group = NCORE * y + core_pos
        row, column = located(index_ref[group])
        picks_ref[y] = column_picks(column)
        factors = row_factors(row, row_ref[group])
        fraction = on_lanes(column_ref[group])
        both_ref[y, :FINE_ROWS] = factors * (1.0 - fraction)
        both_ref[y, FINE_ROWS:] = factors * fraction


def interpolated(field, picks, both):
    shifted = jnp.concatenate([field[:, 1:], field[:, :1]], axis=1)
    got = jnp.dot(
        halves(jnp.concatenate([field, shifted], axis=0)), picks, preferred_element_type=FLOAT
    )
    got = (got[: 2 * FINE_ROWS] + got[2 * FINE_ROWS :]) * both
    return on_slots(jnp.sum(got, axis=0, keepdims=True))


def obs_kernel(
    a_ref, b_ref, c_ref, d_ref, picks_ref, both_ref, length_ref,
    spread_ref, weight_ref, full_ref, data_ref,
):
    _, core_pos, y_pos = place()
    slots = lax.broadcasted_iota(jnp.int32, (SLOTS, BATCHES), 0)
    for y in range(NY):
        field = sum(ref[y, :, :WIDTH] for ref in (b_ref, c_ref, d_ref)) + a_ref[y, :, :WIDTH]
        for step, ref in enumerate((a_ref, b_ref, c_ref, d_ref)):
            source = lax.bitwise_xor(y_pos, step) * (NCORE * NTILE)
            load = ref[y, :, 256:]
            for core in range(NCORE):
                start = pl.multiple_of(source + core * NTILE, NTILE)
                data_ref[y, pl.ds(start, NTILE)] = pltpu.roll(
                    load, (BATCHES - RIDE - 2 * NTILE * core) % BATCHES, 1
                )
        data = jnp.transpose(data_ref[y])
        value, error = data[:SLOTS], data[SLOTS : 2 * SLOTS]
        gain = data[2 * SLOTS : 2 * SLOTS + 1]
        group = NCORE * y + core_pos
        picks, both = picks_ref[y], both_ref[y]
        live = jnp.where(slots < length_ref[pl.ds(group, 1)], 1.0, 0.0)
        state = interpolated(field, picks, both)
        bounded = jnp.tanh(state)
        derivative = 1.0 + gain * (1.0 - bounded * bounded)
        misfit = state + gain * bounded - value
        precision = live / (error * error)
        residual = derivative * misfit * precision

        @pl.when(y == y_pos)
        def _():
            weight_ref[...] = derivative * derivative * precision
            full_ref[...] = field

        got = lax.dot_general(
            halves(both * on_lanes(residual)), picks, (((1,), (1,)), ((), ())), preferred_element_type=FLOAT
        )
        got = got[: 2 * FINE_ROWS] + got[2 * FINE_ROWS :]
        left, right = got[:FINE_ROWS], got[FINE_ROWS:]
        spread_ref[y] = left + jnp.concatenate([right[:, -1:], right[:, :-1]], axis=1)


def curve_kernel(
    a_ref, b_ref, c_ref, d_ref, picks_ref, both_ref, weight_ref, square_ref, field_ref, sent_ref
):
    _, _, y_pos = place()
    field = a_ref[...] + b_ref[...] + c_ref[...] + d_ref[...]
    field_ref[...] = field
    observed = interpolated(field, picks_ref[y_pos], both_ref[y_pos])
    curvature = jnp.sum(weight_ref[...] * observed * observed, keepdims=True)
    square = jnp.sum(square_ref[...], keepdims=True)
    lanes = lax.broadcasted_iota(jnp.int32, (BATCHES, 128), 1)
    sent_ref[...] = jnp.where(lanes < 64, square, curvature)


def step_kernel(
    shared_ref, own_ref, grad_ref, full_ref, base_ref, image_ref, coarse_ref, increment_ref
):
    totals = jnp.sum(shared_ref[...], axis=0, keepdims=True)
    lanes = lax.broadcasted_iota(jnp.int32, (1, 128), 1)
    square = jnp.sum(jnp.where(lanes == 0, totals, 0.0), keepdims=True)
    curvature = jnp.sum(jnp.where(lanes == 127, totals, 0.0), keepdims=True)
    step = square / (square + curvature)
    for r in range(ROWS):
        coarse_ref[:, r, :] = own_ref[row_slice(r)] - step * grad_ref[row_slice(r)]
    increment_ref[...] = full_ref[...] - base_ref[...] - step * image_ref[...]


def shards(
    perturb,
    weights,
    column_map,
    background,
    stencil_index,
    row_fraction,
    column_fraction,
    block_lengths,
    obs_value,
    obs_error,
    instrument_gain,
):
    perturb, column_map = near(perturb), near(column_map)
    matrix = member_matrix()
    matrix = near(jnp.asarray(np.concatenate([matrix, matrix], axis=1), HALF))
    flat = (ROWS * MEMBERS_HERE, COARSE_COLS)
    sent, own, half = call(
        start_kernel,
        (((2 * NTILE, 128), FLOAT), (flat, FLOAT), (flat, HALF)),
        (obs_value[0].T, obs_error[0].T, instrument_gain, weights),
        far=(0, 1, 3),
        scalar=(2,),
        work=WORK,
        scratch=[pltpu.VMEM((SLOTS, BATCHES), FLOAT)] * 2
        + [pltpu.VMEM((MEMBERS_HERE, ROWS, COARSE_COLS), FLOAT), pltpu.SemaphoreType.DMA((3,))],
    )
    near_rows, far_rows = swap_both(half, half)

    data = lax.all_to_all(sent, "tile", split_axis=0, concat_axis=0, tiled=True)

    index = jnp.transpose(stencil_index[0], (1, 2, 0))
    row_frac = jnp.transpose(row_fraction[0], (1, 2, 0))
    column_frac = jnp.transpose(column_fraction[0], (1, 2, 0))
    lengths = block_lengths[0].T

    operators = (matrix, perturb, column_map)
    mine, there = partial_forward(LADEN, near_rows, own, far_rows, operators, (data,))
    (mine,) = call(add_kernel, (LADEN,), (mine, there, background))
    pieces = [mine]
    for i in range(1, NY):
        pieces.append(across(mine, i))
    picks, both = call(
        prepare_kernel,
        (
            ((NY, WIDTH, SLOTS * BATCHES), HALF),
            ((NY, 2 * FINE_ROWS, SLOTS * BATCHES), FLOAT),
        ),
        (index, row_frac, column_frac),
    )
    region = ((FINE_ROWS, WIDTH), FLOAT)
    spread, weight, full = call(
        obs_kernel,
        (REGIONS, ((SLOTS, BATCHES), FLOAT), region),
        (*pieces, picks, both, lengths),
        scratch=[pltpu.VMEM((NY, BATCHES, 128), FLOAT)],
    )
    part, up, down = partial_adjoint(spread, perturb, column_map)
    near_rows, far_rows = swap_both(up, down)
    gradient, half, square = gradient_of(near_rows, part, far_rows, own)
    near_rows, far_rows = swap_both(half, half)
    mine, there = partial_forward(REGIONS, near_rows, gradient, far_rows, operators)
    turned = call(pick_kernel, (region,) * NY, (mine, there))
    pieces = [turned[0]]
    for i in range(1, NY):
        pieces.append(across(turned[i], i))
    image, sent = call(
        curve_kernel,
        (region, ((BATCHES, 128), FLOAT)),
        (*pieces, picks, both, weight, square),
    )
    shared = lax.all_to_all(sent, ("member", "tile"), split_axis=0, concat_axis=0, tiled=True)
    return call(
        step_kernel,
        (((MEMBERS_HERE, ROWS, COARSE_COLS), FLOAT), region),
        (shared, own, gradient, full, background, image),
        far_out=(0, 1),
    )


def solution(mesh):
    placed = (
        P("member", "tile", None),
        P("member", "tile", None),
        P(),
        P("tile", "member"),
        P("tile", None, None, None),
        P("tile", None, None, None),
        P("tile", None, None, None),
        P("tile", None, None),
        P(("member", "tile"), None, None),
        P(("member", "tile"), None, None),
        P(("member", "tile")),
    )
    return jax.shard_map(
        shards,
        mesh=mesh,
        in_specs=placed,
        out_specs=(P("member", "tile", None), P("tile", "member")),
        check_vma=False,
    )
```
